256 devices in a mesh: layer: 16 (over z_hi, y, core), phi: 16 (over x, z_lo).
Axes of the slice: x: 4, y: 4, z: 8 (z_hi: 2, z_lo: 4; z = z_hi * 4 + z_lo), core: 2. Of those that a mesh axis runs over, the one named last changes fastest.
Arguments:
- features: bfloat16 [65536, 256], P(('layer', 'phi')), may hold values from -6 to 6
- w_layers: bfloat16 [4, 256, 256], replicated, may hold values from -0.375 to 0.375
- b_layers: float32 [4, 256], replicated, may hold values from -1.5 to 1.5
- w_coord: bfloat16 [16, 256], replicated, may hold values from -0.09375 to 0.09375
- w_beta: bfloat16 [256], replicated, may hold values from -0.375 to 0.375
- point_hit: int32 [2048], P(('layer', 'phi')), may hold values from 0 to 255
- track: int32 [65536], P(('layer', 'phi')), may hold values from 0 to 2047
- noise: int32 [65536], P(('layer', 'phi')), may hold values 0 or 1
Outputs:
- grad_w_layers: float32 [4, 256, 256], replicated
- grad_b_layers: float32 [4, 256], replicated
- grad_w_coord: float32 [16, 256], replicated
- grad_w_beta: float32 [256], replicated
- loss: float32 [], replicated
The draws below stay inside these ranges and needn't reach their ends.
Inputs may be any that keep to these rules, and one draw needn't show every extreme that they name: `point_hit`: an index among the 256 hits of the device holding the entry. A non-noise hit of track k is attracted to point k.
All inputs are finite; a program needn't handle non-finite values. No bound on the sum of `noise` on one device may be relied on, other than what follows from the above.
Results may differ from the reference program's by a relative error of at most 0.0013.
Values sent between devices are 32-bit elements; how exact they have to be, the bound alone decides.
A program may use at most 64 MiB of HBM per device.

```python
import jax
import jax.numpy as jnp
from jax import lax

WIDTH = 256
LAYERS = 4
CDIM = 16
HITS_DEV = 256
P_DEV = 8
HITS = 65536
K = 2048
N_LAYER = 16
N_PHI = 16


def set_ends(drawn, rng, smallest, high):
    longest = drawn.shape.index(max(drawn.shape))
    spots = []
    for shift in (0, 1):
        where = [jax.random.randint(jax.random.fold_in(rng, axis), (), 0, length) for axis, length in enumerate(drawn.shape)]
        where[longest] = (where[longest] + shift) % drawn.shape[longest]
        spots.append(tuple(where))
    return drawn.at[spots[0]].set(smallest).at[spots[1]].set(high)


def levels(stream_key, shape, pieces, smallest, top_value):
    loudness = 1.0
    for dim, blocks in pieces:
        draws = jax.random.uniform(jax.random.fold_in(jax.random.fold_in(stream_key, 6), dim), (blocks,), jnp.float32, smallest / len(pieces), top_value / len(pieces))
        loudness = loudness * jnp.repeat(jnp.exp(draws), shape[dim] // blocks).reshape((-1,) + (1,) * (len(shape) - 1 - dim))
    return loudness


def normal_values(rng, extent, scale, most, cuts=(), held_as=jnp.bfloat16):
    values = jax.random.normal(rng, extent, jnp.float32) * scale
    if len(cuts) > 0:
        values = levels(rng, extent, cuts, -0.22, 0.18) * values
    return jnp.clip(values, min=-most, max=most).astype(held_as)


def setup_inputs(seed: int = 0) -> dict:
    arg_keys = jax.random.split(jax.random.key(seed), 9)
    return {
        "features": normal_values(arg_keys[0], (HITS, WIDTH), 1.0, 6.0, ((0, 256),)),
        "w_layers": normal_values(arg_keys[1], (LAYERS, WIDTH, WIDTH), WIDTH ** -0.5, 0.375),
        "b_layers": normal_values(arg_keys[2], (LAYERS, WIDTH), 0.3, 1.5, (), jnp.float32),
        "w_coord": normal_values(arg_keys[3], (CDIM, WIDTH), (16 * WIDTH) ** -0.5, 0.09375),
        "w_beta": normal_values(arg_keys[4], (WIDTH,), WIDTH ** -0.5, 0.375),
        "point_hit": set_ends(jax.random.randint(arg_keys[5], (K,), 0, HITS_DEV), jax.random.fold_in(arg_keys[5], 1), 0, HITS_DEV - 1).astype(jnp.int32),
        "track": set_ends(jax.random.randint(arg_keys[6], (HITS,), 0, K), jax.random.fold_in(arg_keys[6], 1), 0, K - 1).astype(jnp.int32),
        "noise": set_ends((jax.random.randint(arg_keys[7], (HITS,), 0, 5) < 1).astype(jnp.int32), jax.random.fold_in(arg_keys[7], 1), 0, 1),
    }


dist_eps = 0.0001
charge_floor = 0.5

def mlp_forward(features, w_layers, b_layers, w_coord, w_beta):
    hidden = features
    states = [features]
    preacts = []
    for layer_num in range(w_layers.shape[0]):
        pre = jnp.dot(hidden, w_layers[layer_num], preferred_element_type=jnp.float32) + b_layers[layer_num]
        preacts.append(pre)
        hidden = jax.nn.silu(pre).astype(jnp.bfloat16)
        states.append(hidden)
    coords = lax.dot_general(w_coord, hidden, (((1,), (1,)), ((), ())), preferred_element_type=jnp.float32)
    logits = jnp.dot(hidden, w_beta, preferred_element_type=jnp.float32)
    return (states, preacts, coords, logits)

def charges(logits):
    expz = jnp.exp(logits)
    spread = jnp.log1p(2.0 * expz)
    charge = 0.25 * spread * spread + charge_floor
    slope = 0.5 * spread * (2.0 * expz / (1.0 + 2.0 * expz))
    return (jax.nn.sigmoid(logits), charge, slope)

def pair_terms(coords, charge, track, live, point_rows, first, hits_all):
    point_y = point_rows[:-1]
    point_q = point_rows[-1]
    width = point_rows.shape[1]
    hit_sq = lax.optimization_barrier(jnp.sum(coords * coords, 0))
    point_sq = lax.optimization_barrier(jnp.sum(point_y * point_y, 0))
    cross = lax.dot_general(coords, point_y, (((0,), (0,)), ((), ())), precision=lax.Precision.HIGHEST, preferred_element_type=jnp.float32)
    dist_sq = jnp.maximum(hit_sq[:, None] + point_sq[None, :] - 2.0 * cross, 0.0)
    dist = jnp.sqrt(dist_sq + dist_eps)
    index = first + lax.iota(jnp.int32, width)
    match = jnp.where((track[:, None] == index[None, :]) & (live[:, None] > 0), 1.0, 0.0)
    reach = jnp.maximum(1.0 - dist, 0.0)
    potential = match * dist_sq + (1.0 - match) * reach * reach
    pot_rows = lax.optimization_barrier(jnp.sum(potential * point_q[None, :], 1))
    coef = (charge / hits_all)[:, None] * point_q[None, :] * (2.0 * match - (1.0 - match) * 2.0 * reach / dist)
    row_sums = lax.optimization_barrier(jnp.sum(coef, 1))
    col_sums = lax.optimization_barrier(jnp.sum(coef, 0))
    pulls = lax.dot_general(point_y, coef, (((1,), (1,)), ((), ())), precision=lax.Precision.HIGHEST, preferred_element_type=jnp.float32)
    point_grad = point_y * col_sums[None, :] - lax.dot_general(coords, coef, (((1,), (0,)), ((), ())), precision=lax.Precision.HIGHEST, preferred_element_type=jnp.float32)
    charge_grad = jnp.dot(charge, potential, precision=lax.Precision.HIGHEST) / hits_all
    return (row_sums, pot_rows, pulls, jnp.concatenate([point_grad, charge_grad[None, :]], 0))

def head_backward(states, preacts, w_layers, w_coord, w_beta, coord_grad, logit_grad):
    coord_low = coord_grad.astype(jnp.bfloat16)
    logit_low = logit_grad.astype(jnp.bfloat16)
    hidden = states[-1]
    grad_coord_w = lax.dot_general(coord_low, hidden, (((1,), (0,)), ((), ())), preferred_element_type=jnp.float32)
    grad_beta_w = jnp.dot(logit_low, hidden, preferred_element_type=jnp.float32)
    upstream = lax.dot_general(coord_low, w_coord, (((0,), (0,)), ((), ())), preferred_element_type=jnp.float32)
    upstream = upstream + logit_low.astype(jnp.float32)[:, None] * w_beta.astype(jnp.float32)[None, :]
    count = w_layers.shape[0]
    weight_grads = [None] * count
    bias_grads = [None] * count
    for layer_num in range(count - 1, -1, -1):
        pre = preacts[layer_num]
        sig = jax.nn.sigmoid(pre)
        local = (upstream * sig * (1.0 + pre * (1.0 - sig))).astype(jnp.bfloat16)
        weight_grads[layer_num] = lax.dot_general(states[layer_num], local, (((0,), (0,)), ((), ())), preferred_element_type=jnp.float32)
        bias_grads[layer_num] = lax.optimization_barrier(jnp.sum(local.astype(jnp.float32), 0))
        if layer_num > 0:
            upstream = lax.dot_general(local, w_layers[layer_num], (((1,), (1,)), ((), ())), preferred_element_type=jnp.float32)
    return (jnp.stack(weight_grads), jnp.stack(bias_grads), grad_coord_w, grad_beta_w)

def reference(features, w_layers, b_layers, w_coord, w_beta, point_hit, track, noise):
    ndev = N_LAYER * N_PHI
    hits_all = HITS * 1.0
    feat_blocks = features.reshape(ndev, HITS_DEV, WIDTH)

    def forward_one(feat):
        states, preacts, coords, logits = mlp_forward(feat, w_layers, b_layers, w_coord, w_beta)
        return (coords, logits)
    coords_all, logits_all = lax.map(forward_one, feat_blocks)
    beta_all, charge_all, slope_all = charges(logits_all)
    owner = jnp.arange(K, dtype=jnp.int32) // P_DEV
    point_y = coords_all[owner, :, point_hit]
    point_rows = jnp.concatenate([point_y.T, charge_all[owner, point_hit][None, :]], 0)
    track_blocks = track.reshape(ndev, HITS_DEV)
    noise_blocks = noise.reshape(ndev, HITS_DEV)
    live_blocks = 1 - noise_blocks

    def scan_pairs(carry, items):
        grads, loss_acc = carry
        coords, charge, trk, live = items
        row_sums, pot_rows, pulls, point_grads = pair_terms(coords, charge, trk, live, point_rows, 0, hits_all)
        coord_grad = coords * row_sums[None, :] - pulls
        return ((grads + point_grads, loss_acc + jnp.sum(charge * pot_rows) / hits_all), (coord_grad, pot_rows))
    init = (jnp.zeros((CDIM + 1, K), jnp.float32), jnp.zeros((), jnp.float32))
    (point_grads, loss_pot), (coord_grads, pot_all) = lax.scan(scan_pairs, init, (coords_all, charge_all, track_blocks, live_blocks))
    coord_grads = coord_grads.at[owner, :, point_hit].add(point_grads[:CDIM].T)
    charge_grad = (pot_all / hits_all).at[owner, point_hit].add(point_grads[CDIM])
    noise_float = noise_blocks.astype(jnp.float32)
    beta_grad = (noise_float / hits_all).at[owner, point_hit].add(-1.0 / K)
    logit_grads = charge_grad * slope_all + beta_grad * beta_all * (1.0 - beta_all)
    loss = loss_pot + jnp.sum(1.0 - beta_all[owner, point_hit]) / K + jnp.sum(noise_float * beta_all) / hits_all

    def scan_back(carry, items):
        feat, coord_grad, logit_grad = items
        states, preacts, coords, logits = mlp_forward(feat, w_layers, b_layers, w_coord, w_beta)
        parts = head_backward(states, preacts, w_layers, w_coord, w_beta, coord_grad, logit_grad)
        return (tuple((total + part for total, part in zip(carry, parts))), None)
    zeros = (jnp.zeros((LAYERS, WIDTH, WIDTH), jnp.float32), jnp.zeros((LAYERS, WIDTH), jnp.float32), jnp.zeros((CDIM, WIDTH), jnp.float32), jnp.zeros((WIDTH,), jnp.float32))
    totals, unused = lax.scan(scan_back, zeros, (feat_blocks, coord_grads, logit_grads))
    return (totals[0], totals[1], totals[2], totals[3], loss)
```

```python
import jax
import jax.numpy as jnp
from jax import lax
from jax.sharding import PartitionSpec as P
from jax.experimental import pallas as pl
from jax.experimental.pallas import tpu as pltpu

f32 = jnp.float32
bf16 = jnp.bfloat16
dist_eps = 0.0001
charge_floor = 0.5
MESH = pl.DeviceIdType.MESH
HITS = 65536.0
POINTS = 2048.0


def split3(v):
    hi = v.astype(bf16).astype(f32)
    rest = v - hi
    mid = rest.astype(bf16).astype(f32)
    low = (rest - mid).astype(bf16).astype(f32)
    return hi, mid, low


def rows_of(shape):
    return lax.broadcasted_iota(jnp.int32, shape, 0)


def lanes_of(shape):
    return lax.broadcasted_iota(jnp.int32, shape, 1)


def nt_dot(a, b):
    return lax.dot_general(a, b, (((1,), (1,)), ((), ())), preferred_element_type=f32)


def tn_dot(a, b):
    return lax.dot_general(a, b, (((0,), (0,)), ((), ())), preferred_element_type=f32)


def kernel(
    feat_ref, w_ref, b_ref, wc_ref, wb_ref, hit_ref, track_ref, noise_ref,
    gw_ref, gb_ref, gc_ref, gbeta_ref, loss_ref,
    pre_ref, act_ref, actt_ref,
    hits_ref, hits_back, hits_out, pts_ref, pts_back, pts_out,
    ycat_ref, yqt_ref, qp_ref, id_ref, pot_ref, ptacc_ref,
    part_ref, core_in, xy_in, zsum_ref, full_ref,
    s_hit, r_hit, s_pt, r_pt, s_hb, r_hb, s_pb, r_pb,
    s_core, r_core, s_xy, r_xy, s_z, r_z, s_g, r_g, s_f, r_f,
):
    lay = lax.axis_index("layer")
    phi = lax.axis_index("phi")
    z = (lay // 8) * 4 + phi % 4
    y = (lay // 2) % 4
    core = lay % 2
    x = phi // 4
    other = 1 - core
    here = x * 4 + y

    def device(px, py, pz, pc):
        return ((pz // 4) * 8 + py * 2 + pc, px * 4 + pz % 4)

    def plane(step):
        return device((x + step // 4) % 4, (y + step % 4) % 4, z, core)

    def plane_back(step):
        return device((x + 4 - step // 4) % 4, (y + 4 - step % 4) % 4, z, core)

    def column(step):
        return device(x, y, (z + step // 2) % 8, (core + step % 2) % 2)

    def column_back(step):
        return device(x, y, (z + 8 - step // 2) % 8, (core + 2 - step % 2) % 2)

    def ring(step):
        return device(x, y, (z + step) % 8, core)

    partner = device(x, y, z, other)

    def copy(src, dst, ssem, rsem, target):
        return pltpu.make_async_remote_copy(
            src_ref=src, dst_ref=dst, send_sem=ssem, recv_sem=rsem,
            device_id=target, device_id_type=MESH,
        )

    def each(first, last, body):
        def step(i, carry):
            body(i)
            return carry
        lax.fori_loop(first, last, step, 0)

    barrier = pltpu.get_barrier_semaphore()

    def greet(i):
        pl.semaphore_signal(barrier, inc=1, device_id=plane(i), device_id_type=MESH)
        pl.semaphore_signal(barrier, inc=1, device_id=column(i), device_id_type=MESH)
    each(1, 16, greet)

    hidden = feat_ref[...]
    for layer in range(4):
        pre = jnp.dot(hidden, w_ref[layer], preferred_element_type=f32) + b_ref[layer : layer + 1, :]
        pre_ref[layer] = pre
        hidden = (pre * jax.nn.sigmoid(pre)).astype(bf16)
        act_ref[layer] = hidden
    wcb = jnp.concatenate(
        [
            wc_ref[...].astype(f32),
            jnp.where(rows_of((16, 256)) == 0, wb_ref[...].astype(f32).reshape(1, 256), 0.0),
        ],
        0,
    ).astype(bf16)
    xz = nt_dot(wcb, hidden)
    coords = xz[0:16]
    logits = xz[16:17]
    expz = jnp.exp(logits)
    spread = jnp.log1p(2.0 * expz)
    charge = 0.25 * spread * spread + charge_floor
    slope = 0.5 * spread * (2.0 * expz / (1.0 + 2.0 * expz))
    beta = jax.nn.sigmoid(logits)
    noise = noise_ref[...].reshape(1, 256)
    track = track_ref[...].reshape(1, 256)
    key = jnp.where(noise == 0, track, -1).astype(f32)
    noise_f = noise.astype(f32)
    square = jnp.sum(coords * coords, 0, keepdims=True)
    row8 = rows_of((8, 256))
    lane8 = lanes_of((8, 256))
    pack = jnp.where(row8 == 0, charge, jnp.where(row8 == 1, key, jnp.where(row8 == 2, square, 0.0)))
    mine = jnp.concatenate([coords, pack], 0)
    hits_ref[0] = mine
    sel = jnp.zeros((8, 256), f32)
    for k in range(8):
        sel = jnp.where((row8 == k) & (lane8 == hit_ref[k]), 1.0, sel)
    sel_low = sel.astype(bf16)
    mine128 = jnp.concatenate([mine, jnp.zeros((104, 256), f32)], 0)
    mh, mm, ml = split3(mine128)
    own_pts = (nt_dot(sel_low, mh.astype(bf16)) + nt_dot(sel_low, mm.astype(bf16))) + nt_dot(sel_low, ml.astype(bf16))
    linear = lay * 16 + phi
    ident = (linear * 8 + rows_of((8, 128))).astype(f32)
    own_pts = jnp.where(lanes_of((8, 128)) == 17, ident, own_pts)
    pts_ref[0] = own_pts

    pl.semaphore_wait(barrier, 30)

    def pt_copy(i):
        return copy(pts_ref.at[0], pts_ref.at[i], s_pt.at[i], r_pt.at[i], column(i))

    def hit_copy(i):
        return copy(hits_ref.at[0], hits_ref.at[i], s_hit.at[i], r_hit.at[i], plane(i))

    each(1, 16, lambda i: pt_copy(i).start())
    each(1, 16, lambda i: hit_copy(i).start())

    actt_ref[0] = feat_ref[...].T
    for layer in range(4):
        pre = pre_ref[layer]
        sig = jax.nn.sigmoid(pre)
        pre_ref[layer] = sig * (1.0 + pre * (1.0 - sig))
        if layer < 3:
            actt_ref[layer + 1] = act_ref[layer].T
    ptacc_ref[...] = jnp.zeros((128, 128), f32)
    pot_ref[...] = jnp.zeros((128, 256), f32)

    each(1, 16, lambda i: pt_copy(i).wait())
    points = pts_ref[...].reshape(128, 128)
    qp_ref[...] = jnp.broadcast_to(points[:, 16:17], (128, 256))
    id_ref[...] = jnp.broadcast_to(points[:, 17:18], (128, 256))
    pt = points.T
    y_t = pt[0:16]
    qp_t = pt[16:17]
    yh, ym, yl = split3(-2.0 * y_t)
    sqh, sqm, sql = split3(pt[18:19])
    row16 = rows_of((16, 128))
    tail = jnp.where(row16 < 3, 1.0, jnp.where(row16 == 3, sqh, jnp.where(row16 == 4, sqm, jnp.where(row16 == 5, sql, 0.0))))
    ycat_ref[...] = jnp.concatenate([yh, yh, ym, ym, yh, yl, tail, jnp.zeros((16, 128), f32)], 0).T.astype(bf16)
    yq = jnp.concatenate([y_t * qp_t, jnp.where(row16 == 0, qp_t, 0.0)], 0)
    yqh, yqm, yql = split3(yq)
    yqt = jnp.concatenate([yqh, yqm, yql], 0).astype(bf16)
    yqt_ref[...] = jnp.concatenate([yqt, yqt], 1)

    def hb_copy(i):
        return copy(hits_out.at[i], hits_back.at[i], s_hb.at[i], r_hb.at[i], plane_back(i))

    def pairs(i):
        @pl.when(i > 0)
        def _():
            hit_copy(i).wait()

        blk = hits_ref[i]
        xs = blk[0:16]
        q = blk[16:17]
        key_i = blk[17:18]
        xh, xm, xl = split3(xs)
        sh, sm, sl = split3(blk[18:19])
        r16 = rows_of((16, 256))
        tail_x = jnp.where(r16 == 0, sh, jnp.where(r16 == 1, sm, jnp.where(r16 == 2, sl, jnp.where(r16 < 6, 1.0, 0.0))))
        xcat = jnp.concatenate([xh, xm, xh, xm, xl, xh, tail_x, jnp.zeros((16, 256), f32)], 0).astype(bf16)
        d2 = jnp.maximum(jnp.dot(ycat_ref[...], xcat, preferred_element_type=f32), 0.0)
        t = d2 + dist_eps
        inv = lax.rsqrt(t)
        reach = jnp.maximum(1.0 - t * inv, 0.0)
        match = id_ref[...] == key_i
        pot = jnp.where(match, d2, reach * reach)
        cc = jnp.where(match, 1.0, -(reach * inv))
        pot_rows = jnp.sum(pot * qp_ref[...], 0, keepdims=True)
        pot_ref[...] += pot * q
        cc_hi = cc.astype(bf16)
        cc_lo = (cc - cc_hi.astype(f32)).astype(bf16)
        ht = jnp.dot(yqt_ref[...], jnp.concatenate([cc_hi, cc_lo], 0), preferred_element_type=f32)
        ht = (ht[0:32] + ht[32:64]) + ht[64:96]
        hits_out[i] = jnp.concatenate([ht[0:16], jnp.where(row8 == 1, pot_rows, ht[16:24])], 0)
        xq = jnp.concatenate([xs * q, jnp.where(r16 == 0, q, 0.0)], 0)
        xqh, xqm, xql = split3(xq)
        xq_all = jnp.concatenate([xqh, xqm, xql, jnp.zeros((32, 256), f32)], 0).astype(bf16)
        ptacc_ref[...] += nt_dot(cc_hi, xq_all) + nt_dot(cc_lo, xq_all)

        @pl.when(i > 0)
        def _():
            hb_copy(i).start()

    each(0, 16, pairs)

    acc = ptacc_ref[...]
    acc = (acc + pltpu.roll(acc, 96, 1)) + pltpu.roll(acc, 64, 1)
    pot_cols = jnp.sum(pot_ref[...], 1, keepdims=True)
    pts_out[...] = jnp.where(lanes_of((128, 128)) == 17, pot_cols, acc).reshape(16, 8, 128)

    def pb_copy(i):
        return copy(pts_out.at[i], pts_back.at[i], s_pb.at[i], r_pb.at[i], column_back(i))

    each(1, 16, lambda i: pb_copy(i).start())
    each(1, 16, lambda i: hb_copy(i).wait())
    hsum = hits_out[0]
    for i in range(1, 16):
        hsum = hsum + hits_back[i]
    pot_i = hsum[17:18]
    coord_grad = (2.0 * charge / HITS) * (coords * hsum[16:17] - hsum[0:16])
    each(1, 16, lambda i: pb_copy(i).wait())
    psum = pts_out[0]
    for i in range(1, 16):
        psum = psum + pts_back[i]
    lane = lanes_of((8, 128))
    grads = jnp.where(
        lane < 16,
        (2.0 * own_pts[:, 16:17] / HITS) * (own_pts * psum[:, 16:17] - psum),
        jnp.where(lane == 16, psum[:, 17:18] / HITS, 0.0),
    )
    gh, gm, gl = split3(grads)
    zeros8 = jnp.zeros((8, 128), f32)
    g3 = jnp.concatenate([gh, gm, gl, zeros8], 0).astype(bf16)
    sel3 = jnp.concatenate([sel, sel, sel, jnp.zeros((8, 256), f32)], 0).astype(bf16)
    spread_back = tn_dot(g3, sel3)
    count = jnp.sum(sel, 0, keepdims=True)
    coord_grad = coord_grad + spread_back[0:16]
    charge_grad = pot_i / HITS + spread_back[16:17]
    beta_grad = noise_f / HITS - count * (1.0 / POINTS)
    logit_grad = charge_grad * slope + beta_grad * beta * (1.0 - beta)
    loss_row = charge * pot_i / HITS + (count - count * beta) / POINTS + noise_f * beta / HITS
    loss_local = jnp.sum(loss_row, 1, keepdims=True)

    low = jnp.concatenate([coord_grad, jnp.where(rows_of((16, 256)) == 0, logit_grad, 0.0)], 0).astype(bf16)
    head = jnp.dot(low, act_ref[3], preferred_element_type=f32)
    up = tn_dot(low, wcb)

    def core_copy(j):
        if j < 4:
            src = part_ref.at[other, :, pl.ds(2 * j, 2)]
            dst = core_in.at[:, pl.ds(2 * j, 2)]
        else:
            src = part_ref.at[other, :, pl.ds(8, 1)]
            dst = core_in.at[:, pl.ds(8, 1)]
        return copy(src, dst, s_core.at[j], r_core.at[j], partner)

    biases = [None] * 4
    for layer in range(3, -1, -1):
        local = (up * pre_ref[layer]).astype(bf16)
        wg = jnp.dot(actt_ref[layer], local, preferred_element_type=f32)
        for half in range(2):
            part_ref[:, :, 2 * layer + half] = wg[:, half * 128 : half * 128 + 128].reshape(2, 16, 8, 128)
        core_copy(layer).start()
        biases[layer] = jnp.sum(local.astype(f32), 0, keepdims=True)
        if layer > 0:
            up = nt_dot(local, w_ref[layer])
    ext8 = jnp.where(
        row8 == 0,
        head[16:17],
        jnp.where(
            row8 == 1,
            biases[0],
            jnp.where(
                row8 == 2,
                biases[1],
                jnp.where(row8 == 3, biases[2], jnp.where(row8 == 4, biases[3], jnp.where(row8 == 5, loss_local, 0.0))),
            ),
        ),
    )
    ext = jnp.concatenate([head[0:16], ext8], 0)
    for half in range(2):
        cols = ext[:, half * 128 : half * 128 + 128].reshape(3, 8, 128)
        part_ref[half, :, 8] = jnp.concatenate([cols, jnp.zeros((13, 8, 128), f32)], 0)
    core_copy(4).start()
    for j in (3, 2, 1, 0, 4):
        core_copy(j).wait()
    part_ref[core] = part_ref[core] + core_in[...]

    def xy_copy(i):
        target = ((x + i // 4) % 4) * 4 + (y + i % 4) % 4
        return copy(part_ref.at[core, target], xy_in.at[i], s_xy.at[i], r_xy.at[i], plane(i))

    each(1, 16, lambda i: xy_copy(i).start())
    each(1, 16, lambda i: xy_copy(i).wait())
    total = part_ref[core, here]
    for i in range(1, 16):
        total = total + xy_in[i]
    zsum_ref[z] = total

    def z_copy(i):
        return copy(zsum_ref.at[z], zsum_ref.at[z], s_z.at[i], r_z.at[i], ring(i))

    each(1, 8, lambda i: z_copy(i).start())
    each(1, 8, lambda i: z_copy(i).wait())
    total = zsum_ref[0]
    for i in range(1, 8):
        total = total + zsum_ref[i]
    full_ref[core, here] = total

    def g_copy(i):
        return copy(full_ref.at[core, here], full_ref.at[core, here], s_g.at[i], r_g.at[i], plane(i))

    def f_copy(i):
        block = ((x + 4 - i // 4) % 4) * 4 + (y + 4 - i % 4) % 4
        return copy(full_ref.at[core, block], full_ref.at[core, block], s_f.at[i], r_f.at[i], partner)

    each(1, 16, lambda i: g_copy(i).start())
    f_copy(0).start()

    def forward_on(i):
        g_copy(i).wait_recv()
        f_copy(i).start()

    each(1, 16, forward_on)
    each(1, 16, lambda i: g_copy(i).wait_send())
    each(0, 16, lambda i: f_copy(i).wait())
    for layer in range(4):
        for half in range(2):
            gw_ref[layer, :, half * 128 : half * 128 + 128] = full_ref[:, :, 2 * layer + half].reshape(256, 128)
    gc_ref[...] = jnp.concatenate(
        [full_ref[half, 0:2, 8].reshape(16, 128) for half in range(2)], 1
    )
    last = jnp.concatenate([full_ref[half, 2, 8] for half in range(2)], 1)
    gbeta_ref[...] = last[0:1]
    gb_ref[...] = last[1:5]
    loss_ref[...] = last[5:6, 0:128]


def on_device(features, w_layers, b_layers, w_coord, w_beta, point_hit, track, noise):
    vmem = pl.BlockSpec(memory_space=pltpu.VMEM)
    smem = pl.BlockSpec(memory_space=pltpu.SMEM)
    dma = pltpu.SemaphoreType.DMA
    grad_w, grad_b, grad_c, grad_beta, loss = pl.pallas_call(
        kernel,
        name="condense",
        out_shape=(
            jax.ShapeDtypeStruct((4, 256, 256), f32),
            jax.ShapeDtypeStruct((4, 256), f32),
            jax.ShapeDtypeStruct((16, 256), f32),
            jax.ShapeDtypeStruct((1, 256), f32),
            jax.ShapeDtypeStruct((1, 128), f32),
        ),
        in_specs=[vmem] * 5 + [smem] + [vmem] * 2,
        out_specs=(vmem,) * 5,
        scratch_shapes=[
            pltpu.VMEM((4, 256, 256), f32),
            pltpu.VMEM((4, 256, 256), bf16),
            pltpu.VMEM((4, 256, 256), bf16),
            pltpu.VMEM((16, 24, 256), f32),
            pltpu.VMEM((16, 24, 256), f32),
            pltpu.VMEM((16, 24, 256), f32),
            pltpu.VMEM((16, 8, 128), f32),
            pltpu.VMEM((16, 8, 128), f32),
            pltpu.VMEM((16, 8, 128), f32),
            pltpu.VMEM((128, 128), bf16),
            pltpu.VMEM((96, 256), bf16),
            pltpu.VMEM((128, 256), f32),
            pltpu.VMEM((128, 256), f32),
            pltpu.VMEM((128, 256), f32),
            pltpu.VMEM((128, 128), f32),
            pltpu.VMEM((2, 16, 9, 8, 128), f32),
            pltpu.VMEM((16, 9, 8, 128), f32),
            pltpu.VMEM((16, 9, 8, 128), f32),
            pltpu.VMEM((8, 9, 8, 128), f32),
            pltpu.VMEM((2, 16, 9, 8, 128), f32),
            dma((16,)), dma((16,)), dma((16,)), dma((16,)),
            dma((16,)), dma((16,)), dma((16,)), dma((16,)),
            dma((5,)), dma((5,)), dma((16,)), dma((16,)),
            dma((8,)), dma((8,)), dma((16,)), dma((16,)),
            dma((16,)), dma((16,)),
        ],
        compiler_params=pltpu.CompilerParams(
            collective_id=0, has_side_effects=True, vmem_limit_bytes=48 << 20
        ),
    )(features, w_layers, b_layers, w_coord, w_beta, point_hit, track, noise)
    return grad_w, grad_b, grad_c, grad_beta.reshape(256), loss[0, 0]


def solution(mesh):
    return jax.shard_map(
        on_device,
        mesh=mesh,
        in_specs=(
            P(("layer", "phi"), None),
            P(),
            P(),
            P(),
            P(),
            P(("layer", "phi")),
            P(("layer", "phi")),
            P(("layer", "phi")),
        ),
        out_specs=(P(), P(), P(), P(), P()),
        check_vma=False,
    )
```

```python
import jax
import jax.numpy as jnp
from jax import lax
from jax.sharding import PartitionSpec as P
from jax.experimental import pallas as pl
from jax.experimental.pallas import tpu as pltpu

f32 = jnp.float32
bf16 = jnp.bfloat16
dist_eps = 0.0001
charge_floor = 0.5
MESH = pl.DeviceIdType.MESH
HITS = 65536.0
POINTS = 2048.0


def split3(v):
    hi = v.astype(bf16).astype(f32)
    rest = v - hi
    mid = rest.astype(bf16).astype(f32)
    low = (rest - mid).astype(bf16).astype(f32)
    return hi, mid, low


def rows_of(shape):
    return lax.broadcasted_iota(jnp.int32, shape, 0)


def lanes_of(shape):
    return lax.broadcasted_iota(jnp.int32, shape, 1)


def nt_dot(a, b):
    return lax.dot_general(a, b, (((1,), (1,)), ((), ())), preferred_element_type=f32)


def tn_dot(a, b):
    return lax.dot_general(a, b, (((0,), (0,)), ((), ())), preferred_element_type=f32)


def kernel(
    feat_hbm, w_hbm, b_hbm, wc_hbm, wb_hbm, hit_hbm, track_hbm, noise_hbm,
    gw_ref, gb_ref, gc_ref, gbeta_ref, loss_ref,
    feat_ref, w_ref, b_ref, wc_ref, wb_ref, hit_ref, track_ref, noise_ref, s_in,
    pre_ref, act_ref, actt_ref,
    hits_ref, hits_back, hits_out, pts_ref, pts_back, pts_out,
    ycat_ref, yqt_ref, qp_ref, id_ref, pot_ref, ptacc_ref,
    part_ref, core_in, xy_in, zsum_ref, full_ref,
    s_hit, r_hit, s_pt, r_pt, s_hb, r_hb, s_pb, r_pb,
    s_core, r_core, s_xy, r_xy, s_z, r_z, s_g, r_g, s_f, r_f,
):
    loads = [
        pltpu.make_async_copy(src, dst, s_in.at[i])
        for i, (src, dst) in enumerate(
            [
                (feat_hbm, feat_ref),
                (w_hbm.at[0], w_ref.at[0]),
                (b_hbm, b_ref),
                (w_hbm.at[1], w_ref.at[1]),
                (w_hbm.at[2], w_ref.at[2]),
                (w_hbm.at[3], w_ref.at[3]),
                (wc_hbm, wc_ref),
                (wb_hbm, wb_ref),
                (track_hbm, track_ref),
                (noise_hbm, noise_ref),
                (hit_hbm, hit_ref),
            ]
        )
    ]
    for load in loads:
        load.start()
    lay = lax.axis_index("layer")
    phi = lax.axis_index("phi")
    z = (lay // 8) * 4 + phi % 4
    y = (lay // 2) % 4
    core = lay % 2
    x = phi // 4
    other = 1 - core
    here = x * 4 + y

    def device(px, py, pz, pc):
        return ((pz // 4) * 8 + py * 2 + pc, px * 4 + pz % 4)

    def plane(step):
        return device((x + step // 4) % 4, (y + step % 4) % 4, z, core)

    def plane_back(step):
        return device((x + 4 - step // 4) % 4, (y + 4 - step % 4) % 4, z, core)

    def column(step):
        return device(x, y, (z + step // 2) % 8, (core + step % 2) % 2)

    def column_back(step):
        return device(x, y, (z + 8 - step // 2) % 8, (core + 2 - step % 2) % 2)

    def ring(step):
        return device(x, y, (z + step) % 8, core)

    partner = device(x, y, z, other)

    def copy(src, dst, ssem, rsem, target):
        return pltpu.make_async_remote_copy(
            src_ref=src, dst_ref=dst, send_sem=ssem, recv_sem=rsem,
            device_id=target, device_id_type=MESH,
        )

    def each(first, last, body):
        def step(i, carry):
            body(i)
            return carry
        lax.fori_loop(first, last, step, 0)

    barrier = pltpu.get_barrier_semaphore()

    def greet(i):
        pl.semaphore_signal(barrier, inc=1, device_id=plane(i), device_id_type=MESH)
        pl.semaphore_signal(barrier, inc=1, device_id=column(i), device_id_type=MESH)
    each(1, 16, greet)

    for load in loads[0:3]:
        load.wait()
    hidden = feat_ref[...]
    for layer in range(4):
        if layer > 0:
            loads[2 + layer].wait()
        pre = jnp.dot(hidden, w_ref[layer], preferred_element_type=f32) + b_ref[layer : layer + 1, :]
        pre_ref[layer] = pre
        hidden = (pre * jax.nn.sigmoid(pre)).astype(bf16)
        act_ref[layer] = hidden
    for load in loads[6:11]:
        load.wait()
    wcb = jnp.concatenate(
        [
            wc_ref[...].astype(f32),
            jnp.where(rows_of((16, 256)) == 0, wb_ref[...].astype(f32).reshape(1, 256), 0.0),
        ],
        0,
    ).astype(bf16)
    xz = nt_dot(wcb, hidden)
    coords = xz[0:16]
    logits = xz[16:17]
    expz = jnp.exp(logits)
    spread = jnp.log1p(2.0 * expz)
    charge = 0.25 * spread * spread + charge_floor
    slope = 0.5 * spread * (2.0 * expz / (1.0 + 2.0 * expz))
    beta = jax.nn.sigmoid(logits)
    noise = noise_ref[...].reshape(1, 256)
    track = track_ref[...].reshape(1, 256)
    key = jnp.where(noise == 0, track, -1).astype(f32)
    noise_f = noise.astype(f32)
    square = jnp.sum(coords * coords, 0, keepdims=True)
    row8 = rows_of((8, 256))
    lane8 = lanes_of((8, 256))
    pack = jnp.where(row8 == 0, charge, jnp.where(row8 == 1, key, jnp.where(row8 == 2, square, 0.0)))
    mine = jnp.concatenate([coords, pack], 0)
    hits_ref[0] = mine
    sel = jnp.zeros((8, 256), f32)
    for k in range(8):
        sel = jnp.where((row8 == k) & (lane8 == hit_ref[k]), 1.0, sel)
    sel_low = sel.astype(bf16)
    mine128 = jnp.concatenate([mine, jnp.zeros((104, 256), f32)], 0)
    mh, mm, ml = split3(mine128)
    own_pts = (nt_dot(sel_low, mh.astype(bf16)) + nt_dot(sel_low, mm.astype(bf16))) + nt_dot(sel_low, ml.astype(bf16))
    linear = lay * 16 + phi
    ident = (linear * 8 + rows_of((8, 128))).astype(f32)
    own_pts = jnp.where(lanes_of((8, 128)) == 17, ident, own_pts)
    pts_ref[0] = own_pts

    pl.semaphore_wait(barrier, 30)

    def pt_copy(i):
        return copy(pts_ref.at[0], pts_ref.at[i], s_pt.at[i], r_pt.at[i], column(i))

    def hit_copy(i):
        return copy(hits_ref.at[0], hits_ref.at[i], s_hit.at[i], r_hit.at[i], plane(i))

    each(1, 16, lambda i: pt_copy(i).start())
    each(1, 16, lambda i: hit_copy(i).start())

    actt_ref[0] = feat_ref[...].T
    for layer in range(4):
        pre = pre_ref[layer]
        sig = jax.nn.sigmoid(pre)
        pre_ref[layer] = sig * (1.0 + pre * (1.0 - sig))
        if layer < 3:
            actt_ref[layer + 1] = act_ref[layer].T
    ptacc_ref[...] = jnp.zeros((128, 128), f32)
    pot_ref[...] = jnp.zeros((128, 256), f32)

    each(1, 16, lambda i: pt_copy(i).wait())
    points = pts_ref[...].reshape(128, 128)
    qp_ref[...] = jnp.broadcast_to(points[:, 16:17], (128, 256))
    id_ref[...] = jnp.broadcast_to(points[:, 17:18], (128, 256))
    pt = points.T
    y_t = pt[0:16]
    qp_t = pt[16:17]
    yh, ym, yl = split3(-2.0 * y_t)
    sqh, sqm, sql = split3(pt[18:19])
    row16 = rows_of((16, 128))
    tail = jnp.where(row16 < 3, 1.0, jnp.where(row16 == 3, sqh, jnp.where(row16 == 4, sqm, jnp.where(row16 == 5, sql, 0.0))))
    ycat_ref[...] = jnp.concatenate([yh, yh, ym, ym, yh, yl, tail, jnp.zeros((16, 128), f32)], 0).T.astype(bf16)
    yq = jnp.concatenate([y_t * qp_t, jnp.where(row16 == 0, qp_t, 0.0)], 0)
    yqh, yqm, yql = split3(yq)
    yqt = jnp.concatenate([yqh, yqm, yql], 0).astype(bf16)
    yqt_ref[...] = jnp.concatenate([yqt, yqt], 1)

    def hb_copy(i):
        return copy(hits_out.at[i], hits_back.at[i], s_hb.at[i], r_hb.at[i], plane_back(i))

    def pairs(i):
        @pl.when(i > 0)
        def _():
            hit_copy(i).wait()

        blk = hits_ref[i]
        xs = blk[0:16]
        q = blk[16:17]
        key_i = blk[17:18]
        xh, xm, xl = split3(xs)
        sh, sm, sl = split3(blk[18:19])
        r16 = rows_of((16, 256))
        tail_x = jnp.where(r16 == 0, sh, jnp.where(r16 == 1, sm, jnp.where(r16 == 2, sl, jnp.where(r16 < 6, 1.0, 0.0))))
        xcat = jnp.concatenate([xh, xm, xh, xm, xl, xh, tail_x, jnp.zeros((16, 256), f32)], 0).astype(bf16)
        d2 = jnp.maximum(jnp.dot(ycat_ref[...], xcat, preferred_element_type=f32), 0.0)
        t = d2 + dist_eps
        inv = lax.rsqrt(t)
        reach = jnp.maximum(1.0 - t * inv, 0.0)
        match = id_ref[...] == key_i
        pot = jnp.where(match, d2, reach * reach)
        cc = jnp.where(match, 1.0, -(reach * inv))
        pot_rows = jnp.sum(pot * qp_ref[...], 0, keepdims=True)
        pot_ref[...] += pot * q
        cc_hi = cc.astype(bf16)
        cc_lo = (cc - cc_hi.astype(f32)).astype(bf16)
        ht = jnp.dot(yqt_ref[...], jnp.concatenate([cc_hi, cc_lo], 0), preferred_element_type=f32)
        ht = (ht[0:32] + ht[32:64]) + ht[64:96]
        hits_out[i] = jnp.concatenate([ht[0:16], jnp.where(row8 == 1, pot_rows, ht[16:24])], 0)
        xq = jnp.concatenate([xs * q, jnp.where(r16 == 0, q, 0.0)], 0)
        xqh, xqm, xql = split3(xq)
        xq_all = jnp.concatenate([xqh, xqm, xql, jnp.zeros((32, 256), f32)], 0).astype(bf16)
        ptacc_ref[...] += nt_dot(cc_hi, xq_all) + nt_dot(cc_lo, xq_all)

        @pl.when(i > 0)
        def _():
            hb_copy(i).start()

    each(0, 16, pairs)

    acc = ptacc_ref[...]
    acc = (acc + pltpu.roll(acc, 96, 1)) + pltpu.roll(acc, 64, 1)
    pot_cols = jnp.sum(pot_ref[...], 1, keepdims=True)
    pts_out[...] = jnp.where(lanes_of((128, 128)) == 17, pot_cols, acc).reshape(16, 8, 128)

    def pb_copy(i):
        return copy(pts_out.at[i], pts_back.at[i], s_pb.at[i], r_pb.at[i], column_back(i))

    each(1, 16, lambda i: pb_copy(i).start())
    each(1, 16, lambda i: hb_copy(i).wait())
    hsum = hits_out[0]
    for i in range(1, 16):
        hsum = hsum + hits_back[i]
    pot_i = hsum[17:18]
    coord_grad = (2.0 * charge / HITS) * (coords * hsum[16:17] - hsum[0:16])
    each(1, 16, lambda i: pb_copy(i).wait())
    psum = pts_out[0]
    for i in range(1, 16):
        psum = psum + pts_back[i]
    lane = lanes_of((8, 128))
    grads = jnp.where(
        lane < 16,
        (2.0 * own_pts[:, 16:17] / HITS) * (own_pts * psum[:, 16:17] - psum),
        jnp.where(lane == 16, psum[:, 17:18] / HITS, 0.0),
    )
    gh, gm, gl = split3(grads)
    zeros8 = jnp.zeros((8, 128), f32)
    g3 = jnp.concatenate([gh, gm, gl, zeros8], 0).astype(bf16)
    sel3 = jnp.concatenate([sel, sel, sel, jnp.zeros((8, 256), f32)], 0).astype(bf16)
    spread_back = tn_dot(g3, sel3)
    count = jnp.sum(sel, 0, keepdims=True)
    coord_grad = coord_grad + spread_back[0:16]
    charge_grad = pot_i / HITS + spread_back[16:17]
    beta_grad = noise_f / HITS - count * (1.0 / POINTS)
    logit_grad = charge_grad * slope + beta_grad * beta * (1.0 - beta)
    loss_row = charge * pot_i / HITS + (count - count * beta) / POINTS + noise_f * beta / HITS
    loss_local = jnp.sum(loss_row, 1, keepdims=True)

    low = jnp.concatenate([coord_grad, jnp.where(rows_of((16, 256)) == 0, logit_grad, 0.0)], 0).astype(bf16)
    head = jnp.dot(low, act_ref[3], preferred_element_type=f32)
    up = tn_dot(low, wcb)

    def core_copy(j):
        if j < 4:
            src = part_ref.at[other, :, pl.ds(2 * j, 2)]
            dst = core_in.at[:, pl.ds(2 * j, 2)]
        else:
            src = part_ref.at[other, :, pl.ds(8, 1)]
            dst = core_in.at[:, pl.ds(8, 1)]
        return copy(src, dst, s_core.at[j], r_core.at[j], partner)

    biases = [None] * 4
    for layer in range(3, -1, -1):
        local = (up * pre_ref[layer]).astype(bf16)
        wg = jnp.dot(actt_ref[layer], local, preferred_element_type=f32)
        for half in range(2):
            part_ref[:, :, 2 * layer + half] = wg[:, half * 128 : half * 128 + 128].reshape(2, 16, 8, 128)
        core_copy(layer).start()
        biases[layer] = jnp.sum(local.astype(f32), 0, keepdims=True)
        if layer > 0:
            up = nt_dot(local, w_ref[layer])
    ext8 = jnp.where(
        row8 == 0,
        head[16:17],
        jnp.where(
            row8 == 1,
            biases[0],
            jnp.where(
                row8 == 2,
                biases[1],
                jnp.where(row8 == 3, biases[2], jnp.where(row8 == 4, biases[3], jnp.where(row8 == 5, loss_local, 0.0))),
            ),
        ),
    )
    ext = jnp.concatenate([head[0:16], ext8], 0)
    for half in range(2):
        cols = ext[:, half * 128 : half * 128 + 128].reshape(3, 8, 128)
        part_ref[half, :, 8] = jnp.concatenate([cols, jnp.zeros((13, 8, 128), f32)], 0)
    core_copy(4).start()
    for j in (3, 2, 1, 0, 4):
        core_copy(j).wait()
    part_ref[core] = part_ref[core] + core_in[...]

    def xy_copy(i):
        target = ((x + i // 4) % 4) * 4 + (y + i % 4) % 4
        return copy(part_ref.at[core, target], xy_in.at[i], s_xy.at[i], r_xy.at[i], plane(i))

    each(1, 16, lambda i: xy_copy(i).start())
    each(1, 16, lambda i: xy_copy(i).wait())
    total = part_ref[core, here]
    for i in range(1, 16):
        total = total + xy_in[i]
    zsum_ref[z] = total

    def z_copy(i):
        return copy(zsum_ref.at[z], zsum_ref.at[z], s_z.at[i], r_z.at[i], ring(i))

    each(1, 8, lambda i: z_copy(i).start())
    each(1, 8, lambda i: z_copy(i).wait())
    total = zsum_ref[0]
    for i in range(1, 8):
        total = total + zsum_ref[i]
    full_ref[core, here] = total

    def g_copy(i):
        return copy(full_ref.at[core, here], full_ref.at[core, here], s_g.at[i], r_g.at[i], plane(i))

    def f_copy(i):
        block = ((x + 4 - i // 4) % 4) * 4 + (y + 4 - i % 4) % 4
        return copy(full_ref.at[core, block], full_ref.at[core, block], s_f.at[i], r_f.at[i], partner)

    each(1, 16, lambda i: g_copy(i).start())
    f_copy(0).start()

    def forward_on(i):
        g_copy(i).wait_recv()
        f_copy(i).start()

    each(1, 16, forward_on)
    each(1, 16, lambda i: g_copy(i).wait_send())
    each(0, 16, lambda i: f_copy(i).wait())
    for layer in range(4):
        for half in range(2):
            gw_ref[layer, :, half * 128 : half * 128 + 128] = full_ref[:, :, 2 * layer + half].reshape(256, 128)
    gc_ref[...] = jnp.concatenate(
        [full_ref[half, 0:2, 8].reshape(16, 128) for half in range(2)], 1
    )
    last = jnp.concatenate([full_ref[half, 2, 8] for half in range(2)], 1)
    gbeta_ref[...] = last[0:1]
    gb_ref[...] = last[1:5]
    loss_ref[...] = last[5:6, 0:1]


def deliver(*refs):
    sems = refs[10]
    copies = [pltpu.make_async_copy(refs[i], refs[5 + i], sems.at[i]) for i in range(5)]
    for copy in copies:
        copy.start()
    for copy in copies:
        copy.wait()


def on_device(features, w_layers, b_layers, w_coord, w_beta, point_hit, track, noise):
    vmem = pl.BlockSpec(memory_space=pltpu.VMEM)
    hbm = pl.BlockSpec(memory_space=pltpu.HBM)
    dma = pltpu.SemaphoreType.DMA
    results = (
        jax.ShapeDtypeStruct((4, 256, 256), f32),
        jax.ShapeDtypeStruct((4, 256), f32),
        jax.ShapeDtypeStruct((16, 256), f32),
        jax.ShapeDtypeStruct((1, 256), f32),
        jax.ShapeDtypeStruct((1, 1), f32),
    )
    grads = pl.pallas_call(
        kernel,
        name="condense",
        out_shape=results,
        in_specs=[hbm] * 8,
        out_specs=(vmem,) * 5,
        scratch_shapes=[
            pltpu.VMEM((256, 256), bf16),
            pltpu.VMEM((4, 256, 256), bf16),
            pltpu.VMEM((4, 256), f32),
            pltpu.VMEM((16, 256), bf16),
            pltpu.VMEM((256,), bf16),
            pltpu.SMEM((8,), jnp.int32),
            pltpu.VMEM((256,), jnp.int32),
            pltpu.VMEM((256,), jnp.int32),
            dma((11,)),
            pltpu.VMEM((4, 256, 256), f32),
            pltpu.VMEM((4, 256, 256), bf16),
            pltpu.VMEM((4, 256, 256), bf16),
            pltpu.VMEM((16, 24, 256), f32),
            pltpu.VMEM((16, 24, 256), f32),
            pltpu.VMEM((16, 24, 256), f32),
            pltpu.VMEM((16, 8, 128), f32),
            pltpu.VMEM((16, 8, 128), f32),
            pltpu.VMEM((16, 8, 128), f32),
            pltpu.VMEM((128, 128), bf16),
            pltpu.VMEM((96, 256), bf16),
            pltpu.VMEM((128, 256), f32),
            pltpu.VMEM((128, 256), f32),
            pltpu.VMEM((128, 256), f32),
            pltpu.VMEM((128, 128), f32),
            pltpu.VMEM((2, 16, 9, 8, 128), f32),
            pltpu.VMEM((16, 9, 8, 128), f32),
            pltpu.VMEM((16, 9, 8, 128), f32),
            pltpu.VMEM((8, 9, 8, 128), f32),
            pltpu.VMEM((2, 16, 9, 8, 128), f32),
            dma((16,)), dma((16,)), dma((16,)), dma((16,)),
            dma((16,)), dma((16,)), dma((16,)), dma((16,)),
            dma((5,)), dma((5,)), dma((16,)), dma((16,)),
            dma((8,)), dma((8,)), dma((16,)), dma((16,)),
            dma((16,)), dma((16,)),
        ],
        compiler_params=pltpu.CompilerParams(
            collective_id=0, has_side_effects=True, vmem_limit_bytes=48 << 20
        ),
    )(*[pltpu.with_memory_space_constraint(v, pltpu.HBM) for v in (features, w_layers, b_layers, w_coord, w_beta, point_hit, track, noise)])
    grad_w, grad_b, grad_c, grad_beta, loss = pl.pallas_call(
        deliver,
        name="deliver",
        out_shape=results,
        in_specs=[vmem] * 5,
        out_specs=(hbm,) * 5,
        scratch_shapes=[dma((5,))],
        compiler_params=pltpu.CompilerParams(vmem_limit_bytes=8 << 20),
    )(*grads)
    return grad_w, grad_b, grad_c, grad_beta.reshape(256), loss.reshape(())


def solution(mesh):
    return jax.shard_map(
        on_device,
        mesh=mesh,
        in_specs=(
            P(("layer", "phi"), None),
            P(),
            P(),
            P(),
            P(),
            P(("layer", "phi")),
            P(("layer", "phi")),
            P(("layer", "phi")),
        ),
        out_specs=(P(), P(), P(), P(), P()),
        check_vma=False,
    )
```

```python
import jax
import jax.numpy as jnp
from jax import lax
from jax.sharding import PartitionSpec as P
from jax.experimental import pallas as pl
from jax.experimental.pallas import tpu as pltpu

f32 = jnp.float32
bf16 = jnp.bfloat16
dist_eps = 0.0001
charge_floor = 0.5
MESH = pl.DeviceIdType.MESH
HITS = 65536.0
POINTS = 2048.0
chunks = ((0, 4), (4, 9))


def split3(v):
    hi = v.astype(bf16).astype(f32)
    rest = v - hi
    mid = rest.astype(bf16).astype(f32)
    low = (rest - mid).astype(bf16).astype(f32)
    return hi, mid, low


def rows_of(shape):
    return lax.broadcasted_iota(jnp.int32, shape, 0)


def lanes_of(shape):
    return lax.broadcasted_iota(jnp.int32, shape, 1)


def nt_dot(a, b):
    return lax.dot_general(a, b, (((1,), (1,)), ((), ())), preferred_element_type=f32)


def tn_dot(a, b):
    return lax.dot_general(a, b, (((0,), (0,)), ((), ())), preferred_element_type=f32)


def kernel(
    feat_hbm, w_hbm, b_hbm, wc_hbm, wb_hbm, hit_hbm, track_hbm, noise_hbm,
    gw_ref, gb_ref, gc_ref, gbeta_ref, loss_ref,
    feat_ref, w_ref, b_ref, wc_ref, wb_ref, hit_ref, track_ref, noise_ref, s_in,
    pre_ref, act_ref, actt_ref,
    hits_ref, hits_back, hits_out, pts_ref, pts_back, pts_out,
    ycat_ref, yqt_ref, qp_ref, id_ref, pot_ref, ptacc_ref,
    part_ref, core_in, xy_in, zsum_ref, full_ref,
    s_hit, r_hit, s_pt, r_pt, s_hb, r_hb, s_pb, r_pb,
    s_core, r_core, s_xy, r_xy, s_z, r_z, s_g, r_g, s_f, r_f,
):
    loads = [
        pltpu.make_async_copy(src, dst, s_in.at[i])
        for i, (src, dst) in enumerate(
            [
                (feat_hbm, feat_ref),
                (w_hbm.at[0], w_ref.at[0]),
                (b_hbm, b_ref),
                (w_hbm.at[1], w_ref.at[1]),
                (w_hbm.at[2], w_ref.at[2]),
                (w_hbm.at[3], w_ref.at[3]),
                (wc_hbm, wc_ref),
                (wb_hbm, wb_ref),
                (track_hbm, track_ref),
                (noise_hbm, noise_ref),
                (hit_hbm, hit_ref),
            ]
        )
    ]
    for load in loads:
        load.start()
    lay = lax.axis_index("layer")
    phi = lax.axis_index("phi")
    z = (lay // 8) * 4 + phi % 4
    y = (lay // 2) % 4
    core = lay % 2
    x = phi // 4
    other = 1 - core
    here = x * 4 + y

    def device(px, py, pz, pc):
        return ((pz // 4) * 8 + py * 2 + pc, px * 4 + pz % 4)

    def plane(step):
        return device((x + step // 4) % 4, (y + step % 4) % 4, z, core)

    def plane_back(step):
        return device((x + 4 - step // 4) % 4, (y + 4 - step % 4) % 4, z, core)

    def column(step):
        return device(x, y, (z + step // 2) % 8, (core + step % 2) % 2)

    def column_back(step):
        return device(x, y, (z + 8 - step // 2) % 8, (core + 2 - step % 2) % 2)

    def ring(step):
        return device(x, y, (z + step) % 8, core)

    partner = device(x, y, z, other)

    def copy(src, dst, ssem, rsem, target):
        return pltpu.make_async_remote_copy(
            src_ref=src, dst_ref=dst, send_sem=ssem, recv_sem=rsem,
            device_id=target, device_id_type=MESH,
        )

    def each(first, last, body):
        def step(i, carry):
            body(i)
            return carry
        lax.fori_loop(first, last, step, 0)

    barrier = pltpu.get_barrier_semaphore()

    def greet(i):
        pl.semaphore_signal(barrier, inc=1, device_id=plane(i), device_id_type=MESH)
        pl.semaphore_signal(barrier, inc=1, device_id=column(i), device_id_type=MESH)
    each(1, 16, greet)

    for load in loads[0:3]:
        load.wait()
    hidden = feat_ref[...]
    for layer in range(4):
        if layer > 0:
            loads[2 + layer].wait()
        pre = jnp.dot(hidden, w_ref[layer], preferred_element_type=f32) + b_ref[layer : layer + 1, :]
        pre_ref[layer] = pre
        hidden = (pre * jax.nn.sigmoid(pre)).astype(bf16)
        act_ref[layer] = hidden
    for load in loads[6:11]:
        load.wait()
    wcb = jnp.concatenate(
        [
            wc_ref[...].astype(f32),
            jnp.where(rows_of((16, 256)) == 0, wb_ref[...].astype(f32).reshape(1, 256), 0.0),
        ],
        0,
    ).astype(bf16)
    xz = nt_dot(wcb, hidden)
    coords = xz[0:16]
    logits = xz[16:17]
    expz = jnp.exp(logits)
    spread = jnp.log1p(2.0 * expz)
    charge = 0.25 * spread * spread + charge_floor
    slope = 0.5 * spread * (2.0 * expz / (1.0 + 2.0 * expz))
    beta = jax.nn.sigmoid(logits)
    noise = noise_ref[...].reshape(1, 256)
    track = track_ref[...].reshape(1, 256)
    key = jnp.where(noise == 0, track, -1).astype(f32)
    noise_f = noise.astype(f32)
    square = jnp.sum(coords * coords, 0, keepdims=True)
    row8 = rows_of((8, 256))
    lane8 = lanes_of((8, 256))
    pack = jnp.where(row8 == 0, charge, jnp.where(row8 == 1, key, jnp.where(row8 == 2, square, 0.0)))
    mine = jnp.concatenate([coords, pack], 0)
    hits_ref[0] = mine
    sel = jnp.zeros((8, 256), f32)
    for k in range(8):
        sel = jnp.where((row8 == k) & (lane8 == hit_ref[k]), 1.0, sel)
    sel_low = sel.astype(bf16)
    mine128 = jnp.concatenate([mine, jnp.zeros((104, 256), f32)], 0)
    mh, mm, ml = split3(mine128)
    own_pts = (nt_dot(sel_low, mh.astype(bf16)) + nt_dot(sel_low, mm.astype(bf16))) + nt_dot(sel_low, ml.astype(bf16))
    linear = lay * 16 + phi
    ident = (linear * 8 + rows_of((8, 128))).astype(f32)
    own_pts = jnp.where(lanes_of((8, 128)) == 17, ident, own_pts)
    pts_ref[0] = own_pts

    pl.semaphore_wait(barrier, 30)

    def pt_copy(i):
        return copy(pts_ref.at[0], pts_ref.at[i], s_pt.at[i], r_pt.at[i], column(i))

    def hit_copy(i):
        return copy(hits_ref.at[0], hits_ref.at[i], s_hit.at[i], r_hit.at[i], plane(i))

    each(1, 16, lambda i: pt_copy(i).start())
    each(1, 16, lambda i: hit_copy(i).start())

    actt_ref[0] = feat_ref[...].T
    for layer in range(4):
        pre = pre_ref[layer]
        sig = jax.nn.sigmoid(pre)
        pre_ref[layer] = sig * (1.0 + pre * (1.0 - sig))
        if layer < 3:
            actt_ref[layer + 1] = act_ref[layer].T
    ptacc_ref[...] = jnp.zeros((128, 128), f32)
    pot_ref[...] = jnp.zeros((128, 256), f32)

    each(1, 16, lambda i: pt_copy(i).wait())
    points = pts_ref[...].reshape(128, 128)
    qp_ref[...] = jnp.broadcast_to(points[:, 16:17], (128, 256))
    id_ref[...] = jnp.broadcast_to(points[:, 17:18], (128, 256))
    pt = points.T
    y_t = pt[0:16]
    qp_t = pt[16:17]
    yh, ym, yl = split3(-2.0 * y_t)
    sqh, sqm, sql = split3(pt[18:19])
    row16 = rows_of((16, 128))
    tail = jnp.where(row16 < 3, 1.0, jnp.where(row16 == 3, sqh, jnp.where(row16 == 4, sqm, jnp.where(row16 == 5, sql, 0.0))))
    ycat_ref[...] = jnp.concatenate([yh, yh, ym, ym, yh, yl, tail, jnp.zeros((16, 128), f32)], 0).T.astype(bf16)
    yq = jnp.concatenate([y_t * qp_t, jnp.where(row16 == 0, qp_t, 0.0)], 0)
    yqh, yqm, yql = split3(yq)
    yqt = jnp.concatenate([yqh, yqm, yql], 0).astype(bf16)
    yqt_ref[...] = jnp.concatenate([yqt, yqt], 1)

    def hb_copy(i):
        return copy(hits_out.at[i], hits_back.at[i], s_hb.at[i], r_hb.at[i], plane_back(i))

    def pairs(i):
        @pl.when(i > 0)
        def _():
            hit_copy(i).wait()

        blk = hits_ref[i]
        xs = blk[0:16]
        q = blk[16:17]
        key_i = blk[17:18]
        xh, xm, xl = split3(xs)
        sh, sm, sl = split3(blk[18:19])
        r16 = rows_of((16, 256))
        tail_x = jnp.where(r16 == 0, sh, jnp.where(r16 == 1, sm, jnp.where(r16 == 2, sl, jnp.where(r16 < 6, 1.0, 0.0))))
        xcat = jnp.concatenate([xh, xm, xh, xm, xl, xh, tail_x, jnp.zeros((16, 256), f32)], 0).astype(bf16)
        d2 = jnp.maximum(jnp.dot(ycat_ref[...], xcat, preferred_element_type=f32), 0.0)
        t = d2 + dist_eps
        inv = lax.rsqrt(t)
        reach = jnp.maximum(1.0 - t * inv, 0.0)
        match = id_ref[...] == key_i
        pot = jnp.where(match, d2, reach * reach)
        cc = jnp.where(match, 1.0, -(reach * inv))
        pot_rows = jnp.sum(pot * qp_ref[...], 0, keepdims=True)
        pot_ref[...] += pot * q
        cc_hi = cc.astype(bf16)
        cc_lo = (cc - cc_hi.astype(f32)).astype(bf16)
        ht = jnp.dot(yqt_ref[...], jnp.concatenate([cc_hi, cc_lo], 0), preferred_element_type=f32)
        ht = (ht[0:32] + ht[32:64]) + ht[64:96]
        hits_out[i] = jnp.concatenate([ht[0:16], jnp.where(row8 == 1, pot_rows, ht[16:24])], 0)
        xq = jnp.concatenate([xs * q, jnp.where(r16 == 0, q, 0.0)], 0)
        xqh, xqm, xql = split3(xq)
        xq_all = jnp.concatenate([xqh, xqm, xql, jnp.zeros((32, 256), f32)], 0).astype(bf16)
        ptacc_ref[...] += nt_dot(cc_hi, xq_all) + nt_dot(cc_lo, xq_all)

        @pl.when(i > 0)
        def _():
            hb_copy(i).start()

    each(0, 16, pairs)

    acc = ptacc_ref[...]
    acc = (acc + pltpu.roll(acc, 96, 1)) + pltpu.roll(acc, 64, 1)
    pot_cols = jnp.sum(pot_ref[...], 1, keepdims=True)
    pts_out[...] = jnp.where(lanes_of((128, 128)) == 17, pot_cols, acc).reshape(16, 8, 128)

    def pb_copy(i):
        return copy(pts_out.at[i], pts_back.at[i], s_pb.at[i], r_pb.at[i], column_back(i))

    each(1, 16, lambda i: pb_copy(i).start())
    each(1, 16, lambda i: hb_copy(i).wait())
    hsum = hits_out[0]
    for i in range(1, 16):
        hsum = hsum + hits_back[i]
    pot_i = hsum[17:18]
    coord_grad = (2.0 * charge / HITS) * (coords * hsum[16:17] - hsum[0:16])
    each(1, 16, lambda i: pb_copy(i).wait())
    psum = pts_out[0]
    for i in range(1, 16):
        psum = psum + pts_back[i]
    lane = lanes_of((8, 128))
    grads = jnp.where(
        lane < 16,
        (2.0 * own_pts[:, 16:17] / HITS) * (own_pts * psum[:, 16:17] - psum),
        jnp.where(lane == 16, psum[:, 17:18] / HITS, 0.0),
    )
    gh, gm, gl = split3(grads)
    zeros8 = jnp.zeros((8, 128), f32)
    g3 = jnp.concatenate([gh, gm, gl, zeros8], 0).astype(bf16)
    sel3 = jnp.concatenate([sel, sel, sel, jnp.zeros((8, 256), f32)], 0).astype(bf16)
    spread_back = tn_dot(g3, sel3)
    count = jnp.sum(sel, 0, keepdims=True)
    coord_grad = coord_grad + spread_back[0:16]
    charge_grad = pot_i / HITS + spread_back[16:17]
    beta_grad = noise_f / HITS - count * (1.0 / POINTS)
    logit_grad = charge_grad * slope + beta_grad * beta * (1.0 - beta)
    loss_row = charge * pot_i / HITS + (count - count * beta) / POINTS + noise_f * beta / HITS
    loss_local = jnp.sum(loss_row, 1, keepdims=True)

    low = jnp.concatenate([coord_grad, jnp.where(rows_of((16, 256)) == 0, logit_grad, 0.0)], 0).astype(bf16)
    head = jnp.dot(low, act_ref[3], preferred_element_type=f32)
    up = tn_dot(low, wcb)

    def core_copy(j):
        first, count = (2 * j, 2) if j < 4 else (8, 1)
        return copy(
            part_ref.at[other, :, pl.ds(first, count)], core_in.at[:, pl.ds(first, count)],
            s_core.at[j], r_core.at[j], partner,
        )

    def core_sum(j):
        core_copy(j).wait()
        first, count = (2 * j, 2) if j < 4 else (8, 1)
        part_ref[core, :, first : first + count] += core_in[:, first : first + count]

    def xy_copy(c, i):
        first, last = chunks[c]
        span = pl.ds(first, last - first)
        target = ((x + i // 4) % 4) * 4 + (y + i % 4) % 4
        return copy(
            part_ref.at[core, target, span], xy_in.at[i, span], s_xy.at[c, i], r_xy.at[c, i], plane(i)
        )

    def z_copy(c, i):
        first, last = chunks[c]
        span = pl.ds(first, last - first)
        return copy(zsum_ref.at[z, span], zsum_ref.at[z, span], s_z.at[c, i], r_z.at[c, i], ring(i))

    def g_copy(c, i):
        first, last = chunks[c]
        span = pl.ds(first, last - first)
        block = full_ref.at[core, here, span]
        return copy(block, block, s_g.at[c, i], r_g.at[c, i], plane(i))

    def f_copy(c, i):
        first, last = chunks[c]
        span = pl.ds(first, last - first)
        block = full_ref.at[core, ((x + 4 - i // 4) % 4) * 4 + (y + 4 - i % 4) % 4, span]
        return copy(block, block, s_f.at[c, i], r_f.at[c, i], partner)

    def after_core(j):
        core_sum(j)
        done = 2 * j + 2 if j < 4 else 9
        for c, (first, last) in enumerate(chunks):
            if last == done:
                each(1, 16, lambda i: xy_copy(c, i).start())

    biases = [None] * 4
    for layer in range(3, -1, -1):
        local = (up * pre_ref[layer]).astype(bf16)
        wg = jnp.dot(actt_ref[layer], local, preferred_element_type=f32)
        for half in range(2):
            part_ref[:, :, 2 * (3 - layer) + half] = wg[:, half * 128 : half * 128 + 128].reshape(2, 16, 8, 128)
        core_copy(3 - layer).start()
        biases[layer] = jnp.sum(local.astype(f32), 0, keepdims=True)
        if layer > 0:
            up = nt_dot(local, w_ref[layer])
        if layer < 3:
            after_core(2 - layer)
    ext8 = jnp.where(
        row8 == 0,
        head[16:17],
        jnp.where(
            row8 == 1,
            biases[0],
            jnp.where(
                row8 == 2,
                biases[1],
                jnp.where(row8 == 3, biases[2], jnp.where(row8 == 4, biases[3], jnp.where(row8 == 5, loss_local, 0.0))),
            ),
        ),
    )
    ext = jnp.concatenate([head[0:16], ext8], 0)
    for half in range(2):
        cols = ext[:, half * 128 : half * 128 + 128].reshape(3, 8, 128)
        part_ref[half, :, 8] = jnp.concatenate([cols, jnp.zeros((13, 8, 128), f32)], 0)
    core_copy(4).start()
    after_core(3)
    after_core(4)

    for c, (first, last) in enumerate(chunks):
        each(1, 16, lambda i: xy_copy(c, i).wait())
        total = part_ref[core, here, first:last]
        for i in range(1, 16):
            total = total + xy_in[i, first:last]
        zsum_ref[z, first:last] = total
        each(1, 8, lambda i: z_copy(c, i).start())
    for c, (first, last) in enumerate(chunks):
        each(1, 8, lambda i: z_copy(c, i).wait())
        total = zsum_ref[0, first:last]
        for i in range(1, 8):
            total = total + zsum_ref[i, first:last]
        full_ref[core, here, first:last] = total
        each(1, 16, lambda i: g_copy(c, i).start())
        f_copy(c, 0).start()
    for c in range(len(chunks)):

        def forward_on(i):
            g_copy(c, i).wait_recv()
            f_copy(c, i).start()

        each(1, 16, forward_on)
    for c in range(len(chunks)):
        each(1, 16, lambda i: g_copy(c, i).wait_send())
        each(0, 16, lambda i: f_copy(c, i).wait())
    for layer in range(4):
        for half in range(2):
            gw_ref[layer, :, half * 128 : half * 128 + 128] = full_ref[:, :, 2 * (3 - layer) + half].reshape(256, 128)
    gc_ref[...] = jnp.concatenate(
        [full_ref[half, 0:2, 8].reshape(16, 128) for half in range(2)], 1
    )
    last = jnp.concatenate([full_ref[half, 2, 8] for half in range(2)], 1)
    gbeta_ref[...] = last[0:1]
    gb_ref[...] = last[1:5]
    loss_ref[...] = last[5:6, 0:1]


def deliver(*refs):
    sems = refs[10]
    copies = [pltpu.make_async_copy(refs[i], refs[5 + i], sems.at[i]) for i in range(5)]
    for copy in copies:
        copy.start()
    for copy in copies:
        copy.wait()


def on_device(features, w_layers, b_layers, w_coord, w_beta, point_hit, track, noise):
    vmem = pl.BlockSpec(memory_space=pltpu.VMEM)
    hbm = pl.BlockSpec(memory_space=pltpu.HBM)
    dma = pltpu.SemaphoreType.DMA
    results = (
        jax.ShapeDtypeStruct((4, 256, 256), f32),
        jax.ShapeDtypeStruct((4, 256), f32),
        jax.ShapeDtypeStruct((16, 256), f32),
        jax.ShapeDtypeStruct((1, 256), f32),
        jax.ShapeDtypeStruct((1, 1), f32),
    )
    grads = pl.pallas_call(
        kernel,
        name="condense",
        out_shape=results,
        in_specs=[hbm] * 8,
        out_specs=(vmem,) * 5,
        scratch_shapes=[
            pltpu.VMEM((256, 256), bf16),
            pltpu.VMEM((4, 256, 256), bf16),
            pltpu.VMEM((4, 256), f32),
            pltpu.VMEM((16, 256), bf16),
            pltpu.VMEM((256,), bf16),
            pltpu.SMEM((8,), jnp.int32),
            pltpu.VMEM((256,), jnp.int32),
            pltpu.VMEM((256,), jnp.int32),
            dma((11,)),
            pltpu.VMEM((4, 256, 256), f32),
            pltpu.VMEM((4, 256, 256), bf16),
            pltpu.VMEM((4, 256, 256), bf16),
            pltpu.VMEM((16, 24, 256), f32),
            pltpu.VMEM((16, 24, 256), f32),
            pltpu.VMEM((16, 24, 256), f32),
            pltpu.VMEM((16, 8, 128), f32),
            pltpu.VMEM((16, 8, 128), f32),
            pltpu.VMEM((16, 8, 128), f32),
            pltpu.VMEM((128, 128), bf16),
            pltpu.VMEM((96, 256), bf16),
            pltpu.VMEM((128, 256), f32),
            pltpu.VMEM((128, 256), f32),
            pltpu.VMEM((128, 256), f32),
            pltpu.VMEM((128, 128), f32),
            pltpu.VMEM((2, 16, 9, 8, 128), f32),
            pltpu.VMEM((16, 9, 8, 128), f32),
            pltpu.VMEM((16, 9, 8, 128), f32),
            pltpu.VMEM((8, 9, 8, 128), f32),
            pltpu.VMEM((2, 16, 9, 8, 128), f32),
            dma((16,)), dma((16,)), dma((16,)), dma((16,)),
            dma((16,)), dma((16,)), dma((16,)), dma((16,)),
            dma((5,)), dma((5,)), dma((len(chunks), 16)), dma((len(chunks), 16)),
            dma((len(chunks), 8)), dma((len(chunks), 8)), dma((len(chunks), 16)), dma((len(chunks), 16)),
            dma((len(chunks), 16)), dma((len(chunks), 16)),
        ],
        compiler_params=pltpu.CompilerParams(
            collective_id=0, has_side_effects=True, vmem_limit_bytes=48 << 20
        ),
    )(*[pltpu.with_memory_space_constraint(v, pltpu.HBM) for v in (features, w_layers, b_layers, w_coord, w_beta, point_hit, track, noise)])
    grad_w, grad_b, grad_c, grad_beta, loss = pl.pallas_call(
        deliver,
        name="deliver",
        out_shape=results,
        in_specs=[vmem] * 5,
        out_specs=(hbm,) * 5,
        scratch_shapes=[dma((5,))],
        compiler_params=pltpu.CompilerParams(vmem_limit_bytes=8 << 20),
    )(*grads)
    return grad_w, grad_b, grad_c, grad_beta.reshape(256), loss.reshape(())


def solution(mesh):
    return jax.shard_map(
        on_device,
        mesh=mesh,
        in_specs=(
            P(("layer", "phi"), None),
            P(),
            P(),
            P(),
            P(),
            P(("layer", "phi")),
            P(("layer", "phi")),
            P(("layer", "phi")),
        ),
        out_specs=(P(), P(), P(), P(), P()),
        check_vma=False,
    )
```

```python
import jax
import jax.numpy as jnp
from jax import lax
from jax.sharding import PartitionSpec as P
from jax.experimental import pallas as pl
from jax.experimental.pallas import tpu as pltpu

f32 = jnp.float32
bf16 = jnp.bfloat16
dist_eps = 0.0001
charge_floor = 0.5
MESH = pl.DeviceIdType.MESH
HITS = 65536.0
POINTS = 2048.0
chunks = ((0, 4), (4, 9))


def split3(v):
    hi = v.astype(bf16).astype(f32)
    rest = v - hi
    mid = rest.astype(bf16).astype(f32)
    low = (rest - mid).astype(bf16).astype(f32)
    return hi, mid, low


def rows_of(shape):
    return lax.broadcasted_iota(jnp.int32, shape, 0)


def lanes_of(shape):
    return lax.broadcasted_iota(jnp.int32, shape, 1)


def nt_dot(a, b):
    return lax.dot_general(a, b, (((1,), (1,)), ((), ())), preferred_element_type=f32)


def tn_dot(a, b):
    return lax.dot_general(a, b, (((0,), (0,)), ((), ())), preferred_element_type=f32)


def kernel(
    feat_hbm, w_hbm, b_hbm, wc_hbm, wb_hbm, hit_hbm, track_hbm, noise_hbm,
    gw_ref, gb_ref, gc_ref, gbeta_ref, loss_ref,
    feat_ref, w_ref, b_ref, wc_ref, wb_ref, hit_ref, track_ref, noise_ref, s_in,
    pre_ref, act_ref, actt_ref,
    hits_ref, hits_back, hits_out, pts_ref, pts_back, pts_out,
    ycat_ref, yqt_ref, qp_ref, id_ref, pot_ref, ptacc_ref,
    part_ref, core_in, xy_in, zsum_ref, full_ref,
    s_hit, r_hit, s_pt, r_pt, s_hb, r_hb, s_pb, r_pb,
    s_core, r_core, s_xy, r_xy, s_z, r_z, s_g, r_g, s_f, r_f,
):
    loads = [
        pltpu.make_async_copy(src, dst, s_in.at[i])
        for i, (src, dst) in enumerate(
            [
                (feat_hbm, feat_ref),
                (w_hbm.at[0], w_ref.at[0]),
                (b_hbm, b_ref),
                (w_hbm.at[1], w_ref.at[1]),
                (w_hbm.at[2], w_ref.at[2]),
                (w_hbm.at[3], w_ref.at[3]),
                (wc_hbm, wc_ref),
                (wb_hbm, wb_ref),
                (track_hbm, track_ref),
                (noise_hbm, noise_ref),
                (hit_hbm, hit_ref),
            ]
        )
    ]
    for load in loads:
        load.start()
    lay = lax.axis_index("layer")
    phi = lax.axis_index("phi")
    z = (lay // 8) * 4 + phi % 4
    y = (lay // 2) % 4
    core = lay % 2
    x = phi // 4
    other = 1 - core
    here = x * 4 + y

    def device(px, py, pz, pc):
        return ((pz // 4) * 8 + py * 2 + pc, px * 4 + pz % 4)

    def plane(step):
        return device((x + step // 4) % 4, (y + step % 4) % 4, z, core)

    def plane_back(step):
        return device((x + 4 - step // 4) % 4, (y + 4 - step % 4) % 4, z, core)

    def column(step):
        return device(x, y, (z + step // 2) % 8, (core + step % 2) % 2)

    def column_back(step):
        return device(x, y, (z + 8 - step // 2) % 8, (core + 2 - step % 2) % 2)

    def ring(step):
        return device(x, y, (z + step) % 8, core)

    partner = device(x, y, z, other)

    def copy(src, dst, ssem, rsem, target):
        return pltpu.make_async_remote_copy(
            src_ref=src, dst_ref=dst, send_sem=ssem, recv_sem=rsem,
            device_id=target, device_id_type=MESH,
        )

    def each(first, last, body):
        def step(i, carry):
            body(i)
            return carry
        lax.fori_loop(first, last, step, 0)

    barrier = pltpu.get_barrier_semaphore()

    def greet(i):
        pl.semaphore_signal(barrier, inc=1, device_id=plane(i), device_id_type=MESH)
        pl.semaphore_signal(barrier, inc=1, device_id=column(i), device_id_type=MESH)
    each(1, 16, greet)

    for load in loads[0:3]:
        load.wait()
    hidden = feat_ref[...]
    for layer in range(4):
        if layer > 0:
            loads[2 + layer].wait()
        pre = jnp.dot(hidden, w_ref[layer], preferred_element_type=f32) + b_ref[layer : layer + 1, :]
        pre_ref[layer] = pre
        hidden = (pre * jax.nn.sigmoid(pre)).astype(bf16)
        act_ref[layer] = hidden
    for load in loads[6:11]:
        load.wait()
    wcb = jnp.concatenate(
        [
            wc_ref[...].astype(f32),
            jnp.where(rows_of((16, 256)) == 0, wb_ref[...].astype(f32).reshape(1, 256), 0.0),
        ],
        0,
    ).astype(bf16)
    xz = nt_dot(wcb, hidden)
    coords = xz[0:16]
    logits = xz[16:17]
    expz = jnp.exp(logits)
    spread = jnp.log1p(2.0 * expz)
    charge = 0.25 * spread * spread + charge_floor
    slope = 0.5 * spread * (2.0 * expz / (1.0 + 2.0 * expz))
    beta = jax.nn.sigmoid(logits)
    noise = noise_ref[...].reshape(1, 256)
    track = track_ref[...].reshape(1, 256)
    key = jnp.where(noise == 0, track, -1).astype(f32)
    noise_f = noise.astype(f32)
    square = jnp.sum(coords * coords, 0, keepdims=True)
    row8 = rows_of((8, 256))
    lane8 = lanes_of((8, 256))
    pack = jnp.where(row8 == 0, charge, jnp.where(row8 == 1, key, jnp.where(row8 == 2, square, 0.0)))
    mine = jnp.concatenate([coords, pack], 0)
    r8s = rows_of((8, 128))
    tail_h = jnp.where(r8s == 0, charge[:, 0:128], jnp.where(r8s == 1, charge[:, 128:256], jnp.where(r8s == 2, key[:, 0:128], jnp.where(r8s == 3, key[:, 128:256], 0.0))))
    hits_ref[0] = jnp.concatenate([coords[:, 0:128], coords[:, 128:256], tail_h], 0)
    sel = jnp.zeros((8, 256), f32)
    for k in range(8):
        sel = jnp.where((row8 == k) & (lane8 == hit_ref[k]), 1.0, sel)
    sel_low = sel.astype(bf16)
    mine128 = jnp.concatenate([mine, jnp.zeros((104, 256), f32)], 0)
    mh, mm, ml = split3(mine128)
    own_pts = (nt_dot(sel_low, mh.astype(bf16)) + nt_dot(sel_low, mm.astype(bf16))) + nt_dot(sel_low, ml.astype(bf16))
    linear = lay * 16 + phi
    ident = (linear * 8 + rows_of((8, 128))).astype(f32)
    own_pts = jnp.where(lanes_of((8, 128)) == 17, ident, own_pts)
    pts_ref[0] = own_pts

    pl.semaphore_wait(barrier, 30)

    def pt_copy(i):
        return copy(pts_ref.at[0], pts_ref.at[i], s_pt.at[i], r_pt.at[i], column(i))

    def hit_copy(i):
        return copy(hits_ref.at[0], hits_ref.at[i], s_hit.at[i], r_hit.at[i], plane(i))

    each(1, 16, lambda i: pt_copy(i).start())
    each(1, 16, lambda i: hit_copy(i).start())

    actt_ref[0] = feat_ref[...].T
    for layer in range(4):
        pre = pre_ref[layer]
        sig = jax.nn.sigmoid(pre)
        pre_ref[layer] = sig * (1.0 + pre * (1.0 - sig))
        if layer < 3:
            actt_ref[layer + 1] = act_ref[layer].T
    ptacc_ref[...] = jnp.zeros((128, 128), f32)
    pot_ref[...] = jnp.zeros((128, 256), f32)

    each(1, 16, lambda i: pt_copy(i).wait())
    points = pts_ref[...].reshape(128, 128)
    qp_ref[...] = jnp.broadcast_to(points[:, 16:17], (128, 256))
    id_ref[...] = jnp.broadcast_to(points[:, 17:18], (128, 256))
    pt = points.T
    y_t = pt[0:16]
    qp_t = pt[16:17]
    yh, ym, yl = split3(-2.0 * y_t)
    sqh, sqm, sql = split3(pt[18:19])
    row16 = rows_of((16, 128))
    tail = jnp.where(row16 < 3, 1.0, jnp.where(row16 == 3, sqh, jnp.where(row16 == 4, sqm, jnp.where(row16 == 5, sql, 0.0))))
    ycat_ref[...] = jnp.concatenate([yh, yh, ym, ym, yh, yl, tail, jnp.zeros((16, 128), f32)], 0).T.astype(bf16)
    yq = jnp.concatenate([y_t * qp_t, jnp.where(row16 == 0, qp_t, 0.0)], 0)
    yqh, yqm, yql = split3(yq)
    yqt = jnp.concatenate([yqh, yqm, yql], 0).astype(bf16)
    yqt_ref[...] = jnp.concatenate([yqt, yqt], 1)

    def hb_copy(i):
        return copy(hits_out.at[i], hits_back.at[i], s_hb.at[i], r_hb.at[i], plane_back(i))

    wide = 4
    span = wide * 256
    r16 = rows_of((16, span))

    def over_hits(v):
        return v if wide == 1 else jnp.concatenate([v] * wide, 1)

    def pairs(j):
        first = j * wide
        for k in range(wide):
            if k > 0:
                hit_copy(first + k).wait()
            else:

                @pl.when(j > 0)
                def _():
                    hit_copy(first).wait()

        blks = [hits_ref[first + k] for k in range(wide)]
        xs = jnp.concatenate([v for b in blks for v in (b[0:16], b[16:32])], 1)
        q = jnp.concatenate([v for b in blks for v in (b[32:33], b[33:34])], 1)
        key_i = jnp.concatenate([v for b in blks for v in (b[34:35], b[35:36])], 1)
        xh, xm, xl = split3(xs)
        sh, sm, sl = split3(jnp.sum(xs * xs, 0, keepdims=True))
        tail_x = jnp.where(r16 == 0, sh, jnp.where(r16 == 1, sm, jnp.where(r16 == 2, sl, jnp.where(r16 < 6, 1.0, 0.0))))
        xcat = jnp.concatenate([xh, xm, xh, xm, xl, xh, tail_x, jnp.zeros((16, span), f32)], 0).astype(bf16)
        d2 = jnp.maximum(jnp.dot(ycat_ref[...], xcat, preferred_element_type=f32), 0.0)
        t = d2 + dist_eps
        inv = lax.rsqrt(t)
        reach = jnp.maximum(1.0 - t * inv, 0.0)
        match = over_hits(id_ref[...]) == key_i
        pot = jnp.where(match, d2, reach * reach)
        cc = jnp.where(match, 1.0, -(reach * inv))
        pot_rows = jnp.sum(pot * over_hits(qp_ref[...]), 0, keepdims=True)
        weighted = pot * q
        pot_sum = weighted[:, 0:256]
        for k in range(1, wide):
            pot_sum = pot_sum + weighted[:, 256 * k : 256 * k + 256]
        pot_ref[...] += pot_sum
        cc_hi = cc.astype(bf16)
        cc_lo = (cc - cc_hi.astype(f32)).astype(bf16)
        ht = jnp.dot(yqt_ref[...], jnp.concatenate([cc_hi, cc_lo], 0), preferred_element_type=f32)
        ht = (ht[0:32] + ht[32:64]) + ht[64:96]
        for k in range(wide):
            lo = slice(256 * k, 256 * k + 128)
            hi = slice(256 * k + 128, 256 * k + 256)
            ends = jnp.where(
                r8s == 0, ht[16:17, lo], jnp.where(r8s == 1, ht[16:17, hi], jnp.where(r8s == 2, pot_rows[:, lo], pot_rows[:, hi]))
            )
            hits_out[first + k] = jnp.concatenate([ht[0:16, lo], ht[0:16, hi], ends], 0)
        xq = jnp.concatenate([xs * q, jnp.where(r16 == 0, q, 0.0)], 0)
        xqh, xqm, xql = split3(xq)
        xq_all = jnp.concatenate([xqh, xqm, xql, jnp.zeros((32, span), f32)], 0).astype(bf16)
        ptacc_ref[...] += nt_dot(cc_hi, xq_all) + nt_dot(cc_lo, xq_all)
        for k in range(wide):
            if k > 0:
                hb_copy(first + k).start()
            else:

                @pl.when(j > 0)
                def _():
                    hb_copy(first).start()

    each(0, 16 // wide, pairs)

    acc = ptacc_ref[...]
    acc = (acc + pltpu.roll(acc, 96, 1)) + pltpu.roll(acc, 64, 1)
    pot_cols = jnp.sum(pot_ref[...], 1, keepdims=True)
    pts_out[...] = jnp.where(lanes_of((128, 128)) == 17, pot_cols, acc).reshape(16, 8, 128)

    def pb_copy(i):
        return copy(pts_out.at[i], pts_back.at[i], s_pb.at[i], r_pb.at[i], column_back(i))

    each(1, 16, lambda i: pb_copy(i).start())
    each(1, 16, lambda i: hb_copy(i).wait())
    hsum = hits_out[0]
    for i in range(1, 16):
        hsum = hsum + hits_back[i]
    pull = jnp.concatenate([hsum[0:16], hsum[16:32]], 1)
    coef_i = jnp.concatenate([hsum[32:33], hsum[33:34]], 1)
    pot_i = jnp.concatenate([hsum[34:35], hsum[35:36]], 1)
    coord_grad = (2.0 * charge / HITS) * (coords * coef_i - pull)
    each(1, 16, lambda i: pb_copy(i).wait())
    psum = pts_out[0]
    for i in range(1, 16):
        psum = psum + pts_back[i]
    lane = lanes_of((8, 128))
    grads = jnp.where(
        lane < 16,
        (2.0 * own_pts[:, 16:17] / HITS) * (own_pts * psum[:, 16:17] - psum),
        jnp.where(lane == 16, psum[:, 17:18] / HITS, 0.0),
    )
    gh, gm, gl = split3(grads)
    zeros8 = jnp.zeros((8, 128), f32)
    g3 = jnp.concatenate([gh, gm, gl, zeros8], 0).astype(bf16)
    sel3 = jnp.concatenate([sel, sel, sel, jnp.zeros((8, 256), f32)], 0).astype(bf16)
    spread_back = tn_dot(g3, sel3)
    count = jnp.sum(sel, 0, keepdims=True)
    coord_grad = coord_grad + spread_back[0:16]
    charge_grad = pot_i / HITS + spread_back[16:17]
    beta_grad = noise_f / HITS - count * (1.0 / POINTS)
    logit_grad = charge_grad * slope + beta_grad * beta * (1.0 - beta)
    loss_row = charge * pot_i / HITS + (count - count * beta) / POINTS + noise_f * beta / HITS
    loss_local = jnp.sum(loss_row, 1, keepdims=True)

    low = jnp.concatenate([coord_grad, jnp.where(rows_of((16, 256)) == 0, logit_grad, 0.0)], 0).astype(bf16)
    head = jnp.dot(low, act_ref[3], preferred_element_type=f32)
    up = tn_dot(low, wcb)

    def core_copy(j):
        first, count = (2 * j, 2) if j < 4 else (8, 1)
        return copy(
            part_ref.at[other, :, pl.ds(first, count)], core_in.at[:, pl.ds(first, count)],
            s_core.at[j], r_core.at[j], partner,
        )

    def core_sum(j):
        core_copy(j).wait()
        first, count = (2 * j, 2) if j < 4 else (8, 1)
        part_ref[core, :, first : first + count] += core_in[:, first : first + count]

    def xy_copy(c, i):
        first, last = chunks[c]
        span = pl.ds(first, last - first)
        target = ((x + i // 4) % 4) * 4 + (y + i % 4) % 4
        return copy(
            part_ref.at[core, target, span], xy_in.at[i, span], s_xy.at[c, i], r_xy.at[c, i], plane(i)
        )

    def z_copy(c, i):
        first, last = chunks[c]
        span = pl.ds(first, last - first)
        return copy(zsum_ref.at[z, span], zsum_ref.at[z, span], s_z.at[c, i], r_z.at[c, i], ring(i))

    def g_copy(c, i):
        first, last = chunks[c]
        span = pl.ds(first, last - first)
        block = full_ref.at[core, here, span]
        return copy(block, block, s_g.at[c, i], r_g.at[c, i], plane(i))

    def f_copy(c, i):
        first, last = chunks[c]
        span = pl.ds(first, last - first)
        block = full_ref.at[core, ((x + 4 - i // 4) % 4) * 4 + (y + 4 - i % 4) % 4, span]
        return copy(block, block, s_f.at[c, i], r_f.at[c, i], partner)

    def after_core(j):
        core_sum(j)
        done = 2 * j + 2 if j < 4 else 9
        for c, (first, last) in enumerate(chunks):
            if last == done:
                each(1, 16, lambda i: xy_copy(c, i).start())

    biases = [None] * 4
    for layer in range(3, -1, -1):
        local = (up * pre_ref[layer]).astype(bf16)
        wg = jnp.dot(actt_ref[layer], local, preferred_element_type=f32)
        for half in range(2):
            part_ref[:, :, 2 * (3 - layer) + half] = wg[:, half * 128 : half * 128 + 128].reshape(2, 16, 8, 128)
        core_copy(3 - layer).start()
        biases[layer] = jnp.sum(local.astype(f32), 0, keepdims=True)
        if layer > 0:
            up = nt_dot(local, w_ref[layer])
        if layer < 3:
            after_core(2 - layer)
    ext8 = jnp.where(
        row8 == 0,
        head[16:17],
        jnp.where(
            row8 == 1,
            biases[0],
            jnp.where(
                row8 == 2,
                biases[1],
                jnp.where(row8 == 3, biases[2], jnp.where(row8 == 4, biases[3], jnp.where(row8 == 5, loss_local, 0.0))),
            ),
        ),
    )
    ext = jnp.concatenate([head[0:16], ext8], 0)
    for half in range(2):
        cols = ext[:, half * 128 : half * 128 + 128].reshape(3, 8, 128)
        part_ref[half, :, 8] = jnp.concatenate([cols, jnp.zeros((13, 8, 128), f32)], 0)
    core_copy(4).start()
    after_core(3)
    after_core(4)

    for c, (first, last) in enumerate(chunks):
        each(1, 16, lambda i: xy_copy(c, i).wait())
        total = part_ref[core, here, first:last]
        for i in range(1, 16):
            total = total + xy_in[i, first:last]
        zsum_ref[z, first:last] = total
        each(1, 8, lambda i: z_copy(c, i).start())
    for c, (first, last) in enumerate(chunks):
        each(1, 8, lambda i: z_copy(c, i).wait())
        total = zsum_ref[0, first:last]
        for i in range(1, 8):
            total = total + zsum_ref[i, first:last]
        full_ref[core, here, first:last] = total
        each(1, 16, lambda i: g_copy(c, i).start())
        f_copy(c, 0).start()
    for c in range(len(chunks)):

        def forward_on(i):
            g_copy(c, i).wait_recv()
            f_copy(c, i).start()

        each(1, 16, forward_on)
    for c in range(len(chunks)):
        each(1, 16, lambda i: g_copy(c, i).wait_send())
        each(0, 16, lambda i: f_copy(c, i).wait())
    for layer in range(4):
        for half in range(2):
            gw_ref[layer, :, half * 128 : half * 128 + 128] = full_ref[:, :, 2 * (3 - layer) + half].reshape(256, 128)
    gc_ref[...] = jnp.concatenate(
        [full_ref[half, 0:2, 8].reshape(16, 128) for half in range(2)], 1
    )
    last = jnp.concatenate([full_ref[half, 2, 8] for half in range(2)], 1)
    gbeta_ref[...] = last[0:1]
    gb_ref[...] = last[1:5]
    loss_ref[...] = last[5:6, 0:1]


def deliver(*refs):
    sems = refs[10]
    copies = [pltpu.make_async_copy(refs[i], refs[5 + i], sems.at[i]) for i in range(5)]
    for copy in copies:
        copy.start()
    for copy in copies:
        copy.wait()


def on_device(features, w_layers, b_layers, w_coord, w_beta, point_hit, track, noise):
    vmem = pl.BlockSpec(memory_space=pltpu.VMEM)
    hbm = pl.BlockSpec(memory_space=pltpu.HBM)
    dma = pltpu.SemaphoreType.DMA
    results = (
        jax.ShapeDtypeStruct((4, 256, 256), f32),
        jax.ShapeDtypeStruct((4, 256), f32),
        jax.ShapeDtypeStruct((16, 256), f32),
        jax.ShapeDtypeStruct((1, 256), f32),
        jax.ShapeDtypeStruct((1, 1), f32),
    )
    grads = pl.pallas_call(
        kernel,
        name="condense",
        out_shape=results,
        in_specs=[hbm] * 8,
        out_specs=(vmem,) * 5,
        scratch_shapes=[
            pltpu.VMEM((256, 256), bf16),
            pltpu.VMEM((4, 256, 256), bf16),
            pltpu.VMEM((4, 256), f32),
            pltpu.VMEM((16, 256), bf16),
            pltpu.VMEM((256,), bf16),
            pltpu.SMEM((8,), jnp.int32),
            pltpu.VMEM((256,), jnp.int32),
            pltpu.VMEM((256,), jnp.int32),
            dma((11,)),
            pltpu.VMEM((4, 256, 256), f32),
            pltpu.VMEM((4, 256, 256), bf16),
            pltpu.VMEM((4, 256, 256), bf16),
            pltpu.VMEM((16, 40, 128), f32),
            pltpu.VMEM((16, 40, 128), f32),
            pltpu.VMEM((16, 40, 128), f32),
            pltpu.VMEM((16, 8, 128), f32),
            pltpu.VMEM((16, 8, 128), f32),
            pltpu.VMEM((16, 8, 128), f32),
            pltpu.VMEM((128, 128), bf16),
            pltpu.VMEM((96, 256), bf16),
            pltpu.VMEM((128, 256), f32),
            pltpu.VMEM((128, 256), f32),
            pltpu.VMEM((128, 256), f32),
            pltpu.VMEM((128, 128), f32),
            pltpu.VMEM((2, 16, 9, 8, 128), f32),
            pltpu.VMEM((16, 9, 8, 128), f32),
            pltpu.VMEM((16, 9, 8, 128), f32),
            pltpu.VMEM((8, 9, 8, 128), f32),
            pltpu.VMEM((2, 16, 9, 8, 128), f32),
            dma((16,)), dma((16,)), dma((16,)), dma((16,)),
            dma((16,)), dma((16,)), dma((16,)), dma((16,)),
            dma((5,)), dma((5,)), dma((len(chunks), 16)), dma((len(chunks), 16)),
            dma((len(chunks), 8)), dma((len(chunks), 8)), dma((len(chunks), 16)), dma((len(chunks), 16)),
            dma((len(chunks), 16)), dma((len(chunks), 16)),
        ],
        compiler_params=pltpu.CompilerParams(
            collective_id=0, has_side_effects=True, vmem_limit_bytes=48 << 20
        ),
    )(*[pltpu.with_memory_space_constraint(v, pltpu.HBM) for v in (features, w_layers, b_layers, w_coord, w_beta, point_hit, track, noise)])
    grad_w, grad_b, grad_c, grad_beta, loss = pl.pallas_call(
        deliver,
        name="deliver",
        out_shape=results,
        in_specs=[vmem] * 5,
        out_specs=(hbm,) * 5,
        scratch_shapes=[dma((5,))],
        compiler_params=pltpu.CompilerParams(vmem_limit_bytes=8 << 20),
    )(*grads)
    return grad_w, grad_b, grad_c, grad_beta.reshape(256), loss.reshape(())


def solution(mesh):
    return jax.shard_map(
        on_device,
        mesh=mesh,
        in_specs=(
            P(("layer", "phi"), None),
            P(),
            P(),
            P(),
            P(),
            P(("layer", "phi")),
            P(("layer", "phi")),
            P(("layer", "phi")),
        ),
        out_specs=(P(), P(), P(), P(), P()),
        check_vma=False,
    )
```

```python
import jax
import jax.numpy as jnp
from jax import lax
from jax.sharding import PartitionSpec as P
from jax.experimental import pallas as pl
from jax.experimental.pallas import tpu as pltpu

f32 = jnp.float32
bf16 = jnp.bfloat16
dist_eps = 0.0001
charge_floor = 0.5
MESH = pl.DeviceIdType.MESH
HITS = 65536.0
POINTS = 2048.0
chunks = ((0, 4), (4, 6))
zchunks = ((0, 4), (4, 5))


def split3(v):
    hi = v.astype(bf16).astype(f32)
    rest = v - hi
    mid = rest.astype(bf16).astype(f32)
    low = (rest - mid).astype(bf16).astype(f32)
    return hi, mid, low


def rows_of(shape):
    return lax.broadcasted_iota(jnp.int32, shape, 0)


def lanes_of(shape):
    return lax.broadcasted_iota(jnp.int32, shape, 1)


def nt_dot(a, b):
    return lax.dot_general(a, b, (((1,), (1,)), ((), ())), preferred_element_type=f32)


def tn_dot(a, b):
    return lax.dot_general(a, b, (((0,), (0,)), ((), ())), preferred_element_type=f32)


def kernel(
    feat_hbm, w_hbm, b_hbm, wc_hbm, wb_hbm, hit_hbm, track_hbm, noise_hbm,
    gw_ref, gb_ref, gc_ref, gbeta_ref, loss_ref,
    feat_ref, w_ref, b_ref, wc_ref, wb_ref, hit_ref, track_ref, noise_ref, s_in,
    pre_ref, act_ref, actt_ref,
    hits_ref, hits_back, hits_out, pts_ref, pts_back, pts_out,
    ycat_ref, yqt_ref, qp_ref, id_ref, pot_ref, ptacc_ref,
    part_ref, core_in, xy_in, zsum_ref, full_ref,
    partz_ref, corez_in, z_in, xysum_ref, fullz_ref,
    s_hit, r_hit, s_pt, r_pt, s_hb, r_hb, s_pb, r_pb,
    s_core, r_core, s_xy, r_xy, s_z, r_z, s_g, r_g, s_f, r_f,
    s_bz, r_bz, s_bx, r_bx, s_bg, r_bg, s_bf, r_bf,
):
    loads = [
        pltpu.make_async_copy(src, dst, s_in.at[i])
        for i, (src, dst) in enumerate(
            [
                (feat_hbm, feat_ref),
                (w_hbm.at[0], w_ref.at[0]),
                (b_hbm, b_ref),
                (w_hbm.at[1], w_ref.at[1]),
                (w_hbm.at[2], w_ref.at[2]),
                (w_hbm.at[3], w_ref.at[3]),
                (wc_hbm, wc_ref),
                (wb_hbm, wb_ref),
                (track_hbm, track_ref),
                (noise_hbm, noise_ref),
                (hit_hbm, hit_ref),
            ]
        )
    ]
    for load in loads:
        load.start()
    lay = lax.axis_index("layer")
    phi = lax.axis_index("phi")
    z = (lay // 8) * 4 + phi % 4
    y = (lay // 2) % 4
    core = lay % 2
    x = phi // 4
    other = 1 - core
    here = x * 4 + y

    def device(px, py, pz, pc):
        return ((pz // 4) * 8 + py * 2 + pc, px * 4 + pz % 4)

    def plane(step):
        return device((x + step // 4) % 4, (y + step % 4) % 4, z, core)

    def plane_back(step):
        return device((x + 4 - step // 4) % 4, (y + 4 - step % 4) % 4, z, core)

    def column(step):
        return device(x, y, (z + step // 2) % 8, (core + step % 2) % 2)

    def column_back(step):
        return device(x, y, (z + 8 - step // 2) % 8, (core + 2 - step % 2) % 2)

    def ring(step):
        return device(x, y, (z + step) % 8, core)

    partner = device(x, y, z, other)

    def copy(src, dst, ssem, rsem, target):
        return pltpu.make_async_remote_copy(
            src_ref=src, dst_ref=dst, send_sem=ssem, recv_sem=rsem,
            device_id=target, device_id_type=MESH,
        )

    def settle(ref, *sems):
        for sem in sems:
            pltpu.make_async_copy(ref, ref, sem).wait()

    def each(first, last, body):
        def step(i, carry):
            body(i)
            return carry
        lax.fori_loop(first, last, step, 0)

    barrier = pltpu.get_barrier_semaphore()

    def greet(i):
        pl.semaphore_signal(barrier, inc=1, device_id=plane(i), device_id_type=MESH)
        pl.semaphore_signal(barrier, inc=1, device_id=column(i), device_id_type=MESH)
    each(1, 16, greet)

    for load in loads[0:3]:
        load.wait()
    hidden = feat_ref[...]
    for layer in range(4):
        if layer > 0:
            loads[2 + layer].wait()
        pre = jnp.dot(hidden, w_ref[layer], preferred_element_type=f32) + b_ref[layer : layer + 1, :]
        pre_ref[layer] = pre
        hidden = (pre * jax.nn.sigmoid(pre)).astype(bf16)
        act_ref[layer] = hidden
    for load in loads[6:11]:
        load.wait()
    wcb = jnp.concatenate(
        [
            wc_ref[...].astype(f32),
            jnp.where(rows_of((16, 256)) == 0, wb_ref[...].astype(f32).reshape(1, 256), 0.0),
        ],
        0,
    ).astype(bf16)
    xz = nt_dot(wcb, hidden)
    coords = xz[0:16]
    logits = xz[16:17]
    expz = jnp.exp(logits)
    spread = jnp.log1p(2.0 * expz)
    charge = 0.25 * spread * spread + charge_floor
    slope = 0.5 * spread * (2.0 * expz / (1.0 + 2.0 * expz))
    beta = jax.nn.sigmoid(logits)
    noise = noise_ref[...].reshape(1, 256)
    track = track_ref[...].reshape(1, 256)
    key = jnp.where(noise == 0, track, -1).astype(f32)
    noise_f = noise.astype(f32)
    square = jnp.sum(coords * coords, 0, keepdims=True)
    row8 = rows_of((8, 256))
    lane8 = lanes_of((8, 256))
    pack = jnp.where(row8 == 0, charge, jnp.where(row8 == 1, key, jnp.where(row8 == 2, square, 0.0)))
    mine = jnp.concatenate([coords, pack], 0)
    r8s = rows_of((8, 128))
    tail_h = jnp.where(r8s == 0, charge[:, 0:128], jnp.where(r8s == 1, charge[:, 128:256], jnp.where(r8s == 2, key[:, 0:128], jnp.where(r8s == 3, key[:, 128:256], 0.0))))
    hits_ref[0] = jnp.concatenate([coords[:, 0:128], coords[:, 128:256], tail_h], 0)
    sel = jnp.zeros((8, 256), f32)
    for k in range(8):
        sel = jnp.where((row8 == k) & (lane8 == hit_ref[k]), 1.0, sel)
    sel_low = sel.astype(bf16)
    mine128 = jnp.concatenate([mine, jnp.zeros((104, 256), f32)], 0)
    mh, mm, ml = split3(mine128)
    own_pts = (nt_dot(sel_low, mh.astype(bf16)) + nt_dot(sel_low, mm.astype(bf16))) + nt_dot(sel_low, ml.astype(bf16))
    linear = lay * 16 + phi
    ident = (linear * 8 + rows_of((8, 128))).astype(f32)
    own_pts = jnp.where(lanes_of((8, 128)) == 17, ident, own_pts)
    pts_ref[0] = own_pts

    pl.semaphore_wait(barrier, 30)

    def pt_copy(i):
        return copy(pts_ref.at[0], pts_ref.at[i], s_pt.at[0], r_pt.at[0], column(i))

    def hit_copy(i):
        return copy(hits_ref.at[0], hits_ref.at[i], s_hit.at[0], r_hit.at[i // 4], plane(i))

    each(1, 16, lambda i: pt_copy(i).start())
    each(1, 16, lambda i: hit_copy(i).start())

    actt_ref[0] = feat_ref[...].T
    for layer in range(4):
        pre = pre_ref[layer]
        sig = jax.nn.sigmoid(pre)
        pre_ref[layer] = sig * (1.0 + pre * (1.0 - sig))
        if layer < 3:
            actt_ref[layer + 1] = act_ref[layer].T
    ptacc_ref[...] = jnp.zeros((128, 128), f32)
    pot_ref[...] = jnp.zeros((128, 256), f32)

    settle(pts_ref.at[pl.ds(1, 15)], s_pt.at[0], r_pt.at[0])
    points = pts_ref[...].reshape(128, 128)
    qp_ref[...] = jnp.broadcast_to(points[:, 16:17], (128, 256))
    id_ref[...] = jnp.broadcast_to(points[:, 17:18], (128, 256))
    pt = points.T
    y_t = pt[0:16]
    qp_t = pt[16:17]
    yh, ym, yl = split3(-2.0 * y_t)
    sqh, sqm, sql = split3(pt[18:19])
    row16 = rows_of((16, 128))
    tail = jnp.where(row16 < 3, 1.0, jnp.where(row16 == 3, sqh, jnp.where(row16 == 4, sqm, jnp.where(row16 == 5, sql, 0.0))))
    ycat_ref[...] = jnp.concatenate([yh, yh, ym, ym, yh, yl, tail, jnp.zeros((16, 128), f32)], 0).T.astype(bf16)
    yq = jnp.concatenate([y_t * qp_t, jnp.where(row16 == 0, qp_t, 0.0)], 0)
    yqh, yqm, yql = split3(yq)
    yqt = jnp.concatenate([yqh, yqm, yql], 0).astype(bf16)
    yqt_ref[...] = jnp.concatenate([yqt, yqt], 1)

    def hb_copy(i):
        return copy(hits_out.at[i], hits_back.at[i], s_hb.at[0], r_hb.at[0], plane_back(i))

    wide = 4
    span = wide * 256
    r16 = rows_of((16, span))

    def over_hits(v):
        return v if wide == 1 else jnp.concatenate([v] * wide, 1)

    def pairs(j):
        first = j * wide
        @pl.when(j == 0)
        def _():
            settle(hits_ref.at[pl.ds(1, wide - 1)], r_hit.at[0])

        @pl.when(j > 0)
        def _():
            settle(hits_ref.at[pl.ds(first, wide)], r_hit.at[j])

        blks = [hits_ref[first + k] for k in range(wide)]
        xs = jnp.concatenate([v for b in blks for v in (b[0:16], b[16:32])], 1)
        q = jnp.concatenate([v for b in blks for v in (b[32:33], b[33:34])], 1)
        key_i = jnp.concatenate([v for b in blks for v in (b[34:35], b[35:36])], 1)
        xh, xm, xl = split3(xs)
        sh, sm, sl = split3(jnp.sum(xs * xs, 0, keepdims=True))
        tail_x = jnp.where(r16 == 0, sh, jnp.where(r16 == 1, sm, jnp.where(r16 == 2, sl, jnp.where(r16 < 6, 1.0, 0.0))))
        xcat = jnp.concatenate([xh, xm, xh, xm, xl, xh, tail_x, jnp.zeros((16, span), f32)], 0).astype(bf16)
        d2 = jnp.maximum(jnp.dot(ycat_ref[...], xcat, preferred_element_type=f32), 0.0)
        t = d2 + dist_eps
        inv = lax.rsqrt(t)
        reach = jnp.maximum(1.0 - t * inv, 0.0)
        match = over_hits(id_ref[...]) == key_i
        pot = jnp.where(match, d2, reach * reach)
        cc = jnp.where(match, 1.0, -(reach * inv))
        pot_rows = jnp.sum(pot * over_hits(qp_ref[...]), 0, keepdims=True)
        weighted = pot * q
        pot_sum = weighted[:, 0:256]
        for k in range(1, wide):
            pot_sum = pot_sum + weighted[:, 256 * k : 256 * k + 256]
        pot_ref[...] += pot_sum
        cc_hi = cc.astype(bf16)
        cc_lo = (cc - cc_hi.astype(f32)).astype(bf16)
        ht = jnp.dot(yqt_ref[...], jnp.concatenate([cc_hi, cc_lo], 0), preferred_element_type=f32)
        ht = (ht[0:32] + ht[32:64]) + ht[64:96]
        for k in range(wide):
            lo = slice(256 * k, 256 * k + 128)
            hi = slice(256 * k + 128, 256 * k + 256)
            ends = jnp.where(
                r8s == 0, ht[16:17, lo], jnp.where(r8s == 1, ht[16:17, hi], jnp.where(r8s == 2, pot_rows[:, lo], pot_rows[:, hi]))
            )
            hits_out[first + k] = jnp.concatenate([ht[0:16, lo], ht[0:16, hi], ends], 0)
        xq = jnp.concatenate([xs * q, jnp.where(r16 == 0, q, 0.0)], 0)
        xqh, xqm, xql = split3(xq)
        xq_all = jnp.concatenate([xqh, xqm, xql, jnp.zeros((32, span), f32)], 0).astype(bf16)
        ptacc_ref[...] += nt_dot(cc_hi, xq_all) + nt_dot(cc_lo, xq_all)
        for k in range(wide):
            if k > 0:
                hb_copy(first + k).start()
            else:

                @pl.when(j > 0)
                def _():
                    hb_copy(first).start()

    each(0, 16 // wide, pairs)
    settle(hits_ref.at[pl.ds(1, 15)], s_hit.at[0])

    acc = ptacc_ref[...]
    acc = (acc + pltpu.roll(acc, 96, 1)) + pltpu.roll(acc, 64, 1)
    pot_cols = jnp.sum(pot_ref[...], 1, keepdims=True)
    pts_out[...] = jnp.where(lanes_of((128, 128)) == 17, pot_cols, acc).reshape(16, 8, 128)

    def pb_copy(i):
        return copy(pts_out.at[i], pts_back.at[i], s_pb.at[0], r_pb.at[0], column_back(i))

    each(1, 16, lambda i: pb_copy(i).start())
    settle(hits_back.at[pl.ds(1, 15)], s_hb.at[0], r_hb.at[0])
    hsum = hits_out[0]
    for i in range(1, 16):
        hsum = hsum + hits_back[i]
    pull = jnp.concatenate([hsum[0:16], hsum[16:32]], 1)
    coef_i = jnp.concatenate([hsum[32:33], hsum[33:34]], 1)
    pot_i = jnp.concatenate([hsum[34:35], hsum[35:36]], 1)
    coord_grad = (2.0 * charge / HITS) * (coords * coef_i - pull)
    settle(pts_back.at[pl.ds(1, 15)], s_pb.at[0], r_pb.at[0])
    psum = pts_out[0]
    for i in range(1, 16):
        psum = psum + pts_back[i]
    lane = lanes_of((8, 128))
    grads = jnp.where(
        lane < 16,
        (2.0 * own_pts[:, 16:17] / HITS) * (own_pts * psum[:, 16:17] - psum),
        jnp.where(lane == 16, psum[:, 17:18] / HITS, 0.0),
    )
    gh, gm, gl = split3(grads)
    zeros8 = jnp.zeros((8, 128), f32)
    g3 = jnp.concatenate([gh, gm, gl, zeros8], 0).astype(bf16)
    sel3 = jnp.concatenate([sel, sel, sel, jnp.zeros((8, 256), f32)], 0).astype(bf16)
    spread_back = tn_dot(g3, sel3)
    count = jnp.sum(sel, 0, keepdims=True)
    coord_grad = coord_grad + spread_back[0:16]
    charge_grad = pot_i / HITS + spread_back[16:17]
    beta_grad = noise_f / HITS - count * (1.0 / POINTS)
    logit_grad = charge_grad * slope + beta_grad * beta * (1.0 - beta)
    loss_row = charge * pot_i / HITS + (count - count * beta) / POINTS + noise_f * beta / HITS
    loss_local = jnp.sum(loss_row, 1, keepdims=True)

    low = jnp.concatenate([coord_grad, jnp.where(rows_of((16, 256)) == 0, logit_grad, 0.0)], 0).astype(bf16)
    head = jnp.dot(low, act_ref[3], preferred_element_type=f32)
    up = tn_dot(low, wcb)

    def core_copy(j):
        if j == 0 or j == 4:
            span = pl.ds(0, 4) if j == 0 else pl.ds(4, 1)
            src, dst = partz_ref.at[other, :, span], corez_in.at[:, span]
        else:
            span = pl.ds(2 * j - 2, 2)
            src, dst = part_ref.at[other, :, span], core_in.at[:, span]
        return copy(src, dst, s_core.at[j], r_core.at[j], partner)

    def core_sum(j):
        core_copy(j).wait()
        if j == 0 or j == 4:
            first, last = (0, 4) if j == 0 else (4, 5)
            partz_ref[core, :, first:last] += corez_in[:, first:last]
        else:
            part_ref[core, :, 2 * j - 2 : 2 * j] += core_in[:, 2 * j - 2 : 2 * j]

    def span_of(c, table):
        first, last = table[c]
        return pl.ds(first, last - first)

    def xy_copy(c, i):
        span = span_of(c, chunks)
        target = ((x + i // 4) % 4) * 4 + (y + i % 4) % 4
        return copy(part_ref.at[core, target, span], xy_in.at[i, span], s_xy.at[c], r_xy.at[c], plane(i))

    def z_copy(c, i):
        block = zsum_ref.at[z, span_of(c, chunks)]
        return copy(block, block, s_z.at[c], r_z.at[c], ring(i))

    def g_copy(c, i):
        block = full_ref.at[core, here, span_of(c, chunks)]
        return copy(block, block, s_g.at[c], r_g.at[c, i // 4], plane(i))

    def f_copy(c, i):
        block = full_ref.at[core, pl.ds(((x + 4 - i) % 4) * 4, 4), span_of(c, chunks)]
        return copy(block, block, s_f.at[c], r_f.at[c], partner)

    def bz_copy(c, i):
        span = span_of(c, zchunks)
        return copy(partz_ref.at[core, (z + i) % 8, span], z_in.at[i, span], s_bz.at[c], r_bz.at[c], ring(i))

    def bx_copy(c, i):
        block = xysum_ref.at[here, span_of(c, zchunks)]
        return copy(block, block, s_bx.at[c], r_bx.at[c], plane(i))

    def bg_copy(c, i):
        block = fullz_ref.at[core, z, span_of(c, zchunks)]
        return copy(block, block, s_bg.at[c], r_bg.at[c], ring(i))

    def bf_copy(c):
        block = fullz_ref.at[core, :, span_of(c, zchunks)]
        return copy(block, block, s_bf.at[c], r_bf.at[c], partner)

    def layer_grad(layer, up):
        local = (up * pre_ref[layer]).astype(bf16)
        wg = jnp.dot(actt_ref[layer], local, preferred_element_type=f32)
        for half in range(2):
            cols = wg[:, half * 128 : half * 128 + 128]
            if layer == 3:
                partz_ref[:, :, 2 * half : 2 * half + 2] = cols.reshape(2, 8, 2, 8, 128)
            else:
                part_ref[:, :, 2 * (2 - layer) + half] = cols.reshape(2, 16, 8, 128)
        core_copy(3 - layer).start()
        bias = jnp.sum(local.astype(f32), 0, keepdims=True)
        return bias, nt_dot(local, w_ref[layer]) if layer > 0 else None

    biases = [None] * 4
    biases[3], up = layer_grad(3, up)
    biases[2], up = layer_grad(2, up)
    biases[1], up = layer_grad(1, up)
    biases[0], up = layer_grad(0, up)
    core_sum(0)
    each(1, 8, lambda i: bz_copy(0, i).start())
    ext8 = jnp.where(
        row8 == 0,
        head[16:17],
        jnp.where(
            row8 == 1,
            biases[0],
            jnp.where(
                row8 == 2,
                biases[1],
                jnp.where(row8 == 3, biases[2], jnp.where(row8 == 4, biases[3], jnp.where(row8 == 5, loss_local, 0.0))),
            ),
        ),
    )
    ext = jnp.concatenate([head[0:16], ext8], 0)
    for half in range(2):
        cols = ext[:, half * 128 : half * 128 + 128].reshape(3, 8, 128)
        partz_ref[half, :, 4] = jnp.concatenate([cols, jnp.zeros((5, 8, 128), f32)], 0)
    core_copy(4).start()
    core_sum(1)
    core_sum(2)
    each(1, 16, lambda i: xy_copy(0, i).start())
    core_sum(3)
    each(1, 16, lambda i: xy_copy(1, i).start())
    core_sum(4)
    each(1, 8, lambda i: bz_copy(1, i).start())

    def z_first(c):
        first, last = zchunks[c]
        settle(z_in.at[pl.ds(1, 7), span_of(c, zchunks)], s_bz.at[c], r_bz.at[c])
        total = partz_ref[core, z, first:last]
        for i in range(1, 8):
            total = total + z_in[i, first:last]
        xysum_ref[here, first:last] = total
        each(1, 16, lambda i: bx_copy(c, i).start())

    def plane_first(c):
        first, last = chunks[c]
        settle(xy_in.at[pl.ds(1, 15), span_of(c, chunks)], s_xy.at[c], r_xy.at[c])
        total = part_ref[core, here, first:last]
        for i in range(1, 16):
            total = total + xy_in[i, first:last]
        zsum_ref[z, first:last] = total
        each(1, 8, lambda i: z_copy(c, i).start())

    def z_last(c):
        first, last = zchunks[c]
        settle(xysum_ref.at[pl.ds(1, 15), span_of(c, zchunks)], s_bx.at[c], r_bx.at[c])
        total = xysum_ref[0, first:last]
        for i in range(1, 16):
            total = total + xysum_ref[i, first:last]
        fullz_ref[core, z, first:last] = total
        each(1, 8, lambda i: bg_copy(c, i).start())

    def plane_last(c):
        first, last = chunks[c]
        settle(zsum_ref.at[pl.ds(1, 7), span_of(c, chunks)], s_z.at[c], r_z.at[c])
        total = zsum_ref[0, first:last]
        for i in range(1, 8):
            total = total + zsum_ref[i, first:last]
        full_ref[core, here, first:last] = total
        each(1, 16, lambda i: g_copy(c, i).start())

    z_first(0)
    plane_first(0)
    z_first(1)
    plane_first(1)
    z_last(0)
    plane_last(0)
    z_last(1)
    plane_last(1)
    def z_hand_on(c):
        settle(fullz_ref.at[core, pl.ds(1, 7), span_of(c, zchunks)], s_bg.at[c], r_bg.at[c])
        bf_copy(c).start()

    def plane_hand_on(c):
        span = span_of(c, chunks)
        settle(full_ref.at[core, pl.ds(1, 3), span], r_g.at[c, 0])
        f_copy(c, 0).start()

        def step(i):
            settle(full_ref.at[core, pl.ds(0, 4), span], r_g.at[c, i])
            f_copy(c, i).start()
        each(1, 4, step)

    def place(layer):
        for half in range(2):
            cols = slice(half * 128, half * 128 + 128)
            if layer == 3:
                gw_ref[3, :, cols] = fullz_ref[:, :, 2 * half : 2 * half + 2].reshape(256, 128)
            else:
                gw_ref[layer, :, cols] = full_ref[:, :, 2 * (2 - layer) + half].reshape(256, 128)

    z_hand_on(0)
    z_hand_on(1)
    plane_hand_on(0)
    plane_hand_on(1)
    bf_copy(0).wait()
    place(3)
    bf_copy(1).wait()
    gc_ref[...] = jnp.concatenate(
        [fullz_ref[half, 0:2, 4].reshape(16, 128) for half in range(2)], 1
    )
    last = jnp.concatenate([fullz_ref[half, 2, 4] for half in range(2)], 1)
    gbeta_ref[...] = last[0:1]
    gb_ref[...] = last[1:5]
    loss_ref[...] = last[5:6, 0:1]

    for c in range(2):
        settle(full_ref.at[core, pl.ds(1, 15), span_of(c, chunks)], s_g.at[c])
        settle(full_ref.at[core, :, span_of(c, chunks)], s_f.at[c], r_f.at[c])
    place(2)
    place(1)
    place(0)


def deliver(*refs):
    sems = refs[10]
    copies = [pltpu.make_async_copy(refs[i], refs[5 + i], sems.at[i]) for i in range(5)]
    for copy in copies:
        copy.start()
    for copy in copies:
        copy.wait()


def on_device(features, w_layers, b_layers, w_coord, w_beta, point_hit, track, noise):
    vmem = pl.BlockSpec(memory_space=pltpu.VMEM)
    hbm = pl.BlockSpec(memory_space=pltpu.HBM)
    dma = pltpu.SemaphoreType.DMA
    results = (
        jax.ShapeDtypeStruct((4, 256, 256), f32),
        jax.ShapeDtypeStruct((4, 256), f32),
        jax.ShapeDtypeStruct((16, 256), f32),
        jax.ShapeDtypeStruct((1, 256), f32),
        jax.ShapeDtypeStruct((1, 1), f32),
    )
    grads = pl.pallas_call(
        kernel,
        name="condense",
        out_shape=results,
        in_specs=[hbm] * 8,
        out_specs=(vmem,) * 5,
        scratch_shapes=[
            pltpu.VMEM((256, 256), bf16),
            pltpu.VMEM((4, 256, 256), bf16),
            pltpu.VMEM((4, 256), f32),
            pltpu.VMEM((16, 256), bf16),
            pltpu.VMEM((256,), bf16),
            pltpu.SMEM((8,), jnp.int32),
            pltpu.VMEM((256,), jnp.int32),
            pltpu.VMEM((256,), jnp.int32),
            dma((11,)),
            pltpu.VMEM((4, 256, 256), f32),
            pltpu.VMEM((4, 256, 256), bf16),
            pltpu.VMEM((4, 256, 256), bf16),
            pltpu.VMEM((16, 40, 128), f32),
            pltpu.VMEM((16, 40, 128), f32),
            pltpu.VMEM((16, 40, 128), f32),
            pltpu.VMEM((16, 8, 128), f32),
            pltpu.VMEM((16, 8, 128), f32),
            pltpu.VMEM((16, 8, 128), f32),
            pltpu.VMEM((128, 128), bf16),
            pltpu.VMEM((96, 256), bf16),
            pltpu.VMEM((128, 256), f32),
            pltpu.VMEM((128, 256), f32),
            pltpu.VMEM((128, 256), f32),
            pltpu.VMEM((128, 128), f32),
            pltpu.VMEM((2, 16, 6, 8, 128), f32),
            pltpu.VMEM((16, 6, 8, 128), f32),
            pltpu.VMEM((16, 6, 8, 128), f32),
            pltpu.VMEM((8, 6, 8, 128), f32),
            pltpu.VMEM((2, 16, 6, 8, 128), f32),
            pltpu.VMEM((2, 8, 5, 8, 128), f32),
            pltpu.VMEM((8, 5, 8, 128), f32),
            pltpu.VMEM((8, 5, 8, 128), f32),
            pltpu.VMEM((16, 5, 8, 128), f32),
            pltpu.VMEM((2, 8, 5, 8, 128), f32),
            dma((1,)), dma((4,)), dma((1,)), dma((1,)),
            dma((1,)), dma((1,)), dma((1,)), dma((1,)),
            dma((5,)), dma((5,)), dma((2,)), dma((2,)),
            dma((2,)), dma((2,)), dma((2,)), dma((2, 4)),
            dma((2,)), dma((2,)),
            dma((2,)), dma((2,)), dma((2,)), dma((2,)),
            dma((2,)), dma((2,)), dma((2,)), dma((2,)),
        ],
        compiler_params=pltpu.CompilerParams(
            collective_id=0, has_side_effects=True, vmem_limit_bytes=48 << 20
        ),
    )(*[pltpu.with_memory_space_constraint(v, pltpu.HBM) for v in (features, w_layers, b_layers, w_coord, w_beta, point_hit, track, noise)])
    grad_w, grad_b, grad_c, grad_beta, loss = pl.pallas_call(
        deliver,
        name="deliver",
        out_shape=results,
        in_specs=[vmem] * 5,
        out_specs=(hbm,) * 5,
        scratch_shapes=[dma((5,))],
        compiler_params=pltpu.CompilerParams(vmem_limit_bytes=8 << 20),
    )(*grads)
    return grad_w, grad_b, grad_c, grad_beta.reshape(256), loss.reshape(())


def solution(mesh):
    return jax.shard_map(
        on_device,
        mesh=mesh,
        in_specs=(
            P(("layer", "phi"), None),
            P(),
            P(),
            P(),
            P(),
            P(("layer", "phi")),
            P(("layer", "phi")),
            P(("layer", "phi")),
        ),
        out_specs=(P(), P(), P(), P(), P()),
        check_vma=False,
    )
```

```python
import jax
import jax.numpy as jnp
from jax import lax
from jax.sharding import PartitionSpec as P
from jax.experimental import pallas as pl
from jax.experimental.pallas import tpu as pltpu

f32 = jnp.float32
bf16 = jnp.bfloat16
dist_eps = 0.0001
charge_floor = 0.5
MESH = pl.DeviceIdType.MESH
HITS = 65536.0
POINTS = 2048.0
far_plane = (10, 6, 9, 11, 14, 2, 8, 5, 7, 13, 15, 1, 3, 4, 12)
far_column = (9, 8, 7, 11, 6, 10, 5, 13, 4, 12, 3, 15, 2, 14, 1)
far_ring = (4, 3, 5, 2, 6, 1, 7)
chunks = ((0, 2), (2, 4), (4, 6))
zchunks = ((0, 4), (4, 5))


def split3(v):
    hi = v.astype(bf16).astype(f32)
    rest = v - hi
    mid = rest.astype(bf16).astype(f32)
    low = (rest - mid).astype(bf16).astype(f32)
    return hi, mid, low


def rows_of(shape):
    return lax.broadcasted_iota(jnp.int32, shape, 0)


def lanes_of(shape):
    return lax.broadcasted_iota(jnp.int32, shape, 1)


def nt_dot(a, b):
    return lax.dot_general(a, b, (((1,), (1,)), ((), ())), preferred_element_type=f32)


def tn_dot(a, b):
    return lax.dot_general(a, b, (((0,), (0,)), ((), ())), preferred_element_type=f32)


def kernel(
    feat_hbm, w_hbm, b_hbm, wc_hbm, wb_hbm, hit_hbm, track_hbm, noise_hbm,
    gw_ref, gb_ref, gc_ref, gbeta_ref, loss_ref,
    feat_ref, w_ref, b_ref, wc_ref, wb_ref, hit_ref, track_ref, noise_ref, s_in,
    pre_ref, act_ref, actt_ref,
    hits_ref, hits_back, hits_out, pts_ref, pts_back, pts_out,
    ycat_ref, yqt_ref, qp_ref, id_ref, pot_ref, ptacc_ref,
    part_ref, core_in, xy_in, zsum_ref, full_ref,
    partz_ref, corez_in, z_in, xysum_ref, fullz_ref,
    s_hit, r_hit, s_pt, r_pt, s_hb, r_hb, s_pb, r_pb,
    s_core, r_core, s_xy, r_xy, s_z, r_z, s_g, r_g, s_f, r_f,
    s_bz, r_bz, s_bx, r_bx, s_bg, r_bg, s_bf, r_bf,
):
    loads = [
        pltpu.make_async_copy(src, dst, s_in.at[i])
        for i, (src, dst) in enumerate(
            [
                (feat_hbm, feat_ref),
                (w_hbm.at[0], w_ref.at[0]),
                (b_hbm, b_ref),
                (w_hbm.at[1], w_ref.at[1]),
                (w_hbm.at[2], w_ref.at[2]),
                (w_hbm.at[3], w_ref.at[3]),
                (wc_hbm, wc_ref),
                (wb_hbm, wb_ref),
                (track_hbm, track_ref),
                (noise_hbm, noise_ref),
                (hit_hbm, hit_ref),
            ]
        )
    ]
    for load in loads:
        load.start()
    lay = lax.axis_index("layer")
    phi = lax.axis_index("phi")
    z = (lay // 8) * 4 + phi % 4
    y = (lay // 2) % 4
    core = lay % 2
    x = phi // 4
    other = 1 - core
    here = x * 4 + y

    def device(px, py, pz, pc):
        return ((pz // 4) * 8 + py * 2 + pc, px * 4 + pz % 4)

    def plane(step):
        return device((x + step // 4) % 4, (y + step % 4) % 4, z, core)

    def plane_back(step):
        return device((x + 4 - step // 4) % 4, (y + 4 - step % 4) % 4, z, core)

    def column(step):
        return device(x, y, (z + step // 2) % 8, (core + step % 2) % 2)

    def column_back(step):
        return device(x, y, (z + 8 - step // 2) % 8, (core + 2 - step % 2) % 2)

    def ring(step):
        return device(x, y, (z + step) % 8, core)

    partner = device(x, y, z, other)

    def copy(src, dst, ssem, rsem, target):
        return pltpu.make_async_remote_copy(
            src_ref=src, dst_ref=dst, send_sem=ssem, recv_sem=rsem,
            device_id=target, device_id_type=MESH,
        )

    def settle(ref, *sems):
        for sem in sems:
            pltpu.make_async_copy(ref, ref, sem).wait()

    def each(first, last, body):
        def step(i, carry):
            body(i)
            return carry
        lax.fori_loop(first, last, step, 0)

    def over(order, body):
        for i in order:
            body(i)

    barrier = pltpu.get_barrier_semaphore()

    def greet(i):
        pl.semaphore_signal(barrier, inc=1, device_id=plane(i), device_id_type=MESH)
        pl.semaphore_signal(barrier, inc=1, device_id=column(i), device_id_type=MESH)
    each(1, 16, greet)

    for load in loads[0:3]:
        load.wait()
    hidden = feat_ref[...]
    for layer in range(4):
        if layer > 0:
            loads[2 + layer].wait()
        pre = jnp.dot(hidden, w_ref[layer], preferred_element_type=f32) + b_ref[layer : layer + 1, :]
        pre_ref[layer] = pre
        hidden = (pre * jax.nn.sigmoid(pre)).astype(bf16)
        act_ref[layer] = hidden
    for load in loads[6:11]:
        load.wait()
    wcb = jnp.concatenate(
        [
            wc_ref[...].astype(f32),
            jnp.where(rows_of((16, 256)) == 0, wb_ref[...].astype(f32).reshape(1, 256), 0.0),
        ],
        0,
    ).astype(bf16)
    xz = nt_dot(wcb, hidden)
    coords = xz[0:16]
    logits = xz[16:17]
    expz = jnp.exp(logits)
    spread = jnp.log1p(2.0 * expz)
    charge = 0.25 * spread * spread + charge_floor
    slope = 0.5 * spread * (2.0 * expz / (1.0 + 2.0 * expz))
    beta = jax.nn.sigmoid(logits)
    noise = noise_ref[...].reshape(1, 256)
    track = track_ref[...].reshape(1, 256)
    key = jnp.where(noise == 0, track, -1).astype(f32)
    noise_f = noise.astype(f32)
    square = jnp.sum(coords * coords, 0, keepdims=True)
    row8 = rows_of((8, 256))
    lane8 = lanes_of((8, 256))
    pack = jnp.where(row8 == 0, charge, jnp.where(row8 == 1, key, jnp.where(row8 == 2, square, 0.0)))
    mine = jnp.concatenate([coords, pack], 0)
    r8s = rows_of((8, 128))
    tail_h = jnp.where(r8s == 0, charge[:, 0:128], jnp.where(r8s == 1, charge[:, 128:256], jnp.where(r8s == 2, key[:, 0:128], jnp.where(r8s == 3, key[:, 128:256], 0.0))))
    hits_ref[0] = jnp.concatenate([coords[:, 0:128], coords[:, 128:256], tail_h], 0)
    sel = jnp.zeros((8, 256), f32)
    for k in range(8):
        sel = jnp.where((row8 == k) & (lane8 == hit_ref[k]), 1.0, sel)
    sel_low = sel.astype(bf16)
    mine128 = jnp.concatenate([mine, jnp.zeros((104, 256), f32)], 0)
    mh, mm, ml = split3(mine128)
    own_pts = (nt_dot(sel_low, mh.astype(bf16)) + nt_dot(sel_low, mm.astype(bf16))) + nt_dot(sel_low, ml.astype(bf16))
    linear = lay * 16 + phi
    ident = (linear * 8 + rows_of((8, 128))).astype(f32)
    own_pts = jnp.where(lanes_of((8, 128)) == 17, ident, own_pts)
    pts_ref[0] = own_pts

    pl.semaphore_wait(barrier, 30)

    def pt_copy(i):
        return copy(pts_ref.at[0], pts_ref.at[i], s_pt.at[0], r_pt.at[0], column(i))

    def hit_copy(i):
        return copy(hits_ref.at[0], hits_ref.at[i], s_hit.at[0], r_hit.at[i // 4], plane(i))

    over(far_column, lambda i: pt_copy(i).start())
    over(far_plane, lambda i: hit_copy(i).start())

    actt_ref[0] = feat_ref[...].T
    for layer in range(4):
        pre = pre_ref[layer]
        sig = jax.nn.sigmoid(pre)
        pre_ref[layer] = sig * (1.0 + pre * (1.0 - sig))
        if layer < 3:
            actt_ref[layer + 1] = act_ref[layer].T
    ptacc_ref[...] = jnp.zeros((128, 128), f32)
    pot_ref[...] = jnp.zeros((128, 256), f32)

    settle(pts_ref.at[pl.ds(1, 15)], s_pt.at[0], r_pt.at[0])
    points = pts_ref[...].reshape(128, 128)
    qp_ref[...] = jnp.broadcast_to(points[:, 16:17], (128, 256))
    id_ref[...] = jnp.broadcast_to(points[:, 17:18], (128, 256))
    pt = points.T
    y_t = pt[0:16]
    qp_t = pt[16:17]
    yh, ym, yl = split3(-2.0 * y_t)
    sqh, sqm, sql = split3(pt[18:19])
    row16 = rows_of((16, 128))
    tail = jnp.where(row16 < 3, 1.0, jnp.where(row16 == 3, sqh, jnp.where(row16 == 4, sqm, jnp.where(row16 == 5, sql, 0.0))))
    ycat_ref[...] = jnp.concatenate([yh, yh, ym, ym, yh, yl, tail, jnp.zeros((16, 128), f32)], 0).T.astype(bf16)
    yq = jnp.concatenate([y_t * qp_t, jnp.where(row16 == 0, qp_t, 0.0)], 0)
    yqh, yqm, yql = split3(yq)
    yqt = jnp.concatenate([yqh, yqm, yql], 0).astype(bf16)
    yqt_ref[...] = jnp.concatenate([yqt, yqt], 1)

    def hb_copy(i):
        return copy(hits_out.at[i], hits_back.at[i], s_hb.at[0], r_hb.at[0], plane_back(i))

    wide = 4
    span = wide * 256
    r16 = rows_of((16, span))

    def over_hits(v):
        return v if wide == 1 else jnp.concatenate([v] * wide, 1)

    def pairs(turn):
        j = (turn * 2) % 4 + turn // 2
        first = j * wide
        @pl.when(j == 0)
        def _():
            settle(hits_ref.at[pl.ds(1, wide - 1)], r_hit.at[0])

        @pl.when(j > 0)
        def _():
            settle(hits_ref.at[pl.ds(first, wide)], r_hit.at[j])

        blks = [hits_ref[first + k] for k in range(wide)]
        xs = jnp.concatenate([v for b in blks for v in (b[0:16], b[16:32])], 1)
        q = jnp.concatenate([v for b in blks for v in (b[32:33], b[33:34])], 1)
        key_i = jnp.concatenate([v for b in blks for v in (b[34:35], b[35:36])], 1)
        xh, xm, xl = split3(xs)
        sh, sm, sl = split3(jnp.sum(xs * xs, 0, keepdims=True))
        tail_x = jnp.where(r16 == 0, sh, jnp.where(r16 == 1, sm, jnp.where(r16 == 2, sl, jnp.where(r16 < 6, 1.0, 0.0))))
        xcat = jnp.concatenate([xh, xm, xh, xm, xl, xh, tail_x, jnp.zeros((16, span), f32)], 0).astype(bf16)
        d2 = jnp.maximum(jnp.dot(ycat_ref[...], xcat, preferred_element_type=f32), 0.0)
        t = d2 + dist_eps
        inv = lax.rsqrt(t)
        reach = jnp.maximum(1.0 - t * inv, 0.0)
        match = over_hits(id_ref[...]) == key_i
        pot = jnp.where(match, d2, reach * reach)
        cc = jnp.where(match, 1.0, -(reach * inv))
        pot_rows = jnp.sum(pot * over_hits(qp_ref[...]), 0, keepdims=True)
        weighted = pot * q
        pot_sum = weighted[:, 0:256]
        for k in range(1, wide):
            pot_sum = pot_sum + weighted[:, 256 * k : 256 * k + 256]
        pot_ref[...] += pot_sum
        cc_hi = cc.astype(bf16)
        cc_lo = (cc - cc_hi.astype(f32)).astype(bf16)
        ht = jnp.dot(yqt_ref[...], jnp.concatenate([cc_hi, cc_lo], 0), preferred_element_type=f32)
        ht = (ht[0:32] + ht[32:64]) + ht[64:96]
        for k in range(wide):
            lo = slice(256 * k, 256 * k + 128)
            hi = slice(256 * k + 128, 256 * k + 256)
            ends = jnp.where(
                r8s == 0, ht[16:17, lo], jnp.where(r8s == 1, ht[16:17, hi], jnp.where(r8s == 2, pot_rows[:, lo], pot_rows[:, hi]))
            )
            hits_out[first + k] = jnp.concatenate([ht[0:16, lo], ht[0:16, hi], ends], 0)
        xq = jnp.concatenate([xs * q, jnp.where(r16 == 0, q, 0.0)], 0)
        xqh, xqm, xql = split3(xq)
        xq_all = jnp.concatenate([xqh, xqm, xql, jnp.zeros((32, span), f32)], 0).astype(bf16)
        ptacc_ref[...] += nt_dot(cc_hi, xq_all) + nt_dot(cc_lo, xq_all)
        for k in range(wide):
            if k > 0:
                hb_copy(first + k).start()
            else:

                @pl.when(j > 0)
                def _():
                    hb_copy(first).start()

    each(0, 16 // wide, pairs)
    settle(hits_ref.at[pl.ds(1, 15)], s_hit.at[0])

    acc = ptacc_ref[...]
    acc = (acc + pltpu.roll(acc, 96, 1)) + pltpu.roll(acc, 64, 1)
    pot_cols = jnp.sum(pot_ref[...], 1, keepdims=True)
    pts_out[...] = jnp.where(lanes_of((128, 128)) == 17, pot_cols, acc).reshape(16, 8, 128)

    def pb_copy(i):
        return copy(pts_out.at[i], pts_back.at[i], s_pb.at[0], r_pb.at[0], column_back(i))

    over(far_column, lambda i: pb_copy(i).start())
    settle(hits_back.at[pl.ds(1, 15)], s_hb.at[0], r_hb.at[0])
    hsum = hits_out[0]
    for i in range(1, 16):
        hsum = hsum + hits_back[i]
    pull = jnp.concatenate([hsum[0:16], hsum[16:32]], 1)
    coef_i = jnp.concatenate([hsum[32:33], hsum[33:34]], 1)
    pot_i = jnp.concatenate([hsum[34:35], hsum[35:36]], 1)
    coord_grad = (2.0 * charge / HITS) * (coords * coef_i - pull)
    settle(pts_back.at[pl.ds(1, 15)], s_pb.at[0], r_pb.at[0])
    psum = pts_out[0]
    for i in range(1, 16):
        psum = psum + pts_back[i]
    lane = lanes_of((8, 128))
    grads = jnp.where(
        lane < 16,
        (2.0 * own_pts[:, 16:17] / HITS) * (own_pts * psum[:, 16:17] - psum),
        jnp.where(lane == 16, psum[:, 17:18] / HITS, 0.0),
    )
    gh, gm, gl = split3(grads)
    zeros8 = jnp.zeros((8, 128), f32)
    g3 = jnp.concatenate([gh, gm, gl, zeros8], 0).astype(bf16)
    sel3 = jnp.concatenate([sel, sel, sel, jnp.zeros((8, 256), f32)], 0).astype(bf16)
    spread_back = tn_dot(g3, sel3)
    count = jnp.sum(sel, 0, keepdims=True)
    coord_grad = coord_grad + spread_back[0:16]
    charge_grad = pot_i / HITS + spread_back[16:17]
    beta_grad = noise_f / HITS - count * (1.0 / POINTS)
    logit_grad = charge_grad * slope + beta_grad * beta * (1.0 - beta)
    loss_row = charge * pot_i / HITS + (count - count * beta) / POINTS + noise_f * beta / HITS
    loss_local = jnp.sum(loss_row, 1, keepdims=True)

    low = jnp.concatenate([coord_grad, jnp.where(rows_of((16, 256)) == 0, logit_grad, 0.0)], 0).astype(bf16)
    head = jnp.dot(low, act_ref[3], preferred_element_type=f32)
    up = tn_dot(low, wcb)

    def core_copy(j):
        if j == 0 or j == 4:
            span = pl.ds(0, 4) if j == 0 else pl.ds(4, 1)
            src, dst = partz_ref.at[other, :, span], corez_in.at[:, span]
        else:
            span = pl.ds(2 * j - 2, 2)
            src, dst = part_ref.at[other, :, span], core_in.at[:, span]
        return copy(src, dst, s_core.at[j], r_core.at[j], partner)

    def core_sum(j):
        core_copy(j).wait()
        if j == 0 or j == 4:
            first, last = (0, 4) if j == 0 else (4, 5)
            partz_ref[core, :, first:last] += corez_in[:, first:last]
        else:
            part_ref[core, :, 2 * j - 2 : 2 * j] += core_in[:, 2 * j - 2 : 2 * j]

    def span_of(c, table):
        first, last = table[c]
        return pl.ds(first, last - first)

    def xy_copy(c, i):
        span = span_of(c, chunks)
        target = ((x + i // 4) % 4) * 4 + (y + i % 4) % 4
        return copy(part_ref.at[core, target, span], xy_in.at[i, span], s_xy.at[c], r_xy.at[c], plane(i))

    def z_copy(c, i):
        block = zsum_ref.at[z, span_of(c, chunks)]
        return copy(block, block, s_z.at[c], r_z.at[c], ring(i))

    def g_copy(c, i):
        block = full_ref.at[core, here, span_of(c, chunks)]
        return copy(block, block, s_g.at[c], r_g.at[c, i // 4], plane(i))

    def f_copy(c, i):
        block = full_ref.at[core, pl.ds(((x + 4 - i) % 4) * 4, 4), span_of(c, chunks)]
        return copy(block, block, s_f.at[c], r_f.at[c], partner)

    def bz_copy(c, i):
        span = span_of(c, zchunks)
        return copy(partz_ref.at[core, (z + i) % 8, span], z_in.at[i, span], s_bz.at[c], r_bz.at[c], ring(i))

    def bx_copy(c, i):
        block = xysum_ref.at[here, span_of(c, zchunks)]
        return copy(block, block, s_bx.at[c], r_bx.at[c], plane(i))

    def bg_copy(c, i):
        block = fullz_ref.at[core, z, span_of(c, zchunks)]
        return copy(block, block, s_bg.at[c], r_bg.at[c], ring(i))

    def bf_copy(c):
        block = fullz_ref.at[core, :, span_of(c, zchunks)]
        return copy(block, block, s_bf.at[c], r_bf.at[c], partner)

    def layer_grad(layer, up):
        local = (up * pre_ref[layer]).astype(bf16)
        wg = jnp.dot(actt_ref[layer], local, preferred_element_type=f32)
        for half in range(2):
            cols = wg[:, half * 128 : half * 128 + 128]
            if layer == 3:
                partz_ref[:, :, 2 * half : 2 * half + 2] = cols.reshape(2, 8, 2, 8, 128)
            else:
                part_ref[:, :, 2 * (2 - layer) + half] = cols.reshape(2, 16, 8, 128)
        core_copy(3 - layer).start()
        bias = jnp.sum(local.astype(f32), 0, keepdims=True)
        return bias, nt_dot(local, w_ref[layer]) if layer > 0 else None

    biases = [None] * 4
    biases[3], up = layer_grad(3, up)
    biases[2], up = layer_grad(2, up)
    biases[1], up = layer_grad(1, up)
    biases[0], up = layer_grad(0, up)
    core_sum(0)
    over(far_ring, lambda i: bz_copy(0, i).start())
    ext8 = jnp.where(
        row8 == 0,
        head[16:17],
        jnp.where(
            row8 == 1,
            biases[0],
            jnp.where(
                row8 == 2,
                biases[1],
                jnp.where(row8 == 3, biases[2], jnp.where(row8 == 4, biases[3], jnp.where(row8 == 5, loss_local, 0.0))),
            ),
        ),
    )
    ext = jnp.concatenate([head[0:16], ext8], 0)
    for half in range(2):
        cols = ext[:, half * 128 : half * 128 + 128].reshape(3, 8, 128)
        partz_ref[half, :, 4] = jnp.concatenate([cols, jnp.zeros((5, 8, 128), f32)], 0)
    core_copy(4).start()
    core_sum(1)
    over(far_plane, lambda i: xy_copy(0, i).start())
    core_sum(2)
    over(far_plane, lambda i: xy_copy(1, i).start())
    core_sum(3)
    over(far_plane, lambda i: xy_copy(2, i).start())
    core_sum(4)
    over(far_ring, lambda i: bz_copy(1, i).start())

    def z_first(c):
        first, last = zchunks[c]
        settle(z_in.at[pl.ds(1, 7), span_of(c, zchunks)], s_bz.at[c], r_bz.at[c])
        total = partz_ref[core, z, first:last]
        for i in range(1, 8):
            total = total + z_in[i, first:last]
        xysum_ref[here, first:last] = total
        over(far_plane, lambda i: bx_copy(c, i).start())

    def plane_first(c):
        first, last = chunks[c]
        settle(xy_in.at[pl.ds(1, 15), span_of(c, chunks)], s_xy.at[c], r_xy.at[c])
        total = part_ref[core, here, first:last]
        for i in range(1, 16):
            total = total + xy_in[i, first:last]
        zsum_ref[z, first:last] = total
        over(far_ring, lambda i: z_copy(c, i).start())

    def z_last(c):
        first, last = zchunks[c]
        settle(xysum_ref.at[pl.ds(1, 15), span_of(c, zchunks)], s_bx.at[c], r_bx.at[c])
        total = xysum_ref[0, first:last]
        for i in range(1, 16):
            total = total + xysum_ref[i, first:last]
        fullz_ref[core, z, first:last] = total
        over(far_ring, lambda i: bg_copy(c, i).start())

    def plane_last(c):
        first, last = chunks[c]
        settle(zsum_ref.at[pl.ds(1, 7), span_of(c, chunks)], s_z.at[c], r_z.at[c])
        total = zsum_ref[0, first:last]
        for i in range(1, 8):
            total = total + zsum_ref[i, first:last]
        full_ref[core, here, first:last] = total
        over(far_plane, lambda i: g_copy(c, i).start())

    z_first(0)
    plane_first(0)
    plane_first(1)
    z_first(1)
    plane_first(2)
    z_last(0)
    plane_last(0)
    plane_last(1)
    z_last(1)
    plane_last(2)

    def z_hand_on(c):
        settle(fullz_ref.at[core, pl.ds(1, 7), span_of(c, zchunks)], s_bg.at[c], r_bg.at[c])
        bf_copy(c).start()

    def plane_hand_on(c):
        span = span_of(c, chunks)
        settle(full_ref.at[core, pl.ds(1, 3), span], r_g.at[c, 0])
        f_copy(c, 0).start()

        def step(i):
            settle(full_ref.at[core, pl.ds(0, 4), span], r_g.at[c, i])
            f_copy(c, i).start()
        each(1, 4, step)

    def place(layer):
        for half in range(2):
            cols = slice(half * 128, half * 128 + 128)
            if layer == 3:
                gw_ref[3, :, cols] = fullz_ref[:, :, 2 * half : 2 * half + 2].reshape(256, 128)
            else:
                gw_ref[layer, :, cols] = full_ref[:, :, 2 * (2 - layer) + half].reshape(256, 128)

    plane_hand_on(0)
    z_hand_on(0)
    z_hand_on(1)
    plane_hand_on(1)
    plane_hand_on(2)
    bf_copy(0).wait()
    place(3)
    bf_copy(1).wait()
    gc_ref[...] = jnp.concatenate(
        [fullz_ref[half, 0:2, 4].reshape(16, 128) for half in range(2)], 1
    )
    last = jnp.concatenate([fullz_ref[half, 2, 4] for half in range(2)], 1)
    gbeta_ref[...] = last[0:1]
    gb_ref[...] = last[1:5]
    loss_ref[...] = last[5:6, 0:1]

    for c in range(3):
        settle(full_ref.at[core, pl.ds(1, 15), span_of(c, chunks)], s_g.at[c])
        settle(full_ref.at[core, :, span_of(c, chunks)], s_f.at[c], r_f.at[c])
    place(2)
    place(1)
    place(0)


def deliver(*refs):
    sems = refs[10]
    copies = [pltpu.make_async_copy(refs[i], refs[5 + i], sems.at[i]) for i in range(5)]
    for copy in copies:
        copy.start()
    for copy in copies:
        copy.wait()


def on_device(features, w_layers, b_layers, w_coord, w_beta, point_hit, track, noise):
    vmem = pl.BlockSpec(memory_space=pltpu.VMEM)
    hbm = pl.BlockSpec(memory_space=pltpu.HBM)
    dma = pltpu.SemaphoreType.DMA
    results = (
        jax.ShapeDtypeStruct((4, 256, 256), f32),
        jax.ShapeDtypeStruct((4, 256), f32),
        jax.ShapeDtypeStruct((16, 256), f32),
        jax.ShapeDtypeStruct((1, 256), f32),
        jax.ShapeDtypeStruct((1, 1), f32),
    )
    grads = pl.pallas_call(
        kernel,
        name="condense",
        out_shape=results,
        in_specs=[hbm] * 8,
        out_specs=(vmem,) * 5,
        scratch_shapes=[
            pltpu.VMEM((256, 256), bf16),
            pltpu.VMEM((4, 256, 256), bf16),
            pltpu.VMEM((4, 256), f32),
            pltpu.VMEM((16, 256), bf16),
            pltpu.VMEM((256,), bf16),
            pltpu.SMEM((8,), jnp.int32),
            pltpu.VMEM((256,), jnp.int32),
            pltpu.VMEM((256,), jnp.int32),
            dma((11,)),
            pltpu.VMEM((4, 256, 256), f32),
            pltpu.VMEM((4, 256, 256), bf16),
            pltpu.VMEM((4, 256, 256), bf16),
            pltpu.VMEM((16, 40, 128), f32),
            pltpu.VMEM((16, 40, 128), f32),
            pltpu.VMEM((16, 40, 128), f32),
            pltpu.VMEM((16, 8, 128), f32),
            pltpu.VMEM((16, 8, 128), f32),
            pltpu.VMEM((16, 8, 128), f32),
            pltpu.VMEM((128, 128), bf16),
            pltpu.VMEM((96, 256), bf16),
            pltpu.VMEM((128, 256), f32),
            pltpu.VMEM((128, 256), f32),
            pltpu.VMEM((128, 256), f32),
            pltpu.VMEM((128, 128), f32),
            pltpu.VMEM((2, 16, 6, 8, 128), f32),
            pltpu.VMEM((16, 6, 8, 128), f32),
            pltpu.VMEM((16, 6, 8, 128), f32),
            pltpu.VMEM((8, 6, 8, 128), f32),
            pltpu.VMEM((2, 16, 6, 8, 128), f32),
            pltpu.VMEM((2, 8, 5, 8, 128), f32),
            pltpu.VMEM((8, 5, 8, 128), f32),
            pltpu.VMEM((8, 5, 8, 128), f32),
            pltpu.VMEM((16, 5, 8, 128), f32),
            pltpu.VMEM((2, 8, 5, 8, 128), f32),
            dma((1,)), dma((4,)), dma((1,)), dma((1,)),
            dma((1,)), dma((1,)), dma((1,)), dma((1,)),
            dma((5,)), dma((5,)), dma((3,)), dma((3,)),
            dma((3,)), dma((3,)), dma((3,)), dma((3, 4)),
            dma((3,)), dma((3,)),
            dma((2,)), dma((2,)), dma((2,)), dma((2,)),
            dma((2,)), dma((2,)), dma((2,)), dma((2,)),
        ],
        compiler_params=pltpu.CompilerParams(
            collective_id=0, has_side_effects=True, vmem_limit_bytes=48 << 20
        ),
    )(*[pltpu.with_memory_space_constraint(v, pltpu.HBM) for v in (features, w_layers, b_layers, w_coord, w_beta, point_hit, track, noise)])
    grad_w, grad_b, grad_c, grad_beta, loss = pl.pallas_call(
        deliver,
        name="deliver",
        out_shape=results,
        in_specs=[vmem] * 5,
        out_specs=(hbm,) * 5,
        scratch_shapes=[dma((5,))],
        compiler_params=pltpu.CompilerParams(vmem_limit_bytes=8 << 20),
    )(*grads)
    return grad_w, grad_b, grad_c, grad_beta.reshape(256), loss.reshape(())


def solution(mesh):
    return jax.shard_map(
        on_device,
        mesh=mesh,
        in_specs=(
            P(("layer", "phi"), None),
            P(),
            P(),
            P(),
            P(),
            P(("layer", "phi")),
            P(("layer", "phi")),
            P(("layer", "phi")),
        ),
        out_specs=(P(), P(), P(), P(), P()),
        check_vma=False,
    )
```

```python
import jax
import jax.numpy as jnp
from jax import lax
from jax.sharding import PartitionSpec as P
from jax.experimental import pallas as pl
from jax.experimental.pallas import tpu as pltpu

f32 = jnp.float32
bf16 = jnp.bfloat16
dist_eps = 0.0001
charge_floor = 0.5
MESH = pl.DeviceIdType.MESH
HITS = 65536.0
POINTS = 2048.0
far_plane = (10, 6, 9, 11, 14, 2, 8, 5, 7, 13, 15, 1, 3, 4, 12)
far_column = (9, 8, 7, 11, 6, 10, 5, 13, 4, 12, 3, 15, 2, 14, 1)
far_ring = (4, 3, 5, 2, 6, 1, 7)
chunks = ((0, 2), (2, 4), (4, 6))
zchunks = ((0, 4), (4, 5))


def split3(v):
    hi = v.astype(bf16).astype(f32)
    rest = v - hi
    mid = rest.astype(bf16).astype(f32)
    low = (rest - mid).astype(bf16).astype(f32)
    return hi, mid, low


def rows_of(shape):
    return lax.broadcasted_iota(jnp.int32, shape, 0)


def lanes_of(shape):
    return lax.broadcasted_iota(jnp.int32, shape, 1)


def nt_dot(a, b):
    return lax.dot_general(a, b, (((1,), (1,)), ((), ())), preferred_element_type=f32)


def tn_dot(a, b):
    return lax.dot_general(a, b, (((0,), (0,)), ((), ())), preferred_element_type=f32)


def kernel(
    feat_hbm, w_hbm, b_hbm, wc_hbm, wb_hbm, hit_hbm, track_hbm, noise_hbm,
    gw_ref, gb_ref, gc_ref, gbeta_ref, loss_ref,
    feat_ref, w_ref, b_ref, wc_ref, wb_ref, hit_ref, track_ref, noise_ref, s_in,
    pre_ref, act_ref, actt_ref,
    hits_ref, hits_back, hits_out, pts_ref, pts_back, pts_out,
    ycat_ref, yqt_ref, qp_ref, id_ref, pot_ref, ptacc_ref,
    part_ref, core_in, xy_in, zsum_ref, full_ref,
    partz_ref, corez_in, z_in, xysum_ref, fullz_ref,
    s_hit, r_hit, s_pt, r_pt, s_hb, r_hb, s_pb, r_pb,
    s_core, r_core, s_xy, r_xy, s_z, r_z, s_g, r_g, s_f, r_f,
    s_bz, r_bz, s_bx, r_bx, s_bg, r_bg, s_bf, r_bf,
):
    loads = [
        pltpu.make_async_copy(src, dst, s_in.at[i])
        for i, (src, dst) in enumerate(
            [
                (feat_hbm, feat_ref),
                (w_hbm.at[0], w_ref.at[0]),
                (b_hbm, b_ref),
                (w_hbm.at[1], w_ref.at[1]),
                (w_hbm.at[2], w_ref.at[2]),
                (w_hbm.at[3], w_ref.at[3]),
                (wc_hbm, wc_ref),
                (wb_hbm, wb_ref),
                (track_hbm, track_ref),
                (noise_hbm, noise_ref),
                (hit_hbm, hit_ref),
            ]
        )
    ]
    lay = lax.axis_index("layer")
    phi = lax.axis_index("phi")
    z = (lay // 8) * 4 + phi % 4
    y = (lay // 2) % 4
    core = lay % 2
    x = phi // 4
    other = 1 - core
    here = x * 4 + y

    def device(px, py, pz, pc):
        return ((pz // 4) * 8 + py * 2 + pc, px * 4 + pz % 4)

    def plane(step):
        return device((x + step // 4) % 4, (y + step % 4) % 4, z, core)

    def plane_back(step):
        return device((x + 4 - step // 4) % 4, (y + 4 - step % 4) % 4, z, core)

    def column(step):
        return device(x, y, (z + step // 2) % 8, (core + step % 2) % 2)

    def column_back(step):
        return device(x, y, (z + 8 - step // 2) % 8, (core + 2 - step % 2) % 2)

    def ring(step):
        return device(x, y, (z + step) % 8, core)

    partner = device(x, y, z, other)

    def copy(src, dst, ssem, rsem, target):
        return pltpu.make_async_remote_copy(
            src_ref=src, dst_ref=dst, send_sem=ssem, recv_sem=rsem,
            device_id=target, device_id_type=MESH,
        )

    def settle(ref, *sems):
        for sem in sems:
            pltpu.make_async_copy(ref, ref, sem).wait()

    def each(first, last, body):
        def step(i, carry):
            body(i)
            return carry
        lax.fori_loop(first, last, step, 0)

    def over(order, body):
        for i in order:
            body(i)

    barrier = pltpu.get_barrier_semaphore()

    def greet(i, j):
        pl.semaphore_signal(barrier, inc=1, device_id=column(j), device_id_type=MESH)
        pl.semaphore_signal(barrier, inc=1, device_id=plane(i), device_id_type=MESH)

    for near, tall in zip(far_plane, far_column):
        greet(near, tall)
    for load in loads:
        load.start()

    for load in loads[0:3]:
        load.wait()
    hidden = feat_ref[...]
    for layer in range(4):
        if layer > 0:
            loads[2 + layer].wait()
        pre = jnp.dot(hidden, w_ref[layer], preferred_element_type=f32) + b_ref[layer : layer + 1, :]
        pre_ref[layer] = pre
        hidden = (pre * jax.nn.sigmoid(pre)).astype(bf16)
        act_ref[layer] = hidden
    for load in loads[6:11]:
        load.wait()
    wcb = jnp.concatenate(
        [
            wc_ref[...].astype(f32),
            jnp.where(rows_of((16, 256)) == 0, wb_ref[...].astype(f32).reshape(1, 256), 0.0),
        ],
        0,
    ).astype(bf16)
    xz = nt_dot(wcb, hidden)
    coords = xz[0:16]
    logits = xz[16:17]
    expz = jnp.exp(logits)
    spread = jnp.log1p(2.0 * expz)
    charge = 0.25 * spread * spread + charge_floor
    slope = 0.5 * spread * (2.0 * expz / (1.0 + 2.0 * expz))
    beta = jax.nn.sigmoid(logits)
    noise = noise_ref[...].reshape(1, 256)
    track = track_ref[...].reshape(1, 256)
    key = jnp.where(noise == 0, track, -1).astype(f32)
    noise_f = noise.astype(f32)
    square = jnp.sum(coords * coords, 0, keepdims=True)
    row8 = rows_of((8, 256))
    lane8 = lanes_of((8, 256))
    pack = jnp.where(row8 == 0, charge, jnp.where(row8 == 1, key, jnp.where(row8 == 2, square, 0.0)))
    mine = jnp.concatenate([coords, pack], 0)
    r8s = rows_of((8, 128))
    tail_h = jnp.where(r8s == 0, charge[:, 0:128], jnp.where(r8s == 1, charge[:, 128:256], jnp.where(r8s == 2, key[:, 0:128], jnp.where(r8s == 3, key[:, 128:256], 0.0))))
    hits_ref[0] = jnp.concatenate([coords[:, 0:128], coords[:, 128:256], tail_h], 0)
    sel = jnp.zeros((8, 256), f32)
    for k in range(8):
        sel = jnp.where((row8 == k) & (lane8 == hit_ref[k]), 1.0, sel)
    sel_low = sel.astype(bf16)
    mine128 = jnp.concatenate([mine, jnp.zeros((104, 256), f32)], 0)
    mh, mm, ml = split3(mine128)
    own_pts = (nt_dot(sel_low, mh.astype(bf16)) + nt_dot(sel_low, mm.astype(bf16))) + nt_dot(sel_low, ml.astype(bf16))
    linear = lay * 16 + phi
    ident = (linear * 8 + rows_of((8, 128))).astype(f32)
    own_pts = jnp.where(lanes_of((8, 128)) == 17, ident, own_pts)
    pts_ref[0] = own_pts

    pl.semaphore_wait(barrier, 30)

    def pt_copy(i):
        return copy(pts_ref.at[0], pts_ref.at[i], s_pt.at[0], r_pt.at[0], column(i))

    def hit_copy(i):
        return copy(hits_ref.at[0], hits_ref.at[i], s_hit.at[0], r_hit.at[i // 4], plane(i))

    over(far_column, lambda i: pt_copy(i).start())
    over(far_plane, lambda i: hit_copy(i).start())

    actt_ref[0] = feat_ref[...].T
    for layer in range(4):
        pre = pre_ref[layer]
        sig = jax.nn.sigmoid(pre)
        pre_ref[layer] = sig * (1.0 + pre * (1.0 - sig))
        if layer < 3:
            actt_ref[layer + 1] = act_ref[layer].T
    ptacc_ref[...] = jnp.zeros((128, 128), f32)
    pot_ref[...] = jnp.zeros((128, 256), f32)

    settle(pts_ref.at[pl.ds(1, 15)], s_pt.at[0], r_pt.at[0])
    points = pts_ref[...].reshape(128, 128)
    qp_ref[...] = jnp.broadcast_to(points[:, 16:17], (128, 256))
    id_ref[...] = jnp.broadcast_to(points[:, 17:18], (128, 256))
    pt = points.T
    y_t = pt[0:16]
    qp_t = pt[16:17]
    yh, ym, yl = split3(-2.0 * y_t)
    sqh, sqm, sql = split3(pt[18:19])
    row16 = rows_of((16, 128))
    tail = jnp.where(row16 < 3, 1.0, jnp.where(row16 == 3, sqh, jnp.where(row16 == 4, sqm, jnp.where(row16 == 5, sql, 0.0))))
    ycat_ref[...] = jnp.concatenate([yh, yh, ym, ym, yh, yl, tail, jnp.zeros((16, 128), f32)], 0).T.astype(bf16)
    yq = jnp.concatenate([y_t * qp_t, jnp.where(row16 == 0, qp_t, 0.0)], 0)
    yqh, yqm, yql = split3(yq)
    yqt = jnp.concatenate([yqh, yqm, yql], 0).astype(bf16)
    yqt_ref[...] = jnp.concatenate([yqt, yqt], 1)

    def hb_copy(i):
        return copy(hits_out.at[i], hits_back.at[i], s_hb.at[0], r_hb.at[0], plane_back(i))

    wide = 4
    span = wide * 256
    r16 = rows_of((16, span))

    def over_hits(v):
        return v if wide == 1 else jnp.concatenate([v] * wide, 1)

    def pairs(turn):
        j = (turn * 2) % 4 + turn // 2
        first = j * wide
        @pl.when(j == 0)
        def _():
            settle(hits_ref.at[pl.ds(1, wide - 1)], r_hit.at[0])

        @pl.when(j > 0)
        def _():
            settle(hits_ref.at[pl.ds(first, wide)], r_hit.at[j])

        blks = [hits_ref[first + k] for k in range(wide)]
        xs = jnp.concatenate([v for b in blks for v in (b[0:16], b[16:32])], 1)
        q = jnp.concatenate([v for b in blks for v in (b[32:33], b[33:34])], 1)
        key_i = jnp.concatenate([v for b in blks for v in (b[34:35], b[35:36])], 1)
        xh, xm, xl = split3(xs)
        sh, sm, sl = split3(jnp.sum(xs * xs, 0, keepdims=True))
        tail_x = jnp.where(r16 == 0, sh, jnp.where(r16 == 1, sm, jnp.where(r16 == 2, sl, jnp.where(r16 < 6, 1.0, 0.0))))
        xcat = jnp.concatenate([xh, xm, xh, xm, xl, xh, tail_x, jnp.zeros((16, span), f32)], 0).astype(bf16)
        d2 = jnp.maximum(jnp.dot(ycat_ref[...], xcat, preferred_element_type=f32), 0.0)
        t = d2 + dist_eps
        inv = lax.rsqrt(t)
        reach = jnp.maximum(1.0 - t * inv, 0.0)
        match = over_hits(id_ref[...]) == key_i
        pot = jnp.where(match, d2, reach * reach)
        cc = jnp.where(match, 1.0, -(reach * inv))
        pot_rows = jnp.sum(pot * over_hits(qp_ref[...]), 0, keepdims=True)
        weighted = pot * q
        pot_sum = weighted[:, 0:256]
        for k in range(1, wide):
            pot_sum = pot_sum + weighted[:, 256 * k : 256 * k + 256]
        pot_ref[...] += pot_sum
        cc_hi = cc.astype(bf16)
        cc_lo = (cc - cc_hi.astype(f32)).astype(bf16)
        ht = jnp.dot(yqt_ref[...], jnp.concatenate([cc_hi, cc_lo], 0), preferred_element_type=f32)
        ht = (ht[0:32] + ht[32:64]) + ht[64:96]
        for k in range(wide):
            lo = slice(256 * k, 256 * k + 128)
            hi = slice(256 * k + 128, 256 * k + 256)
            ends = jnp.where(
                r8s == 0, ht[16:17, lo], jnp.where(r8s == 1, ht[16:17, hi], jnp.where(r8s == 2, pot_rows[:, lo], pot_rows[:, hi]))
            )
            hits_out[first + k] = jnp.concatenate([ht[0:16, lo], ht[0:16, hi], ends], 0)
        xq = jnp.concatenate([xs * q, jnp.where(r16 == 0, q, 0.0)], 0)
        xqh, xqm, xql = split3(xq)
        xq_all = jnp.concatenate([xqh, xqm, xql, jnp.zeros((32, span), f32)], 0).astype(bf16)
        ptacc_ref[...] += nt_dot(cc_hi, xq_all) + nt_dot(cc_lo, xq_all)
        for k in (2, 1, 3, 0):
            if k > 0:
                hb_copy(first + k).start()
            else:

                @pl.when(j > 0)
                def _():
                    hb_copy(first).start()

    each(0, 16 // wide, pairs)
    settle(hits_ref.at[pl.ds(1, 15)], s_hit.at[0])

    acc = ptacc_ref[...]
    acc = (acc + pltpu.roll(acc, 96, 1)) + pltpu.roll(acc, 64, 1)
    pot_cols = jnp.sum(pot_ref[...], 1, keepdims=True)
    pts_out[...] = jnp.where(lanes_of((128, 128)) == 17, pot_cols, acc).reshape(16, 8, 128)

    def pb_copy(i):
        return copy(pts_out.at[i], pts_back.at[i], s_pb.at[0], r_pb.at[0], column_back(i))

    over(far_column, lambda i: pb_copy(i).start())
    settle(hits_back.at[pl.ds(1, 15)], s_hb.at[0], r_hb.at[0])
    hsum = hits_out[0]
    for i in range(1, 16):
        hsum = hsum + hits_back[i]
    pull = jnp.concatenate([hsum[0:16], hsum[16:32]], 1)
    coef_i = jnp.concatenate([hsum[32:33], hsum[33:34]], 1)
    pot_i = jnp.concatenate([hsum[34:35], hsum[35:36]], 1)
    coord_grad = (2.0 * charge / HITS) * (coords * coef_i - pull)
    settle(pts_back.at[pl.ds(1, 15)], s_pb.at[0], r_pb.at[0])
    psum = pts_out[0]
    for i in range(1, 16):
        psum = psum + pts_back[i]
    lane = lanes_of((8, 128))
    grads = jnp.where(
        lane < 16,
        (2.0 * own_pts[:, 16:17] / HITS) * (own_pts * psum[:, 16:17] - psum),
        jnp.where(lane == 16, psum[:, 17:18] / HITS, 0.0),
    )
    gh, gm, gl = split3(grads)
    zeros8 = jnp.zeros((8, 128), f32)
    g3 = jnp.concatenate([gh, gm, gl, zeros8], 0).astype(bf16)
    sel3 = jnp.concatenate([sel, sel, sel, jnp.zeros((8, 256), f32)], 0).astype(bf16)
    spread_back = tn_dot(g3, sel3)
    count = jnp.sum(sel, 0, keepdims=True)
    coord_grad = coord_grad + spread_back[0:16]
    charge_grad = pot_i / HITS + spread_back[16:17]
    beta_grad = noise_f / HITS - count * (1.0 / POINTS)
    logit_grad = charge_grad * slope + beta_grad * beta * (1.0 - beta)
    loss_row = charge * pot_i / HITS + (count - count * beta) / POINTS + noise_f * beta / HITS
    loss_local = jnp.sum(loss_row, 1, keepdims=True)

    low = jnp.concatenate([coord_grad, jnp.where(rows_of((16, 256)) == 0, logit_grad, 0.0)], 0).astype(bf16)
    head = jnp.dot(low, act_ref[3], preferred_element_type=f32)
    up = tn_dot(low, wcb)

    def core_copy(j):
        if j == 0 or j == 4:
            span = pl.ds(0, 4) if j == 0 else pl.ds(4, 1)
            src, dst = partz_ref.at[other, :, span], corez_in.at[:, span]
        else:
            span = pl.ds(2 * j - 2, 2)
            src, dst = part_ref.at[other, :, span], core_in.at[:, span]
        return copy(src, dst, s_core.at[j], r_core.at[j], partner)

    def core_sum(j):
        core_copy(j).wait()
        if j == 0 or j == 4:
            first, last = (0, 4) if j == 0 else (4, 5)
            partz_ref[core, :, first:last] += corez_in[:, first:last]
        else:
            part_ref[core, :, 2 * j - 2 : 2 * j] += core_in[:, 2 * j - 2 : 2 * j]

    def span_of(c, table):
        first, last = table[c]
        return pl.ds(first, last - first)

    def xy_copy(c, i):
        span = span_of(c, chunks)
        target = ((x + i // 4) % 4) * 4 + (y + i % 4) % 4
        return copy(part_ref.at[core, target, span], xy_in.at[i, span], s_xy.at[c], r_xy.at[c], plane(i))

    def z_copy(c, i):
        block = zsum_ref.at[z, span_of(c, chunks)]
        return copy(block, block, s_z.at[c], r_z.at[c], ring(i))

    def g_copy(c, i):
        block = full_ref.at[core, here, span_of(c, chunks)]
        return copy(block, block, s_g.at[c], r_g.at[c, i // 4], plane(i))

    def f_copy(c, i):
        block = full_ref.at[core, pl.ds(((x + 4 - i) % 4) * 4, 4), span_of(c, chunks)]
        return copy(block, block, s_f.at[c], r_f.at[c], partner)

    def bz_copy(c, i):
        span = span_of(c, zchunks)
        return copy(partz_ref.at[core, (z + i) % 8, span], z_in.at[i, span], s_bz.at[c], r_bz.at[c], ring(i))

    def bx_copy(c, i):
        block = xysum_ref.at[here, span_of(c, zchunks)]
        return copy(block, block, s_bx.at[c], r_bx.at[c], plane(i))

    def bg_copy(c, i):
        block = fullz_ref.at[core, z, span_of(c, zchunks)]
        return copy(block, block, s_bg.at[c], r_bg.at[c], ring(i))

    def bf_copy(c):
        block = fullz_ref.at[core, :, span_of(c, zchunks)]
        return copy(block, block, s_bf.at[c], r_bf.at[c], partner)

    def layer_grad(layer, up):
        local = (up * pre_ref[layer]).astype(bf16)
        wg = jnp.dot(actt_ref[layer], local, preferred_element_type=f32)
        for half in range(2):
            cols = wg[:, half * 128 : half * 128 + 128]
            if layer == 3:
                partz_ref[:, :, 2 * half : 2 * half + 2] = cols.reshape(2, 8, 2, 8, 128)
            else:
                part_ref[:, :, 2 * (2 - layer) + half] = cols.reshape(2, 16, 8, 128)
        core_copy(3 - layer).start()
        bias = jnp.sum(local.astype(f32), 0, keepdims=True)
        return bias, nt_dot(local, w_ref[layer]) if layer > 0 else None

    biases = [None] * 4
    biases[3], up = layer_grad(3, up)
    biases[2], up = layer_grad(2, up)
    biases[1], up = layer_grad(1, up)
    biases[0], up = layer_grad(0, up)
    core_sum(0)
    over(far_ring, lambda i: bz_copy(0, i).start())
    ext8 = jnp.where(
        row8 == 0,
        head[16:17],
        jnp.where(
            row8 == 1,
            biases[0],
            jnp.where(
                row8 == 2,
                biases[1],
                jnp.where(row8 == 3, biases[2], jnp.where(row8 == 4, biases[3], jnp.where(row8 == 5, loss_local, 0.0))),
            ),
        ),
    )
    ext = jnp.concatenate([head[0:16], ext8], 0)
    for half in range(2):
        cols = ext[:, half * 128 : half * 128 + 128].reshape(3, 8, 128)
        partz_ref[half, :, 4] = jnp.concatenate([cols, jnp.zeros((5, 8, 128), f32)], 0)
    core_copy(4).start()
    core_sum(1)
    over(far_plane, lambda i: xy_copy(0, i).start())
    core_sum(2)
    over(far_plane, lambda i: xy_copy(1, i).start())
    core_sum(3)
    over(far_plane, lambda i: xy_copy(2, i).start())
    core_sum(4)
    over(far_ring, lambda i: bz_copy(1, i).start())

    def z_first(c):
        first, last = zchunks[c]
        settle(z_in.at[pl.ds(1, 7), span_of(c, zchunks)], s_bz.at[c], r_bz.at[c])
        total = partz_ref[core, z, first:last]
        for i in range(1, 8):
            total = total + z_in[i, first:last]
        xysum_ref[here, first:last] = total
        over(far_plane, lambda i: bx_copy(c, i).start())

    def plane_first(c):
        first, last = chunks[c]
        settle(xy_in.at[pl.ds(1, 15), span_of(c, chunks)], s_xy.at[c], r_xy.at[c])
        total = part_ref[core, here, first:last]
        for i in range(1, 16):
            total = total + xy_in[i, first:last]
        zsum_ref[z, first:last] = total
        over(far_ring, lambda i: z_copy(c, i).start())

    def z_last(c):
        first, last = zchunks[c]
        settle(xysum_ref.at[pl.ds(1, 15), span_of(c, zchunks)], s_bx.at[c], r_bx.at[c])
        total = xysum_ref[0, first:last]
        for i in range(1, 16):
            total = total + xysum_ref[i, first:last]
        fullz_ref[core, z, first:last] = total
        over(far_ring, lambda i: bg_copy(c, i).start())

    def plane_last(c):
        first, last = chunks[c]
        settle(zsum_ref.at[pl.ds(1, 7), span_of(c, chunks)], s_z.at[c], r_z.at[c])
        total = zsum_ref[0, first:last]
        for i in range(1, 8):
            total = total + zsum_ref[i, first:last]
        full_ref[core, here, first:last] = total
        over(far_plane, lambda i: g_copy(c, i).start())

    z_first(0)
    plane_first(0)
    plane_first(1)
    z_first(1)
    plane_first(2)
    z_last(0)
    plane_last(0)
    plane_last(1)
    z_last(1)
    plane_last(2)

    def z_hand_on(c):
        settle(fullz_ref.at[core, pl.ds(1, 7), span_of(c, zchunks)], s_bg.at[c], r_bg.at[c])
        bf_copy(c).start()

    def plane_hand_on(c):
        span = span_of(c, chunks)
        settle(full_ref.at[core, pl.ds(1, 3), span], r_g.at[c, 0])
        f_copy(c, 0).start()

        def step(i):
            settle(full_ref.at[core, pl.ds(0, 4), span], r_g.at[c, i])
            f_copy(c, i).start()
        each(1, 4, step)

    def place(layer):
        for half in range(2):
            cols = slice(half * 128, half * 128 + 128)
            if layer == 3:
                gw_ref[3, :, cols] = fullz_ref[:, :, 2 * half : 2 * half + 2].reshape(256, 128)
            else:
                gw_ref[layer, :, cols] = full_ref[:, :, 2 * (2 - layer) + half].reshape(256, 128)

    plane_hand_on(0)
    z_hand_on(0)
    z_hand_on(1)
    plane_hand_on(1)
    plane_hand_on(2)
    bf_copy(0).wait()
    place(3)
    bf_copy(1).wait()
    gc_ref[...] = jnp.concatenate(
        [fullz_ref[half, 0:2, 4].reshape(16, 128) for half in range(2)], 1
    )
    last = jnp.concatenate([fullz_ref[half, 2, 4] for half in range(2)], 1)
    gbeta_ref[...] = last[0:1]
    gb_ref[...] = last[1:5]
    loss_ref[...] = last[5:6, 0:1]

    for c in range(3):
        settle(full_ref.at[core, pl.ds(1, 15), span_of(c, chunks)], s_g.at[c])
        settle(full_ref.at[core, :, span_of(c, chunks)], s_f.at[c], r_f.at[c])
    place(2)
    place(1)
    place(0)


def deliver(*refs):
    sems = refs[10]
    copies = [pltpu.make_async_copy(refs[i], refs[5 + i], sems.at[i]) for i in range(5)]
    for copy in copies:
        copy.start()
    for copy in copies:
        copy.wait()


def on_device(features, w_layers, b_layers, w_coord, w_beta, point_hit, track, noise):
    vmem = pl.BlockSpec(memory_space=pltpu.VMEM)
    hbm = pl.BlockSpec(memory_space=pltpu.HBM)
    dma = pltpu.SemaphoreType.DMA
    results = (
        jax.ShapeDtypeStruct((4, 256, 256), f32),
        jax.ShapeDtypeStruct((4, 256), f32),
        jax.ShapeDtypeStruct((16, 256), f32),
        jax.ShapeDtypeStruct((1, 256), f32),
        jax.ShapeDtypeStruct((1, 1), f32),
    )
    grads = pl.pallas_call(
        kernel,
        name="condense",
        out_shape=results,
        in_specs=[hbm] * 8,
        out_specs=(vmem,) * 5,
        scratch_shapes=[
            pltpu.VMEM((256, 256), bf16),
            pltpu.VMEM((4, 256, 256), bf16),
            pltpu.VMEM((4, 256), f32),
            pltpu.VMEM((16, 256), bf16),
            pltpu.VMEM((256,), bf16),
            pltpu.SMEM((8,), jnp.int32),
            pltpu.VMEM((256,), jnp.int32),
            pltpu.VMEM((256,), jnp.int32),
            dma((11,)),
            pltpu.VMEM((4, 256, 256), f32),
            pltpu.VMEM((4, 256, 256), bf16),
            pltpu.VMEM((4, 256, 256), bf16),
            pltpu.VMEM((16, 40, 128), f32),
            pltpu.VMEM((16, 40, 128), f32),
            pltpu.VMEM((16, 40, 128), f32),
            pltpu.VMEM((16, 8, 128), f32),
            pltpu.VMEM((16, 8, 128), f32),
            pltpu.VMEM((16, 8, 128), f32),
            pltpu.VMEM((128, 128), bf16),
            pltpu.VMEM((96, 256), bf16),
            pltpu.VMEM((128, 256), f32),
            pltpu.VMEM((128, 256), f32),
            pltpu.VMEM((128, 256), f32),
            pltpu.VMEM((128, 128), f32),
            pltpu.VMEM((2, 16, 6, 8, 128), f32),
            pltpu.VMEM((16, 6, 8, 128), f32),
            pltpu.VMEM((16, 6, 8, 128), f32),
            pltpu.VMEM((8, 6, 8, 128), f32),
            pltpu.VMEM((2, 16, 6, 8, 128), f32),
            pltpu.VMEM((2, 8, 5, 8, 128), f32),
            pltpu.VMEM((8, 5, 8, 128), f32),
            pltpu.VMEM((8, 5, 8, 128), f32),
            pltpu.VMEM((16, 5, 8, 128), f32),
            pltpu.VMEM((2, 8, 5, 8, 128), f32),
            dma((1,)), dma((4,)), dma((1,)), dma((1,)),
            dma((1,)), dma((1,)), dma((1,)), dma((1,)),
            dma((5,)), dma((5,)), dma((3,)), dma((3,)),
            dma((3,)), dma((3,)), dma((3,)), dma((3, 4)),
            dma((3,)), dma((3,)),
            dma((2,)), dma((2,)), dma((2,)), dma((2,)),
            dma((2,)), dma((2,)), dma((2,)), dma((2,)),
        ],
        compiler_params=pltpu.CompilerParams(
            collective_id=0, has_side_effects=True, vmem_limit_bytes=48 << 20
        ),
    )(*[pltpu.with_memory_space_constraint(v, pltpu.HBM) for v in (features, w_layers, b_layers, w_coord, w_beta, point_hit, track, noise)])
    grad_w, grad_b, grad_c, grad_beta, loss = pl.pallas_call(
        deliver,
        name="deliver",
        out_shape=results,
        in_specs=[vmem] * 5,
        out_specs=(hbm,) * 5,
        scratch_shapes=[dma((5,))],
        compiler_params=pltpu.CompilerParams(vmem_limit_bytes=8 << 20),
    )(*grads)
    return grad_w, grad_b, grad_c, grad_beta.reshape(256), loss.reshape(())


def solution(mesh):
    return jax.shard_map(
        on_device,
        mesh=mesh,
        in_specs=(
            P(("layer", "phi"), None),
            P(),
            P(),
            P(),
            P(),
            P(("layer", "phi")),
            P(("layer", "phi")),
            P(("layer", "phi")),
        ),
        out_specs=(P(), P(), P(), P(), P()),
        check_vma=False,
    )
```

```python
import jax
import jax.numpy as jnp
from jax import lax
from jax.sharding import PartitionSpec as P
from jax.experimental import pallas as pl
from jax.experimental.pallas import tpu as pltpu

f32 = jnp.float32
bf16 = jnp.bfloat16
dist_eps = 0.0001
charge_floor = 0.5
MESH = pl.DeviceIdType.MESH
HITS = 65536.0
POINTS = 2048.0
far_plane = (10, 6, 9, 11, 14, 2, 8, 5, 7, 13, 15, 1, 3, 4, 12)
far_column = (9, 8, 7, 11, 6, 10, 5, 13, 4, 12, 3, 15, 2, 14, 1)
far_hits = (10, 9, 11, 8, 2, 1, 3, 6, 5, 7, 4, 14, 13, 15, 12)
far_ring = (4, 3, 5, 2, 6, 1, 7)
chunks = ((0, 2), (2, 4), (4, 6))
zchunks = ((0, 4), (4, 5))


def split3(v):
    hi = v.astype(bf16).astype(f32)
    rest = v - hi
    mid = rest.astype(bf16).astype(f32)
    low = (rest - mid).astype(bf16).astype(f32)
    return hi, mid, low


def rows_of(shape):
    return lax.broadcasted_iota(jnp.int32, shape, 0)


def lanes_of(shape):
    return lax.broadcasted_iota(jnp.int32, shape, 1)


def nt_dot(a, b):
    return lax.dot_general(a, b, (((1,), (1,)), ((), ())), preferred_element_type=f32)


def tn_dot(a, b):
    return lax.dot_general(a, b, (((0,), (0,)), ((), ())), preferred_element_type=f32)


def kernel(
    feat_hbm, w_hbm, b_hbm, wc_hbm, wb_hbm, hit_hbm, track_hbm, noise_hbm,
    gw_ref, gb_ref, gc_ref, gbeta_ref, loss_ref,
    feat_ref, w_ref, b_ref, wc_ref, wb_ref, hit_ref, track_ref, noise_ref, s_in,
    pre_ref, act_ref, actt_ref,
    hits_ref, hits_back, hits_out, pts_ref, pts_back, pts_out,
    ycat_ref, yqt_ref, qp_ref, id_ref, pot_ref, ptacc_ref,
    part_ref, core_in, xy_in, zsum_ref, full_ref,
    partz_ref, corez_in, z_in, xysum_ref, fullz_ref,
    s_hit, r_hit, s_pt, r_pt, s_hb, r_hb, s_pb, r_pb,
    s_core, r_core, s_xy, r_xy, s_z, r_z, s_g, r_g, s_f, r_f,
    s_bz, r_bz, s_bx, r_bx, s_bg, r_bg, s_bf, r_bf,
):
    loads = [
        pltpu.make_async_copy(src, dst, s_in.at[i])
        for i, (src, dst) in enumerate(
            [
                (feat_hbm, feat_ref),
                (w_hbm.at[0], w_ref.at[0]),
                (b_hbm, b_ref),
                (w_hbm.at[1], w_ref.at[1]),
                (w_hbm.at[2], w_ref.at[2]),
                (w_hbm.at[3], w_ref.at[3]),
                (wc_hbm, wc_ref),
                (wb_hbm, wb_ref),
                (track_hbm, track_ref),
                (noise_hbm, noise_ref),
                (hit_hbm, hit_ref),
            ]
        )
    ]
    lay = lax.axis_index("layer")
    phi = lax.axis_index("phi")
    z = (lay // 8) * 4 + phi % 4
    y = (lay // 2) % 4
    core = lay % 2
    x = phi // 4
    other = 1 - core
    here = x * 4 + y

    def device(px, py, pz, pc):
        return ((pz // 4) * 8 + py * 2 + pc, px * 4 + pz % 4)

    def plane(step):
        return device((x + step // 4) % 4, (y + step % 4) % 4, z, core)

    def plane_back(step):
        return device((x + 4 - step // 4) % 4, (y + 4 - step % 4) % 4, z, core)

    def column(step):
        return device(x, y, (z + step // 2) % 8, (core + step % 2) % 2)

    def column_back(step):
        return device(x, y, (z + 8 - step // 2) % 8, (core + 2 - step % 2) % 2)

    def ring(step):
        return device(x, y, (z + step) % 8, core)

    partner = device(x, y, z, other)

    def copy(src, dst, ssem, rsem, target):
        return pltpu.make_async_remote_copy(
            src_ref=src, dst_ref=dst, send_sem=ssem, recv_sem=rsem,
            device_id=target, device_id_type=MESH,
        )

    def settle(ref, *sems):
        for sem in sems:
            pltpu.make_async_copy(ref, ref, sem).wait()

    def each(first, last, body):
        def step(i, carry):
            body(i)
            return carry
        lax.fori_loop(first, last, step, 0)

    def over(order, body):
        for i in order:
            body(i)

    barrier = pltpu.get_barrier_semaphore()

    def greet(i, j):
        pl.semaphore_signal(barrier, inc=1, device_id=column(j), device_id_type=MESH)
        pl.semaphore_signal(barrier, inc=1, device_id=plane(i), device_id_type=MESH)

    for near, tall in zip(far_plane, far_column):
        greet(near, tall)
    for load in loads:
        load.start()

    for load in loads[0:3]:
        load.wait()
    hidden = feat_ref[...]
    for layer in range(4):
        if layer > 0:
            loads[2 + layer].wait()
        pre = jnp.dot(hidden, w_ref[layer], preferred_element_type=f32) + b_ref[layer : layer + 1, :]
        pre_ref[layer] = pre
        hidden = (pre * jax.nn.sigmoid(pre)).astype(bf16)
        act_ref[layer] = hidden
    for load in loads[6:11]:
        load.wait()
    wcb = jnp.concatenate(
        [
            wc_ref[...].astype(f32),
            jnp.where(rows_of((16, 256)) == 0, wb_ref[...].astype(f32).reshape(1, 256), 0.0),
        ],
        0,
    ).astype(bf16)
    xz = nt_dot(wcb, hidden)
    coords = xz[0:16]
    logits = xz[16:17]
    expz = jnp.exp(logits)
    spread = jnp.log1p(2.0 * expz)
    charge = 0.25 * spread * spread + charge_floor
    slope = 0.5 * spread * (2.0 * expz / (1.0 + 2.0 * expz))
    beta = jax.nn.sigmoid(logits)
    noise = noise_ref[...].reshape(1, 256)
    track = track_ref[...].reshape(1, 256)
    key = jnp.where(noise == 0, track, -1).astype(f32)
    noise_f = noise.astype(f32)
    square = jnp.sum(coords * coords, 0, keepdims=True)
    row8 = rows_of((8, 256))
    lane8 = lanes_of((8, 256))
    pack = jnp.where(row8 == 0, charge, jnp.where(row8 == 1, key, jnp.where(row8 == 2, square, 0.0)))
    mine = jnp.concatenate([coords, pack], 0)
    r8s = rows_of((8, 128))
    tail_h = jnp.where(r8s == 0, charge[:, 0:128], jnp.where(r8s == 1, charge[:, 128:256], jnp.where(r8s == 2, key[:, 0:128], jnp.where(r8s == 3, key[:, 128:256], 0.0))))
    hits_ref[0] = jnp.concatenate([coords[:, 0:128], coords[:, 128:256], tail_h], 0)
    sel = jnp.zeros((8, 256), f32)
    for k in range(8):
        sel = jnp.where((row8 == k) & (lane8 == hit_ref[k]), 1.0, sel)
    sel_low = sel.astype(bf16)
    mine128 = jnp.concatenate([mine, jnp.zeros((104, 256), f32)], 0)
    mh, mm, ml = split3(mine128)
    own_pts = (nt_dot(sel_low, mh.astype(bf16)) + nt_dot(sel_low, mm.astype(bf16))) + nt_dot(sel_low, ml.astype(bf16))
    linear = lay * 16 + phi
    ident = (linear * 8 + rows_of((8, 128))).astype(f32)
    own_pts = jnp.where(lanes_of((8, 128)) == 17, ident, own_pts)
    pts_ref[0] = own_pts

    pl.semaphore_wait(barrier, 30)

    def pt_copy(i):
        return copy(pts_ref.at[0], pts_ref.at[i], s_pt.at[0], r_pt.at[0], column(i))

    def hit_copy(i):
        return copy(hits_ref.at[0], hits_ref.at[i], s_hit.at[0], r_hit.at[i // 4], plane(i))

    over(far_column, lambda i: pt_copy(i).start())
    over(far_hits, lambda i: hit_copy(i).start())

    actt_ref[0] = feat_ref[...].T
    for layer in range(4):
        pre = pre_ref[layer]
        sig = jax.nn.sigmoid(pre)
        pre_ref[layer] = sig * (1.0 + pre * (1.0 - sig))
        if layer < 3:
            actt_ref[layer + 1] = act_ref[layer].T
    ptacc_ref[...] = jnp.zeros((128, 128), f32)
    pot_ref[...] = jnp.zeros((128, 256), f32)

    settle(pts_ref.at[pl.ds(1, 15)], s_pt.at[0], r_pt.at[0])
    points = pts_ref[...].reshape(128, 128)
    qp_ref[...] = jnp.broadcast_to(points[:, 16:17], (128, 256))
    id_ref[...] = jnp.broadcast_to(points[:, 17:18], (128, 256))
    pt = points.T
    y_t = pt[0:16]
    qp_t = pt[16:17]
    yh, ym, yl = split3(-2.0 * y_t)
    sqh, sqm, sql = split3(pt[18:19])
    row16 = rows_of((16, 128))
    tail = jnp.where(row16 < 3, 1.0, jnp.where(row16 == 3, sqh, jnp.where(row16 == 4, sqm, jnp.where(row16 == 5, sql, 0.0))))
    ycat_ref[...] = jnp.concatenate([yh, yh, ym, ym, yh, yl, tail, jnp.zeros((16, 128), f32)], 0).T.astype(bf16)
    yq = jnp.concatenate([y_t * qp_t, jnp.where(row16 == 0, qp_t, 0.0)], 0)
    yqh, yqm, yql = split3(yq)
    yqt = jnp.concatenate([yqh, yqm, yql], 0).astype(bf16)
    yqt_ref[...] = jnp.concatenate([yqt, yqt], 1)

    def hb_copy(i):
        return copy(hits_out.at[i], hits_back.at[i], s_hb.at[0], r_hb.at[0], plane_back(i))

    wide = 4
    span = wide * 256
    r16 = rows_of((16, span))

    def over_hits(v):
        return v if wide == 1 else jnp.concatenate([v] * wide, 1)

    def pairs(turn):
        j = (turn * 2) % 4 + turn // 2
        first = j * wide
        @pl.when(j == 0)
        def _():
            settle(hits_ref.at[pl.ds(1, wide - 1)], r_hit.at[0])

        @pl.when(j > 0)
        def _():
            settle(hits_ref.at[pl.ds(first, wide)], r_hit.at[j])

        blks = [hits_ref[first + k] for k in range(wide)]
        xs = jnp.concatenate([v for b in blks for v in (b[0:16], b[16:32])], 1)
        q = jnp.concatenate([v for b in blks for v in (b[32:33], b[33:34])], 1)
        key_i = jnp.concatenate([v for b in blks for v in (b[34:35], b[35:36])], 1)
        xh, xm, xl = split3(xs)
        sh, sm, sl = split3(jnp.sum(xs * xs, 0, keepdims=True))
        tail_x = jnp.where(r16 == 0, sh, jnp.where(r16 == 1, sm, jnp.where(r16 == 2, sl, jnp.where(r16 < 6, 1.0, 0.0))))
        xcat = jnp.concatenate([xh, xm, xh, xm, xl, xh, tail_x, jnp.zeros((16, span), f32)], 0).astype(bf16)
        d2 = jnp.maximum(jnp.dot(ycat_ref[...], xcat, preferred_element_type=f32), 0.0)
        t = d2 + dist_eps
        inv = lax.rsqrt(t)
        reach = jnp.maximum(1.0 - t * inv, 0.0)
        match = over_hits(id_ref[...]) == key_i
        pot = jnp.where(match, d2, reach * reach)
        cc = jnp.where(match, 1.0, -(reach * inv))
        pot_rows = jnp.sum(pot * over_hits(qp_ref[...]), 0, keepdims=True)
        weighted = pot * q
        pot_sum = weighted[:, 0:256]
        for k in range(1, wide):
            pot_sum = pot_sum + weighted[:, 256 * k : 256 * k + 256]
        pot_ref[...] += pot_sum
        cc_hi = cc.astype(bf16)
        cc_lo = (cc - cc_hi.astype(f32)).astype(bf16)
        ht = jnp.dot(yqt_ref[...], jnp.concatenate([cc_hi, cc_lo], 0), preferred_element_type=f32)
        ht = (ht[0:32] + ht[32:64]) + ht[64:96]
        for k in range(wide):
            lo = slice(256 * k, 256 * k + 128)
            hi = slice(256 * k + 128, 256 * k + 256)
            ends = jnp.where(
                r8s == 0, ht[16:17, lo], jnp.where(r8s == 1, ht[16:17, hi], jnp.where(r8s == 2, pot_rows[:, lo], pot_rows[:, hi]))
            )
            hits_out[first + k] = jnp.concatenate([ht[0:16, lo], ht[0:16, hi], ends], 0)
        xq = jnp.concatenate([xs * q, jnp.where(r16 == 0, q, 0.0)], 0)
        xqh, xqm, xql = split3(xq)
        xq_all = jnp.concatenate([xqh, xqm, xql, jnp.zeros((32, span), f32)], 0).astype(bf16)
        ptacc_ref[...] += nt_dot(cc_hi, xq_all) + nt_dot(cc_lo, xq_all)
        for k in (2, 1, 3, 0):
            if k > 0:
                hb_copy(first + k).start()
            else:

                @pl.when(j > 0)
                def _():
                    hb_copy(first).start()

    each(0, 16 // wide, pairs)
    settle(hits_ref.at[pl.ds(1, 15)], s_hit.at[0])

    acc = ptacc_ref[...]
    acc = (acc + pltpu.roll(acc, 96, 1)) + pltpu.roll(acc, 64, 1)
    pot_cols = jnp.sum(pot_ref[...], 1, keepdims=True)
    pts_out[...] = jnp.where(lanes_of((128, 128)) == 17, pot_cols, acc).reshape(16, 8, 128)

    def pb_copy(i):
        return copy(pts_out.at[i], pts_back.at[i], s_pb.at[0], r_pb.at[0], column_back(i))

    over(far_column, lambda i: pb_copy(i).start())
    settle(hits_back.at[pl.ds(1, 15)], s_hb.at[0], r_hb.at[0])
    hsum = hits_out[0]
    for i in range(1, 16):
        hsum = hsum + hits_back[i]
    pull = jnp.concatenate([hsum[0:16], hsum[16:32]], 1)
    coef_i = jnp.concatenate([hsum[32:33], hsum[33:34]], 1)
    pot_i = jnp.concatenate([hsum[34:35], hsum[35:36]], 1)
    coord_grad = (2.0 * charge / HITS) * (coords * coef_i - pull)
    settle(pts_back.at[pl.ds(1, 15)], s_pb.at[0], r_pb.at[0])
    psum = pts_out[0]
    for i in range(1, 16):
        psum = psum + pts_back[i]
    lane = lanes_of((8, 128))
    grads = jnp.where(
        lane < 16,
        (2.0 * own_pts[:, 16:17] / HITS) * (own_pts * psum[:, 16:17] - psum),
        jnp.where(lane == 16, psum[:, 17:18] / HITS, 0.0),
    )
    gh, gm, gl = split3(grads)
    zeros8 = jnp.zeros((8, 128), f32)
    g3 = jnp.concatenate([gh, gm, gl, zeros8], 0).astype(bf16)
    sel3 = jnp.concatenate([sel, sel, sel, jnp.zeros((8, 256), f32)], 0).astype(bf16)
    spread_back = tn_dot(g3, sel3)
    count = jnp.sum(sel, 0, keepdims=True)
    coord_grad = coord_grad + spread_back[0:16]
    charge_grad = pot_i / HITS + spread_back[16:17]
    beta_grad = noise_f / HITS - count * (1.0 / POINTS)
    logit_grad = charge_grad * slope + beta_grad * beta * (1.0 - beta)
    loss_row = charge * pot_i / HITS + (count - count * beta) / POINTS + noise_f * beta / HITS
    loss_local = jnp.sum(loss_row, 1, keepdims=True)

    low = jnp.concatenate([coord_grad, jnp.where(rows_of((16, 256)) == 0, logit_grad, 0.0)], 0).astype(bf16)
    head = jnp.dot(low, act_ref[3], preferred_element_type=f32)
    up = tn_dot(low, wcb)

    def core_copy(j):
        if j == 0 or j == 4:
            span = pl.ds(0, 4) if j == 0 else pl.ds(4, 1)
            src, dst = partz_ref.at[other, :, span], corez_in.at[:, span]
        else:
            span = pl.ds(2 * j - 2, 2)
            src, dst = part_ref.at[other, :, span], core_in.at[:, span]
        return copy(src, dst, s_core.at[j], r_core.at[j], partner)

    def core_sum(j):
        core_copy(j).wait()
        if j == 0 or j == 4:
            first, last = (0, 4) if j == 0 else (4, 5)
            partz_ref[core, :, first:last] += corez_in[:, first:last]
        else:
            part_ref[core, :, 2 * j - 2 : 2 * j] += core_in[:, 2 * j - 2 : 2 * j]

    def span_of(c, table):
        first, last = table[c]
        return pl.ds(first, last - first)

    def xy_copy(c, i):
        span = span_of(c, chunks)
        target = ((x + i // 4) % 4) * 4 + (y + i % 4) % 4
        return copy(part_ref.at[core, target, span], xy_in.at[i, span], s_xy.at[c], r_xy.at[c], plane(i))

    def z_copy(c, i):
        block = zsum_ref.at[z, span_of(c, chunks)]
        return copy(block, block, s_z.at[c], r_z.at[c], ring(i))

    def g_copy(c, i):
        block = full_ref.at[core, here, span_of(c, chunks)]
        return copy(block, block, s_g.at[c], r_g.at[c, i // 4], plane(i))

    def f_copy(c, i):
        block = full_ref.at[core, pl.ds(((x + 4 - i) % 4) * 4, 4), span_of(c, chunks)]
        return copy(block, block, s_f.at[c], r_f.at[c], partner)

    def bz_copy(c, i):
        span = span_of(c, zchunks)
        return copy(partz_ref.at[core, (z + i) % 8, span], z_in.at[i, span], s_bz.at[c], r_bz.at[c], ring(i))

    def bx_copy(c, i):
        block = xysum_ref.at[here, span_of(c, zchunks)]
        return copy(block, block, s_bx.at[c], r_bx.at[c], plane(i))

    def bg_copy(c, i):
        block = fullz_ref.at[core, z, span_of(c, zchunks)]
        return copy(block, block, s_bg.at[c], r_bg.at[c], ring(i))

    def bf_copy(c):
        block = fullz_ref.at[core, :, span_of(c, zchunks)]
        return copy(block, block, s_bf.at[c], r_bf.at[c], partner)

    def layer_grad(layer, up):
        local = (up * pre_ref[layer]).astype(bf16)
        wg = jnp.dot(actt_ref[layer], local, preferred_element_type=f32)
        for half in range(2):
            cols = wg[:, half * 128 : half * 128 + 128]
            if layer == 3:
                partz_ref[:, :, 2 * half : 2 * half + 2] = cols.reshape(2, 8, 2, 8, 128)
            else:
                part_ref[:, :, 2 * (2 - layer) + half] = cols.reshape(2, 16, 8, 128)
        core_copy(3 - layer).start()
        bias = jnp.sum(local.astype(f32), 0, keepdims=True)
        return bias, nt_dot(local, w_ref[layer]) if layer > 0 else None

    biases = [None] * 4
    biases[3], up = layer_grad(3, up)
    biases[2], up = layer_grad(2, up)
    biases[1], up = layer_grad(1, up)
    biases[0], up = layer_grad(0, up)
    core_sum(1)
    over(far_plane, lambda i: xy_copy(0, i).start())
    core_sum(0)
    over(far_ring, lambda i: bz_copy(0, i).start())
    ext8 = jnp.where(
        row8 == 0,
        head[16:17],
        jnp.where(
            row8 == 1,
            biases[0],
            jnp.where(
                row8 == 2,
                biases[1],
                jnp.where(row8 == 3, biases[2], jnp.where(row8 == 4, biases[3], jnp.where(row8 == 5, loss_local, 0.0))),
            ),
        ),
    )
    ext = jnp.concatenate([head[0:16], ext8], 0)
    for half in range(2):
        cols = ext[:, half * 128 : half * 128 + 128].reshape(3, 8, 128)
        partz_ref[half, :, 4] = jnp.concatenate([cols, jnp.zeros((5, 8, 128), f32)], 0)
    core_copy(4).start()
    core_sum(2)
    over(far_plane, lambda i: xy_copy(1, i).start())
    core_sum(3)
    over(far_plane, lambda i: xy_copy(2, i).start())
    core_sum(4)
    over(far_ring, lambda i: bz_copy(1, i).start())

    def z_first(c):
        first, last = zchunks[c]
        settle(z_in.at[pl.ds(1, 7), span_of(c, zchunks)], s_bz.at[c], r_bz.at[c])
        total = partz_ref[core, z, first:last]
        for i in range(1, 8):
            total = total + z_in[i, first:last]
        xysum_ref[here, first:last] = total
        over(far_plane, lambda i: bx_copy(c, i).start())

    def plane_first(c):
        first, last = chunks[c]
        settle(xy_in.at[pl.ds(1, 15), span_of(c, chunks)], s_xy.at[c], r_xy.at[c])
        total = part_ref[core, here, first:last]
        for i in range(1, 16):
            total = total + xy_in[i, first:last]
        zsum_ref[z, first:last] = total
        over(far_ring, lambda i: z_copy(c, i).start())

    def z_last(c):
        first, last = zchunks[c]
        settle(xysum_ref.at[pl.ds(1, 15), span_of(c, zchunks)], s_bx.at[c], r_bx.at[c])
        total = xysum_ref[0, first:last]
        for i in range(1, 16):
            total = total + xysum_ref[i, first:last]
        fullz_ref[core, z, first:last] = total
        over(far_ring, lambda i: bg_copy(c, i).start())

    def plane_last(c):
        first, last = chunks[c]
        settle(zsum_ref.at[pl.ds(1, 7), span_of(c, chunks)], s_z.at[c], r_z.at[c])
        total = zsum_ref[0, first:last]
        for i in range(1, 8):
            total = total + zsum_ref[i, first:last]
        full_ref[core, here, first:last] = total
        over(far_plane, lambda i: g_copy(c, i).start())

    z_first(0)
    plane_first(0)
    plane_first(1)
    z_first(1)
    plane_first(2)
    plane_last(0)
    z_last(0)
    plane_last(1)
    z_last(1)
    plane_last(2)

    def z_hand_on(c):
        settle(fullz_ref.at[core, pl.ds(1, 7), span_of(c, zchunks)], s_bg.at[c], r_bg.at[c])
        bf_copy(c).start()

    def plane_hand_on(c):
        span = span_of(c, chunks)
        settle(full_ref.at[core, pl.ds(1, 3), span], r_g.at[c, 0])
        f_copy(c, 0).start()

        def step(i):
            settle(full_ref.at[core, pl.ds(0, 4), span], r_g.at[c, i])
            f_copy(c, i).start()
        each(1, 4, step)

    def place(layer):
        for half in range(2):
            cols = slice(half * 128, half * 128 + 128)
            if layer == 3:
                gw_ref[3, :, cols] = fullz_ref[:, :, 2 * half : 2 * half + 2].reshape(256, 128)
            else:
                gw_ref[layer, :, cols] = full_ref[:, :, 2 * (2 - layer) + half].reshape(256, 128)

    plane_hand_on(0)
    z_hand_on(0)
    z_hand_on(1)
    plane_hand_on(1)
    plane_hand_on(2)
    bf_copy(0).wait()
    place(3)
    bf_copy(1).wait()
    gc_ref[...] = jnp.concatenate(
        [fullz_ref[half, 0:2, 4].reshape(16, 128) for half in range(2)], 1
    )
    last = jnp.concatenate([fullz_ref[half, 2, 4] for half in range(2)], 1)
    gbeta_ref[...] = last[0:1]
    gb_ref[...] = last[1:5]
    loss_ref[...] = last[5:6, 0:1]

    for c in range(3):
        settle(full_ref.at[core, pl.ds(1, 15), span_of(c, chunks)], s_g.at[c])
        settle(full_ref.at[core, :, span_of(c, chunks)], s_f.at[c], r_f.at[c])
        place(2 - c)


def deliver(*refs):
    sems = refs[10]
    copies = [pltpu.make_async_copy(refs[i], refs[5 + i], sems.at[i]) for i in range(5)]
    for copy in copies:
        copy.start()
    for copy in copies:
        copy.wait()


def on_device(features, w_layers, b_layers, w_coord, w_beta, point_hit, track, noise):
    vmem = pl.BlockSpec(memory_space=pltpu.VMEM)
    hbm = pl.BlockSpec(memory_space=pltpu.HBM)
    dma = pltpu.SemaphoreType.DMA
    results = (
        jax.ShapeDtypeStruct((4, 256, 256), f32),
        jax.ShapeDtypeStruct((4, 256), f32),
        jax.ShapeDtypeStruct((16, 256), f32),
        jax.ShapeDtypeStruct((1, 256), f32),
        jax.ShapeDtypeStruct((1, 1), f32),
    )
    grads = pl.pallas_call(
        kernel,
        name="condense",
        out_shape=results,
        in_specs=[hbm] * 8,
        out_specs=(vmem,) * 5,
        scratch_shapes=[
            pltpu.VMEM((256, 256), bf16),
            pltpu.VMEM((4, 256, 256), bf16),
            pltpu.VMEM((4, 256), f32),
            pltpu.VMEM((16, 256), bf16),
            pltpu.VMEM((256,), bf16),
            pltpu.SMEM((8,), jnp.int32),
            pltpu.VMEM((256,), jnp.int32),
            pltpu.VMEM((256,), jnp.int32),
            dma((11,)),
            pltpu.VMEM((4, 256, 256), f32),
            pltpu.VMEM((4, 256, 256), bf16),
            pltpu.VMEM((4, 256, 256), bf16),
            pltpu.VMEM((16, 40, 128), f32),
            pltpu.VMEM((16, 40, 128), f32),
            pltpu.VMEM((16, 40, 128), f32),
            pltpu.VMEM((16, 8, 128), f32),
            pltpu.VMEM((16, 8, 128), f32),
            pltpu.VMEM((16, 8, 128), f32),
            pltpu.VMEM((128, 128), bf16),
            pltpu.VMEM((96, 256), bf16),
            pltpu.VMEM((128, 256), f32),
            pltpu.VMEM((128, 256), f32),
            pltpu.VMEM((128, 256), f32),
            pltpu.VMEM((128, 128), f32),
            pltpu.VMEM((2, 16, 6, 8, 128), f32),
            pltpu.VMEM((16, 6, 8, 128), f32),
            pltpu.VMEM((16, 6, 8, 128), f32),
            pltpu.VMEM((8, 6, 8, 128), f32),
            pltpu.VMEM((2, 16, 6, 8, 128), f32),
            pltpu.VMEM((2, 8, 5, 8, 128), f32),
            pltpu.VMEM((8, 5, 8, 128), f32),
            pltpu.VMEM((8, 5, 8, 128), f32),
            pltpu.VMEM((16, 5, 8, 128), f32),
            pltpu.VMEM((2, 8, 5, 8, 128), f32),
            dma((1,)), dma((4,)), dma((1,)), dma((1,)),
            dma((1,)), dma((1,)), dma((1,)), dma((1,)),
            dma((5,)), dma((5,)), dma((3,)), dma((3,)),
            dma((3,)), dma((3,)), dma((3,)), dma((3, 4)),
            dma((3,)), dma((3,)),
            dma((2,)), dma((2,)), dma((2,)), dma((2,)),
            dma((2,)), dma((2,)), dma((2,)), dma((2,)),
        ],
        compiler_params=pltpu.CompilerParams(
            collective_id=0, has_side_effects=True, vmem_limit_bytes=48 << 20
        ),
    )(*[pltpu.with_memory_space_constraint(v, pltpu.HBM) for v in (features, w_layers, b_layers, w_coord, w_beta, point_hit, track, noise)])
    grad_w, grad_b, grad_c, grad_beta, loss = pl.pallas_call(
        deliver,
        name="deliver",
        out_shape=results,
        in_specs=[vmem] * 5,
        out_specs=(hbm,) * 5,
        scratch_shapes=[dma((5,))],
        compiler_params=pltpu.CompilerParams(vmem_limit_bytes=8 << 20),
    )(*grads)
    return grad_w, grad_b, grad_c, grad_beta.reshape(256), loss.reshape(())


def solution(mesh):
    return jax.shard_map(
        on_device,
        mesh=mesh,
        in_specs=(
            P(("layer", "phi"), None),
            P(),
            P(),
            P(),
            P(),
            P(("layer", "phi")),
            P(("layer", "phi")),
            P(("layer", "phi")),
        ),
        out_specs=(P(), P(), P(), P(), P()),
        check_vma=False,
    )
```

```python
import jax
import jax.numpy as jnp
from jax import lax
from jax.sharding import PartitionSpec as P
from jax.experimental import pallas as pl
from jax.experimental.pallas import tpu as pltpu

f32 = jnp.float32
bf16 = jnp.bfloat16
dist_eps = 0.0001
charge_floor = 0.5
MESH = pl.DeviceIdType.MESH
HITS = 65536.0
POINTS = 2048.0
far_plane = (10, 6, 9, 11, 14, 2, 8, 5, 7, 13, 15, 1, 3, 4, 12)
far_column = (9, 8, 7, 11, 6, 10, 5, 13, 4, 12, 3, 15, 2, 14, 1)
far_hits = (10, 9, 11, 8, 2, 1, 3, 6, 5, 7, 4, 14, 13, 15, 12)
far_ring = (4, 3, 5, 2, 6, 1, 7)
chunks = ((0, 2), (2, 4), (4, 6))
zchunks = ((0, 4), (4, 5))


def split3(v):
    hi = v.astype(bf16).astype(f32)
    rest = v - hi
    mid = rest.astype(bf16).astype(f32)
    low = (rest - mid).astype(bf16).astype(f32)
    return hi, mid, low


def rows_of(shape):
    return lax.broadcasted_iota(jnp.int32, shape, 0)


def lanes_of(shape):
    return lax.broadcasted_iota(jnp.int32, shape, 1)


def nt_dot(a, b):
    return lax.dot_general(a, b, (((1,), (1,)), ((), ())), preferred_element_type=f32)


def tn_dot(a, b):
    return lax.dot_general(a, b, (((0,), (0,)), ((), ())), preferred_element_type=f32)


def kernel(
    feat_hbm, w_hbm, b_hbm, wc_hbm, wb_hbm, hit_hbm, track_hbm, noise_hbm,
    gw_ref, gb_ref, gc_ref, gbeta_ref, loss_ref,
    feat_ref, w_ref, b_ref, wc_ref, wb_ref, hit_ref, track_ref, noise_ref, s_in,
    pre_ref, act_ref, actt_ref,
    hits_ref, hits_back, hits_out, pts_ref, pts_back, pts_out,
    ycat_ref, yqt_ref, qp_ref, id_ref, pot_ref, ptacc_ref,
    part_ref, core_in, xy_in, zsum_ref, full_ref,
    partz_ref, corez_in, z_in, xysum_ref, fullz_ref,
    s_hit, r_hit, s_pt, r_pt, s_hb, r_hb, s_pb, r_pb,
    s_core, r_core, s_xy, r_xy, s_z, r_z, s_g, r_g, s_f, r_f,
    s_bz, r_bz, s_bx, r_bx, s_bg, r_bg, s_bf, r_bf,
):
    loads = [
        pltpu.make_async_copy(src, dst, s_in.at[i])
        for i, (src, dst) in enumerate(
            [
                (feat_hbm, feat_ref),
                (w_hbm.at[0], w_ref.at[0]),
                (b_hbm, b_ref),
                (w_hbm.at[pl.ds(1, 3)], w_ref.at[pl.ds(1, 3)]),
                (wc_hbm, wc_ref),
                (wb_hbm, wb_ref),
                (track_hbm, track_ref),
                (noise_hbm, noise_ref),
                (hit_hbm, hit_ref),
            ]
        )
    ]
    lay = lax.axis_index("layer")
    phi = lax.axis_index("phi")
    z = (lay // 8) * 4 + phi % 4
    y = (lay // 2) % 4
    core = lay % 2
    x = phi // 4
    other = 1 - core
    here = x * 4 + y

    def device(px, py, pz, pc):
        return ((pz // 4) * 8 + py * 2 + pc, px * 4 + pz % 4)

    def plane(step):
        return device((x + step // 4) % 4, (y + step % 4) % 4, z, core)

    def plane_back(step):
        return device((x + 4 - step // 4) % 4, (y + 4 - step % 4) % 4, z, core)

    def column(step):
        return device(x, y, (z + step // 2) % 8, (core + step % 2) % 2)

    def column_back(step):
        return device(x, y, (z + 8 - step // 2) % 8, (core + 2 - step % 2) % 2)

    def ring(step):
        return device(x, y, (z + step) % 8, core)

    partner = device(x, y, z, other)

    def copy(src, dst, ssem, rsem, target):
        return pltpu.make_async_remote_copy(
            src_ref=src, dst_ref=dst, send_sem=ssem, recv_sem=rsem,
            device_id=target, device_id_type=MESH,
        )

    def settle(ref, *sems):
        for sem in sems:
            pltpu.make_async_copy(ref, ref, sem).wait()

    def each(first, last, body):
        def step(i, carry):
            body(i)
            return carry
        lax.fori_loop(first, last, step, 0)

    def over(order, body):
        for i in order:
            body(i)

    barrier = pltpu.get_barrier_semaphore()

    def greet(i, j):
        pl.semaphore_signal(barrier, inc=1, device_id=column(j), device_id_type=MESH)
        pl.semaphore_signal(barrier, inc=1, device_id=plane(i), device_id_type=MESH)

    for near, tall in zip(far_plane, far_column):
        greet(near, tall)
    for load in loads:
        load.start()

    for load in loads[0:3]:
        load.wait()
    hidden = feat_ref[...]
    for layer in range(4):
        if layer == 1:
            loads[3].wait()
        pre = jnp.dot(hidden, w_ref[layer], preferred_element_type=f32) + b_ref[layer : layer + 1, :]
        pre_ref[layer] = pre
        hidden = (pre * jax.nn.sigmoid(pre)).astype(bf16)
        act_ref[layer] = hidden
    for load in loads[4:9]:
        load.wait()
    wcb = jnp.concatenate(
        [
            wc_ref[...].astype(f32),
            jnp.where(rows_of((16, 256)) == 0, wb_ref[...].astype(f32).reshape(1, 256), 0.0),
        ],
        0,
    ).astype(bf16)
    xz = nt_dot(wcb, hidden)
    coords = xz[0:16]
    logits = xz[16:17]
    expz = jnp.exp(logits)
    spread = jnp.log1p(2.0 * expz)
    charge = 0.25 * spread * spread + charge_floor
    slope = 0.5 * spread * (2.0 * expz / (1.0 + 2.0 * expz))
    beta = jax.nn.sigmoid(logits)
    noise = noise_ref[...].reshape(1, 256)
    track = track_ref[...].reshape(1, 256)
    key = jnp.where(noise == 0, track, -1).astype(f32)
    noise_f = noise.astype(f32)
    square = jnp.sum(coords * coords, 0, keepdims=True)
    row8 = rows_of((8, 256))
    lane8 = lanes_of((8, 256))
    pack = jnp.where(row8 == 0, charge, jnp.where(row8 == 1, key, jnp.where(row8 == 2, square, 0.0)))
    mine = jnp.concatenate([coords, pack], 0)
    r8s = rows_of((8, 128))
    tail_h = jnp.where(r8s == 0, charge[:, 0:128], jnp.where(r8s == 1, charge[:, 128:256], jnp.where(r8s == 2, key[:, 0:128], jnp.where(r8s == 3, key[:, 128:256], 0.0))))
    hits_ref[0] = jnp.concatenate([coords[:, 0:128], coords[:, 128:256], tail_h], 0)
    sel = jnp.zeros((8, 256), f32)
    for k in range(8):
        sel = jnp.where((row8 == k) & (lane8 == hit_ref[k]), 1.0, sel)
    sel_low = sel.astype(bf16)
    mine128 = jnp.concatenate([mine, jnp.zeros((104, 256), f32)], 0)
    mh, mm, ml = split3(mine128)
    own_pts = (nt_dot(sel_low, mh.astype(bf16)) + nt_dot(sel_low, mm.astype(bf16))) + nt_dot(sel_low, ml.astype(bf16))
    linear = lay * 16 + phi
    ident = (linear * 8 + rows_of((8, 128))).astype(f32)
    own_pts = jnp.where(lanes_of((8, 128)) == 17, ident, own_pts)
    pts_ref[0] = own_pts

    pl.semaphore_wait(barrier, 30)

    def pt_copy(i):
        return copy(pts_ref.at[0], pts_ref.at[i], s_pt.at[0], r_pt.at[0], column(i))

    def hit_copy(i):
        return copy(hits_ref.at[0], hits_ref.at[i], s_hit.at[0], r_hit.at[i // 4], plane(i))

    over(far_column, lambda i: pt_copy(i).start())
    over(far_hits, lambda i: hit_copy(i).start())

    actt_ref[0] = feat_ref[...].T
    for layer in range(4):
        pre = pre_ref[layer]
        sig = jax.nn.sigmoid(pre)
        pre_ref[layer] = sig * (1.0 + pre * (1.0 - sig))
        if layer < 3:
            actt_ref[layer + 1] = act_ref[layer].T
    ptacc_ref[...] = jnp.zeros((128, 128), f32)
    pot_ref[...] = jnp.zeros((128, 256), f32)

    settle(pts_ref.at[pl.ds(1, 15)], s_pt.at[0], r_pt.at[0])
    points = pts_ref[...].reshape(128, 128)
    qp_ref[...] = jnp.broadcast_to(points[:, 16:17], (128, 256))
    id_ref[...] = jnp.broadcast_to(points[:, 17:18], (128, 256))
    pt = points.T
    y_t = pt[0:16]
    qp_t = pt[16:17]
    yh, ym, yl = split3(-2.0 * y_t)
    sqh, sqm, sql = split3(pt[18:19])
    row16 = rows_of((16, 128))
    tail = jnp.where(row16 < 3, 1.0, jnp.where(row16 == 3, sqh, jnp.where(row16 == 4, sqm, jnp.where(row16 == 5, sql, 0.0))))
    ycat_ref[...] = jnp.concatenate([yh, yh, ym, ym, yh, yl, tail, jnp.zeros((16, 128), f32)], 0).T.astype(bf16)
    yq = jnp.concatenate([y_t * qp_t, jnp.where(row16 == 0, qp_t, 0.0)], 0)
    yqh, yqm, yql = split3(yq)
    yqt = jnp.concatenate([yqh, yqm, yql], 0).astype(bf16)
    yqt_ref[...] = jnp.concatenate([yqt, yqt], 1)

    def hb_copy(i):
        return copy(hits_out.at[i], hits_back.at[i], s_hb.at[0], r_hb.at[0], plane_back(i))

    wide = 4
    span = wide * 256
    r16 = rows_of((16, span))

    def over_hits(v):
        return v if wide == 1 else jnp.concatenate([v] * wide, 1)

    def pairs(turn):
        j = (turn * 2) % 4 + turn // 2
        first = j * wide
        @pl.when(j == 0)
        def _():
            settle(hits_ref.at[pl.ds(1, wide - 1)], r_hit.at[0])

        @pl.when(j > 0)
        def _():
            settle(hits_ref.at[pl.ds(first, wide)], r_hit.at[j])

        blks = [hits_ref[first + k] for k in range(wide)]
        xs = jnp.concatenate([v for b in blks for v in (b[0:16], b[16:32])], 1)
        q = jnp.concatenate([v for b in blks for v in (b[32:33], b[33:34])], 1)
        key_i = jnp.concatenate([v for b in blks for v in (b[34:35], b[35:36])], 1)
        xh, xm, xl = split3(xs)
        sh, sm, sl = split3(jnp.sum(xs * xs, 0, keepdims=True))
        tail_x = jnp.where(r16 == 0, sh, jnp.where(r16 == 1, sm, jnp.where(r16 == 2, sl, jnp.where(r16 < 6, 1.0, 0.0))))
        xcat = jnp.concatenate([xh, xm, xh, xm, xl, xh, tail_x, jnp.zeros((16, span), f32)], 0).astype(bf16)
        d2 = jnp.maximum(jnp.dot(ycat_ref[...], xcat, preferred_element_type=f32), 0.0)
        t = d2 + dist_eps
        inv = lax.rsqrt(t)
        reach = jnp.maximum(1.0 - t * inv, 0.0)
        match = over_hits(id_ref[...]) == key_i
        pot = jnp.where(match, d2, reach * reach)
        cc = jnp.where(match, 1.0, -(reach * inv))
        pot_rows = jnp.sum(pot * over_hits(qp_ref[...]), 0, keepdims=True)
        weighted = pot * q
        pot_sum = weighted[:, 0:256]
        for k in range(1, wide):
            pot_sum = pot_sum + weighted[:, 256 * k : 256 * k + 256]
        pot_ref[...] += pot_sum
        cc_hi = cc.astype(bf16)
        cc_lo = (cc - cc_hi.astype(f32)).astype(bf16)
        ht = jnp.dot(yqt_ref[...], jnp.concatenate([cc_hi, cc_lo], 0), preferred_element_type=f32)
        ht = (ht[0:32] + ht[32:64]) + ht[64:96]
        for k in range(wide):
            lo = slice(256 * k, 256 * k + 128)
            hi = slice(256 * k + 128, 256 * k + 256)
            ends = jnp.where(
                r8s == 0, ht[16:17, lo], jnp.where(r8s == 1, ht[16:17, hi], jnp.where(r8s == 2, pot_rows[:, lo], pot_rows[:, hi]))
            )
            hits_out[first + k] = jnp.concatenate([ht[0:16, lo], ht[0:16, hi], ends], 0)
        xq = jnp.concatenate([xs * q, jnp.where(r16 == 0, q, 0.0)], 0)
        xqh, xqm, xql = split3(xq)
        xq_all = jnp.concatenate([xqh, xqm, xql, jnp.zeros((32, span), f32)], 0).astype(bf16)
        ptacc_ref[...] += nt_dot(cc_hi, xq_all) + nt_dot(cc_lo, xq_all)
        for k in (2, 1, 3, 0):
            if k > 0:
                hb_copy(first + k).start()
            else:

                @pl.when(j > 0)
                def _():
                    hb_copy(first).start()

    each(0, 16 // wide, pairs)
    settle(hits_ref.at[pl.ds(1, 15)], s_hit.at[0])

    acc = ptacc_ref[...]
    acc = (acc + pltpu.roll(acc, 96, 1)) + pltpu.roll(acc, 64, 1)
    pot_cols = jnp.sum(pot_ref[...], 1, keepdims=True)
    pts_out[...] = jnp.where(lanes_of((128, 128)) == 17, pot_cols, acc).reshape(16, 8, 128)

    def pb_copy(i):
        return copy(pts_out.at[i], pts_back.at[i], s_pb.at[0], r_pb.at[0], column_back(i))

    over(far_column, lambda i: pb_copy(i).start())
    settle(hits_back.at[pl.ds(1, 15)], s_hb.at[0], r_hb.at[0])
    hsum = hits_out[0]
    for i in range(1, 16):
        hsum = hsum + hits_back[i]
    pull = jnp.concatenate([hsum[0:16], hsum[16:32]], 1)
    coef_i = jnp.concatenate([hsum[32:33], hsum[33:34]], 1)
    pot_i = jnp.concatenate([hsum[34:35], hsum[35:36]], 1)
    coord_grad = (2.0 * charge / HITS) * (coords * coef_i - pull)
    settle(pts_back.at[pl.ds(1, 15)], s_pb.at[0], r_pb.at[0])
    psum = pts_out[0]
    for i in range(1, 16):
        psum = psum + pts_back[i]
    lane = lanes_of((8, 128))
    grads = jnp.where(
        lane < 16,
        (2.0 * own_pts[:, 16:17] / HITS) * (own_pts * psum[:, 16:17] - psum),
        jnp.where(lane == 16, psum[:, 17:18] / HITS, 0.0),
    )
    gh, gm, gl = split3(grads)
    zeros8 = jnp.zeros((8, 128), f32)
    g3 = jnp.concatenate([gh, gm, gl, zeros8], 0).astype(bf16)
    sel3 = jnp.concatenate([sel, sel, sel, jnp.zeros((8, 256), f32)], 0).astype(bf16)
    spread_back = tn_dot(g3, sel3)
    count = jnp.sum(sel, 0, keepdims=True)
    coord_grad = coord_grad + spread_back[0:16]
    charge_grad = pot_i / HITS + spread_back[16:17]
    beta_grad = noise_f / HITS - count * (1.0 / POINTS)
    logit_grad = charge_grad * slope + beta_grad * beta * (1.0 - beta)
    loss_row = charge * pot_i / HITS + (count - count * beta) / POINTS + noise_f * beta / HITS
    loss_local = jnp.sum(loss_row, 1, keepdims=True)

    low = jnp.concatenate([coord_grad, jnp.where(rows_of((16, 256)) == 0, logit_grad, 0.0)], 0).astype(bf16)
    head = jnp.dot(low, act_ref[3], preferred_element_type=f32)
    up = tn_dot(low, wcb)

    def core_copy(j):
        if j == 0 or j == 4:
            span = pl.ds(0, 4) if j == 0 else pl.ds(4, 1)
            src, dst = partz_ref.at[other, :, span], corez_in.at[:, span]
        else:
            span = pl.ds(2 * j - 2, 2)
            src, dst = part_ref.at[other, :, span], core_in.at[:, span]
        return copy(src, dst, s_core.at[j], r_core.at[j], partner)

    def core_sum(j):
        core_copy(j).wait()
        if j == 0 or j == 4:
            first, last = (0, 4) if j == 0 else (4, 5)
            partz_ref[core, :, first:last] += corez_in[:, first:last]
        else:
            part_ref[core, :, 2 * j - 2 : 2 * j] += core_in[:, 2 * j - 2 : 2 * j]

    def span_of(c, table):
        first, last = table[c]
        return pl.ds(first, last - first)

    def xy_copy(c, i):
        span = span_of(c, chunks)
        target = ((x + i // 4) % 4) * 4 + (y + i % 4) % 4
        return copy(part_ref.at[core, target, span], xy_in.at[i, span], s_xy.at[c], r_xy.at[c], plane(i))

    def z_copy(c, i):
        block = zsum_ref.at[z, span_of(c, chunks)]
        return copy(block, block, s_z.at[c], r_z.at[c], ring(i))

    def g_copy(c, i):
        block = full_ref.at[core, here, span_of(c, chunks)]
        return copy(block, block, s_g.at[c], r_g.at[c, i // 4], plane(i))

    def f_copy(c, i):
        block = full_ref.at[core, pl.ds(((x + 4 - i) % 4) * 4, 4), span_of(c, chunks)]
        return copy(block, block, s_f.at[c], r_f.at[c], partner)

    def bz_copy(c, i):
        span = span_of(c, zchunks)
        return copy(partz_ref.at[core, (z + i) % 8, span], z_in.at[i, span], s_bz.at[c], r_bz.at[c], ring(i))

    def bx_copy(c, i):
        block = xysum_ref.at[here, span_of(c, zchunks)]
        return copy(block, block, s_bx.at[c], r_bx.at[c], plane(i))

    def bg_copy(c, i):
        block = fullz_ref.at[core, z, span_of(c, zchunks)]
        return copy(block, block, s_bg.at[c], r_bg.at[c], ring(i))

    def bf_copy(c):
        block = fullz_ref.at[core, :, span_of(c, zchunks)]
        return copy(block, block, s_bf.at[c], r_bf.at[c], partner)

    def layer_grad(layer, up):
        local = (up * pre_ref[layer]).astype(bf16)
        wg = jnp.dot(actt_ref[layer], local, preferred_element_type=f32)
        for half in range(2):
            cols = wg[:, half * 128 : half * 128 + 128]
            if layer == 3:
                partz_ref[:, :, 2 * half : 2 * half + 2] = cols.reshape(2, 8, 2, 8, 128)
            else:
                part_ref[:, :, 2 * (2 - layer) + half] = cols.reshape(2, 16, 8, 128)
        core_copy(3 - layer).start()
        bias = jnp.sum(local.astype(f32), 0, keepdims=True)
        return bias, nt_dot(local, w_ref[layer]) if layer > 0 else None

    biases = [None] * 4
    biases[3], up = layer_grad(3, up)
    biases[2], up = layer_grad(2, up)
    biases[1], up = layer_grad(1, up)
    biases[0], up = layer_grad(0, up)
    core_sum(1)
    over(far_plane, lambda i: xy_copy(0, i).start())
    core_sum(0)
    over(far_ring, lambda i: bz_copy(0, i).start())
    ext8 = jnp.where(
        row8 == 0,
        head[16:17],
        jnp.where(
            row8 == 1,
            biases[0],
            jnp.where(
                row8 == 2,
                biases[1],
                jnp.where(row8 == 3, biases[2], jnp.where(row8 == 4, biases[3], jnp.where(row8 == 5, loss_local, 0.0))),
            ),
        ),
    )
    ext = jnp.concatenate([head[0:16], ext8], 0)
    for half in range(2):
        cols = ext[:, half * 128 : half * 128 + 128].reshape(3, 8, 128)
        partz_ref[half, :, 4] = jnp.concatenate([cols, jnp.zeros((5, 8, 128), f32)], 0)
    core_copy(4).start()
    core_sum(2)
    over(far_plane, lambda i: xy_copy(1, i).start())
    core_sum(3)
    over(far_plane, lambda i: xy_copy(2, i).start())
    core_sum(4)
    over(far_ring, lambda i: bz_copy(1, i).start())

    def z_first(c):
        first, last = zchunks[c]
        settle(z_in.at[pl.ds(1, 7), span_of(c, zchunks)], s_bz.at[c], r_bz.at[c])
        total = partz_ref[core, z, first:last]
        for i in range(1, 8):
            total = total + z_in[i, first:last]
        xysum_ref[here, first:last] = total
        over(far_plane, lambda i: bx_copy(c, i).start())

    def plane_first(c):
        first, last = chunks[c]
        settle(xy_in.at[pl.ds(1, 15), span_of(c, chunks)], s_xy.at[c], r_xy.at[c])
        total = part_ref[core, here, first:last]
        for i in range(1, 16):
            total = total + xy_in[i, first:last]
        zsum_ref[z, first:last] = total
        over(far_ring, lambda i: z_copy(c, i).start())

    def z_last(c):
        first, last = zchunks[c]
        settle(xysum_ref.at[pl.ds(1, 15), span_of(c, zchunks)], s_bx.at[c], r_bx.at[c])
        total = xysum_ref[0, first:last]
        for i in range(1, 16):
            total = total + xysum_ref[i, first:last]
        fullz_ref[core, z, first:last] = total
        over(far_ring, lambda i: bg_copy(c, i).start())

    def plane_last(c):
        first, last = chunks[c]
        settle(zsum_ref.at[pl.ds(1, 7), span_of(c, chunks)], s_z.at[c], r_z.at[c])
        total = zsum_ref[0, first:last]
        for i in range(1, 8):
            total = total + zsum_ref[i, first:last]
        full_ref[core, here, first:last] = total
        over(far_plane, lambda i: g_copy(c, i).start())

    z_first(0)
    plane_first(0)
    plane_first(1)
    z_first(1)
    plane_first(2)
    plane_last(0)
    z_last(0)
    plane_last(1)
    z_last(1)
    plane_last(2)

    def z_hand_on(c):
        settle(fullz_ref.at[core, pl.ds(1, 7), span_of(c, zchunks)], s_bg.at[c], r_bg.at[c])
        bf_copy(c).start()

    def plane_hand_on(c):
        span = span_of(c, chunks)
        settle(full_ref.at[core, pl.ds(1, 3), span], r_g.at[c, 0])
        f_copy(c, 0).start()

        def step(i):
            settle(full_ref.at[core, pl.ds(0, 4), span], r_g.at[c, i])
            f_copy(c, i).start()
        each(1, 4, step)

    def place(layer):
        for half in range(2):
            cols = slice(half * 128, half * 128 + 128)
            if layer == 3:
                gw_ref[3, :, cols] = fullz_ref[:, :, 2 * half : 2 * half + 2].reshape(256, 128)
            else:
                gw_ref[layer, :, cols] = full_ref[:, :, 2 * (2 - layer) + half].reshape(256, 128)

    plane_hand_on(0)
    z_hand_on(0)
    z_hand_on(1)
    plane_hand_on(1)
    plane_hand_on(2)
    bf_copy(0).wait()
    place(3)
    bf_copy(1).wait()
    gc_ref[...] = jnp.concatenate(
        [fullz_ref[half, 0:2, 4].reshape(16, 128) for half in range(2)], 1
    )
    last = jnp.concatenate([fullz_ref[half, 2, 4] for half in range(2)], 1)
    gbeta_ref[...] = last[0:1]
    gb_ref[...] = last[1:5]
    loss_ref[...] = last[5:6, 0:1]

    for c in range(3):
        settle(full_ref.at[core, pl.ds(1, 15), span_of(c, chunks)], s_g.at[c])
        settle(full_ref.at[core, :, span_of(c, chunks)], s_f.at[c], r_f.at[c])
        place(2 - c)


def deliver(*refs):
    sems = refs[10]
    copies = [pltpu.make_async_copy(refs[i], refs[5 + i], sems.at[i]) for i in range(5)]
    for copy in copies:
        copy.start()
    for copy in copies:
        copy.wait()


def on_device(features, w_layers, b_layers, w_coord, w_beta, point_hit, track, noise):
    vmem = pl.BlockSpec(memory_space=pltpu.VMEM)
    hbm = pl.BlockSpec(memory_space=pltpu.HBM)
    dma = pltpu.SemaphoreType.DMA
    results = (
        jax.ShapeDtypeStruct((4, 256, 256), f32),
        jax.ShapeDtypeStruct((4, 256), f32),
        jax.ShapeDtypeStruct((16, 256), f32),
        jax.ShapeDtypeStruct((1, 256), f32),
        jax.ShapeDtypeStruct((1, 1), f32),
    )
    grads = pl.pallas_call(
        kernel,
        name="condense",
        out_shape=results,
        in_specs=[hbm] * 8,
        out_specs=(vmem,) * 5,
        scratch_shapes=[
            pltpu.VMEM((256, 256), bf16),
            pltpu.VMEM((4, 256, 256), bf16),
            pltpu.VMEM((4, 256), f32),
            pltpu.VMEM((16, 256), bf16),
            pltpu.VMEM((256,), bf16),
            pltpu.SMEM((8,), jnp.int32),
            pltpu.VMEM((256,), jnp.int32),
            pltpu.VMEM((256,), jnp.int32),
            dma((9,)),
            pltpu.VMEM((4, 256, 256), f32),
            pltpu.VMEM((4, 256, 256), bf16),
            pltpu.VMEM((4, 256, 256), bf16),
            pltpu.VMEM((16, 40, 128), f32),
            pltpu.VMEM((16, 40, 128), f32),
            pltpu.VMEM((16, 40, 128), f32),
            pltpu.VMEM((16, 8, 128), f32),
            pltpu.VMEM((16, 8, 128), f32),
            pltpu.VMEM((16, 8, 128), f32),
            pltpu.VMEM((128, 128), bf16),
            pltpu.VMEM((96, 256), bf16),
            pltpu.VMEM((128, 256), f32),
            pltpu.VMEM((128, 256), f32),
            pltpu.VMEM((128, 256), f32),
            pltpu.VMEM((128, 128), f32),
            pltpu.VMEM((2, 16, 6, 8, 128), f32),
            pltpu.VMEM((16, 6, 8, 128), f32),
            pltpu.VMEM((16, 6, 8, 128), f32),
            pltpu.VMEM((8, 6, 8, 128), f32),
            pltpu.VMEM((2, 16, 6, 8, 128), f32),
            pltpu.VMEM((2, 8, 5, 8, 128), f32),
            pltpu.VMEM((8, 5, 8, 128), f32),
            pltpu.VMEM((8, 5, 8, 128), f32),
            pltpu.VMEM((16, 5, 8, 128), f32),
            pltpu.VMEM((2, 8, 5, 8, 128), f32),
            dma((1,)), dma((4,)), dma((1,)), dma((1,)),
            dma((1,)), dma((1,)), dma((1,)), dma((1,)),
            dma((5,)), dma((5,)), dma((3,)), dma((3,)),
            dma((3,)), dma((3,)), dma((3,)), dma((3, 4)),
            dma((3,)), dma((3,)),
            dma((2,)), dma((2,)), dma((2,)), dma((2,)),
            dma((2,)), dma((2,)), dma((2,)), dma((2,)),
        ],
        compiler_params=pltpu.CompilerParams(
            collective_id=0, has_side_effects=True, vmem_limit_bytes=48 << 20
        ),
    )(*[pltpu.with_memory_space_constraint(v, pltpu.HBM) for v in (features, w_layers, b_layers, w_coord, w_beta, point_hit, track, noise)])
    grad_w, grad_b, grad_c, grad_beta, loss = pl.pallas_call(
        deliver,
        name="deliver",
        out_shape=results,
        in_specs=[vmem] * 5,
        out_specs=(hbm,) * 5,
        scratch_shapes=[dma((5,))],
        compiler_params=pltpu.CompilerParams(vmem_limit_bytes=8 << 20),
    )(*grads)
    return grad_w, grad_b, grad_c, grad_beta.reshape(256), loss.reshape(())


def solution(mesh):
    return jax.shard_map(
        on_device,
        mesh=mesh,
        in_specs=(
            P(("layer", "phi"), None),
            P(),
            P(),
            P(),
            P(),
            P(("layer", "phi")),
            P(("layer", "phi")),
            P(("layer", "phi")),
        ),
        out_specs=(P(), P(), P(), P(), P()),
        check_vma=False,
    )
```
